128 devices in a mesh: tracer: 8 (over x, z_hi), tile: 16 (over y, z_lo, core).
Axes of the slice: x: 4, y: 4, z: 4 (z_hi: 2, z_lo: 2; z = z_hi * 2 + z_lo), core: 2. Of those that a mesh axis runs over, the one named last changes fastest.
Arguments:
- tracers: float32 [192, 8, 256, 128], P('tracer', None, 'tile'), may hold values from 0.1 to 2
- air_mass: float32 [8, 8, 256, 128], P('tracer', None, 'tile'), may hold values from 1 to 2
- flux_x: float32 [8, 8, 256, 128], P('tracer', None, 'tile'), may hold values from -0.2 to 0.2
- flux_y: float32 [8, 8, 256, 128], P('tracer', None, 'tile'), may hold values from -0.2 to 0.2
- flux_z: float32 [8, 8, 256, 128], P('tracer', None, 'tile'), may hold values from -0.05 to 0.05
- reactants: int32 [512, 2], replicated, may hold values from 0 to 191
- products: int32 [512, 192], replicated, may hold values 0 or 1
- rate_coeff: float32 [512], replicated, may hold values from 0.01 to 0.1
- record_of_step: int32 [2], replicated, may hold values from 0 to 7
Outputs:
- tracers_out: float32 [192, 8, 256, 128], P('tracer', None, 'tile')
The draws below stay inside these ranges and needn't reach their ends.
Inputs may be any that keep to these rules, and one draw needn't show every extreme that they name: A reaction's two reactants may be the same tracer.
All inputs are finite; a program needn't handle non-finite values.
Results may differ from the reference program's by a relative error of at most 0.0014.
Values may be sent and summed in bfloat16 or wider, within the bound.
No kernel may reach another device: no remote copies, remote signals or barrier semaphores. Data moves between devices by JAX's collectives and lax.ppermute only.
A program may use at most 128 MiB of HBM per device.

```python
import math
import jax
import jax.numpy as jnp
from jax import lax

TRACERS = 192
REACTIONS = 512
LEVELS = 8
STEPS = 2
NY = 128
NX = 256
N_TRACER = 8


def touch_ends(entries, stream_key, smallest, top_value):
    dims = entries.shape
    spot = [jax.random.randint(jax.random.fold_in(stream_key, axis), (), 0, dims[axis]) for axis in range(len(dims))]
    entries = entries.at[tuple(spot)].set(smallest)
    longest = dims.index(max(dims))
    spot[longest] = (spot[longest] + 1) % dims[longest]
    return entries.at[tuple(spot)].set(top_value)


def level_of(key, extent, split, low, high):
    def one(position, shards_of):
        steps = jax.random.uniform(jax.random.fold_in(jax.random.fold_in(key, 6), position), (shards_of,), jnp.float32, low / len(split), high / len(split))
        return jnp.repeat(jnp.exp(steps), extent[position] // shards_of).reshape((-1,) + (1,) * (len(extent) - position - 1))

    gain = one(*split[0])
    for cut in split[1:]:
        gain = gain * one(*cut)
    return gain


def setup_inputs(seed: int = 0) -> dict:
    streams_of = jax.random.split(jax.random.key(seed), 10)
    tracers = jnp.clip(jnp.exp(math.log(2.0) - 2.9957323 * jax.random.uniform(streams_of[0], (TRACERS, LEVELS, NX, NY), jnp.float32) ** level_of(streams_of[0], (TRACERS, LEVELS, NX, NY), ((0, 8), (2, 16)), -0.2, 0.2)), 0.1, 2.0)
    air_mass = jnp.clip(1.0 + 1.0 * jax.random.uniform(streams_of[1], (N_TRACER, LEVELS, NX, NY), jnp.float32) ** level_of(streams_of[1], (N_TRACER, LEVELS, NX, NY), ((0, 8), (2, 16)), -0.2, 0.2), 1.0, 2.0)
    flux_x = jnp.clip(jax.random.uniform(streams_of[2], (N_TRACER, LEVELS, NX, NY), jnp.float32, -0.2, 0.2) * level_of(streams_of[2], (N_TRACER, LEVELS, NX, NY), ((0, 8), (2, 16)), -0.4, 0.0), -0.2, 0.2)
    flux_y = jnp.clip(jax.random.uniform(streams_of[3], (N_TRACER, LEVELS, NX, NY), jnp.float32, -0.2, 0.2) * level_of(streams_of[3], (N_TRACER, LEVELS, NX, NY), ((0, 8), (2, 16)), -0.4, 0.0), -0.2, 0.2)
    flux_z = jnp.clip(jax.random.uniform(streams_of[4], (N_TRACER, LEVELS, NX, NY), jnp.float32, -0.05, 0.05) * level_of(streams_of[4], (N_TRACER, LEVELS, NX, NY), ((0, 8), (2, 16)), -0.4, 0.0), -0.05, 0.05)
    reactants = touch_ends(jax.random.randint(streams_of[5], (REACTIONS, 2), 0, TRACERS), jax.random.fold_in(streams_of[5], 1), 0, TRACERS - 1).astype(jnp.int32)
    products = touch_ends((jax.random.randint(streams_of[6], (REACTIONS, TRACERS), 0, TRACERS) < 3).astype(jnp.int32), jax.random.fold_in(streams_of[6], 1), 0, 1)
    rate_coeff = jnp.clip(jnp.exp(jax.random.uniform(streams_of[7], (REACTIONS,), jnp.float32, math.log(0.01), math.log(0.1))), 0.01, 0.1)
    record_of_step = jax.random.randint(streams_of[8], (STEPS,), 0, N_TRACER).astype(jnp.int32)
    return {"tracers": tracers, "air_mass": air_mass, "flux_x": flux_x, "flux_y": flux_y, "flux_z": flux_z, "reactants": reactants, "products": products, "rate_coeff": rate_coeff, "record_of_step": record_of_step}


def take_slice(values, first_cell, how_many, dim_along):
    return lax.slice_in_dim(values, first_cell, first_cell + how_many, axis=dim_along)


def pad_three(values, dim_along):
    widths = [(0, 0)] * values.ndim
    widths[dim_along] = (3, 3)
    return jnp.pad(values, widths)


def face_flux(tracer_pad, air_pad, crossing, dim_along):
    cell_count = tracer_pad.shape[dim_along] - 6
    lower = take_slice(tracer_pad, 1, cell_count + 3, dim_along)
    upper = take_slice(tracer_pad, 2, cell_count + 3, dim_along)
    outer = take_slice(tracer_pad, 0, cell_count + 3, dim_along) + take_slice(tracer_pad, 3, cell_count + 3, dim_along)
    edges = (7.0 / 12.0) * (lower + upper) - (1.0 / 12.0) * outer
    edges = jnp.clip(edges, jnp.minimum(lower, upper), jnp.maximum(lower, upper))
    left_edge = take_slice(edges, 0, cell_count + 2, dim_along)
    right_edge = take_slice(edges, 1, cell_count + 2, dim_along)
    centre = take_slice(tracer_pad, 2, cell_count + 2, dim_along)
    spread = right_edge - left_edge
    bending = 6.0 * (centre - 0.5 * (left_edge + right_edge))
    upwind_air = jnp.where(crossing > 0, take_slice(air_pad, 2, cell_count + 1, dim_along),
                           take_slice(air_pad, 3, cell_count + 1, dim_along))
    courant = jnp.abs(crossing) / jnp.maximum(upwind_air, 0.5)
    factor = 1.0 - 2.0 * courant / 3.0
    from_left = take_slice(right_edge, 0, cell_count + 1, dim_along) - 0.5 * courant * (
        take_slice(spread, 0, cell_count + 1, dim_along) - factor * take_slice(bending, 0, cell_count + 1, dim_along))
    from_right = take_slice(left_edge, 1, cell_count + 1, dim_along) + 0.5 * courant * (
        take_slice(spread, 1, cell_count + 1, dim_along) + factor * take_slice(bending, 1, cell_count + 1, dim_along))
    return crossing * jnp.where(crossing > 0, from_left, from_right)


def divergence(flux_faces, dim_along, cell_count):
    return take_slice(flux_faces, 1, cell_count, dim_along) - take_slice(flux_faces, 0, cell_count, dim_along)


def close_walls(south_flux, bottom_flux):
    row_index = lax.broadcasted_iota(jnp.int32, south_flux.shape, 3)
    level_index = lax.broadcasted_iota(jnp.int32, bottom_flux.shape, 1)
    return jnp.where(row_index == 0, 0.0, south_flux), jnp.where(level_index == 0, 0.0, bottom_flux)


def advect(tracer_xpad, air_xpad, east_faces, south_flux, bottom_flux, air_now):
    level_count = air_now.shape[1]
    row_count = air_now.shape[2]
    column_count = air_now.shape[3]
    tracer = take_slice(tracer_xpad, 3, row_count, 2)
    north_faces = jnp.concatenate([south_flux, jnp.zeros_like(take_slice(south_flux, 0, 1, 3))], 3)
    upper_faces = jnp.concatenate([bottom_flux, jnp.zeros_like(take_slice(bottom_flux, 0, 1, 1))], 1)
    flux_rows = face_flux(tracer_xpad, air_xpad, east_faces, 2)
    flux_columns = face_flux(pad_three(tracer, 3), pad_three(air_now, 3), north_faces, 3)
    flux_levels = face_flux(pad_three(tracer, 1), pad_three(air_now, 1), upper_faces, 1)
    air_next = (air_now - divergence(east_faces, 2, row_count) - divergence(north_faces, 3, column_count)
                - divergence(upper_faces, 1, level_count))
    tracer_mass = (air_now * tracer - divergence(flux_rows, 2, row_count) - divergence(flux_columns, 3, column_count)
                   - divergence(flux_levels, 1, level_count))
    return tracer_mass / air_next


def reference(tracers, air_mass, flux_x, flux_y, flux_z, reactants, products, rate_coeff, record_of_step):
    reactions, species = products.shape
    ident = lax.broadcasted_iota(jnp.int32, (reactions, species), 1)
    first_hot = (reactants[:, 0:1] == ident).astype(jnp.float32)
    second_hot = (reactants[:, 1:2] == ident).astype(jnp.float32)
    net = products.astype(jnp.float32) - first_hot - second_hot
    mixing = tracers
    for step_index in range(STEPS):
        record = record_of_step[step_index]
        air_now = lax.dynamic_index_in_dim(air_mass, record, 0, keepdims=True)
        east = lax.dynamic_index_in_dim(flux_x, record, 0, keepdims=True)
        south = lax.dynamic_index_in_dim(flux_y, record, 0, keepdims=True)
        bottom = lax.dynamic_index_in_dim(flux_z, record, 0, keepdims=True)
        row_index = lax.broadcasted_iota(jnp.int32, east.shape, 2)
        east = jnp.where(row_index == 0, 0.0, east)
        east_faces = jnp.concatenate([east, jnp.zeros_like(take_slice(east, 0, 1, 2))], 2)
        south, bottom = close_walls(south, bottom)
        air_xpad = pad_three(air_now, 2)

        def advect_one(single):
            return advect(pad_three(single[None], 2), air_xpad, east_faces, south, bottom, air_now)[0]

        advected = lax.map(advect_one, mixing)
        conc = advected.astype(jnp.bfloat16)

        def react_level(level_index):
            layer = lax.dynamic_index_in_dim(conc, level_index, 1, keepdims=False)
            flattened = layer.reshape(species, -1)
            first = jnp.take(flattened, reactants[:, 0], axis=0).astype(jnp.float32)
            second = jnp.take(flattened, reactants[:, 1], axis=0).astype(jnp.float32)
            reaction_rate = (rate_coeff[:, None] * first * second).astype(jnp.bfloat16)
            change = jnp.dot(net.T, reaction_rate.astype(jnp.float32), preferred_element_type=jnp.float32,
                             precision=lax.Precision.HIGHEST)
            return change.astype(jnp.bfloat16).reshape(layer.shape)

        increment = lax.map(react_level, jnp.arange(LEVELS, dtype=jnp.int32))
        mixing = advected + jnp.moveaxis(increment, 0, 1).astype(jnp.float32)
    return mixing
```

```python
import functools

import jax
import jax.numpy as jnp
from jax import lax
from jax.experimental import pallas as pl
from jax.experimental.pallas import tpu as pltpu
from jax.sharding import PartitionSpec as P

STEPS = 2
F32 = jnp.float32
BF16 = jnp.bfloat16
ROWS = 16
GROUPS = 24
XA, XB, XC, YA, YB, YC, WA, WB, WC, ZA, ZB, ZC, MASS, INV = range(14)
VMEM = pl.BlockSpec(memory_space=pltpu.VMEM)
SMEM = pl.BlockSpec(memory_space=pltpu.SMEM)


def roll(x, shift):
    return pltpu.roll(x, shift % 128, axis=1)


def lane_of(shape):
    return lax.broadcasted_iota(jnp.int32, shape, 1)


def slot_of(shape):
    return lane_of(shape) & 15


def exchange_blocks(vectors):
    block = lane_of(vectors[0].shape) >> 4
    out = list(vectors)
    for bit in (1, 2, 4):
        low = (block & bit) == 0
        for i in range(8):
            if i & bit:
                continue
            first, second = out[i], out[i | bit]
            out[i] = jnp.where(low, first, roll(second, 16 * bit))
            out[i | bit] = jnp.where(low, roll(first, -16 * bit), second)
    return out


def pack_kernel(q_ref, mass_ref, fx_ref, fy_ref, fz_ref, out_ref):
    def row(r, carry):
        for tg in range(3):
            levels = [
                q_ref[pl.ds(tg * 1024 + lev * 16 + r, 8, stride=128), :] for lev in range(8)
            ]
            for dest, value in enumerate(exchange_blocks(levels)):
                out_ref[dest, 3 * r + tg] = value
        return carry

    lax.fori_loop(0, ROWS, row, 0)
    for field, ref in enumerate((mass_ref, fx_ref, fy_ref, fz_ref)):
        for half in range(2):
            levels = [ref[0, lev, 8 * half : 8 * half + 8, :] for lev in range(8)]
            for dest, value in enumerate(exchange_blocks(levels)):
                out_ref[dest, 48 + 2 * field + half] = value


def unpack_kernel(in_ref, out_ref):
    def row(r, carry):
        for tg in range(3):
            cols = [in_ref[src, 3 * r + tg] for src in range(8)]
            for lev, value in enumerate(exchange_blocks(cols)):
                out_ref[pl.ds(tg * 1024 + lev * 16 + r, 8, stride=128), :] = value
        return carry

    lax.fori_loop(0, ROWS, row, 0)


def write_edges(state_ref, row_up, row_down, col_right, col_left):
    slot = slot_of((8, 128)) >> 2

    def group(g, carry):
        src = g // 3
        tg = g - 3 * src
        for rr in range(3):
            row_down[src * 9 + 3 * rr + tg] = state_ref[src, 3 * rr + tg]
            row_up[src * 9 + 3 * rr + tg] = state_ref[src, 3 * (13 + rr) + tg]
        for block in range(4):
            rows = [state_ref[src, 3 * (4 * block + i) + tg] for i in range(4)]
            right = roll(rows[0], -12)
            left = rows[0]
            for i in range(1, 4):
                right = jnp.where(slot == i, roll(rows[i], 4 * i - 12) if i < 3 else rows[i], right)
                left = jnp.where(slot == i, roll(rows[i], 4 * i), left)
            col_right[g * 4 + block] = right
            col_left[g * 4 + block] = left
        return carry

    lax.fori_loop(0, GROUPS, group, 0)


def edge_kernel(rec_ref, in_ref, weather_ref, row_up, row_down, col_right, col_left):
    write_edges(in_ref, row_up, row_down, col_right, col_left)
    for s in range(STEPS):
        record = rec_ref[s]
        for k in range(8):
            weather_ref[s, k] = in_ref[record, 48 + k]
        row_up[72 + s] = in_ref[record, 48 + 1]
        row_down[72 + 2 * s] = in_ref[record, 48 + 0]
        row_down[72 + 2 * s + 1] = in_ref[record, 48 + 2]
        for half in range(2):
            col_right[96 + 2 * s + half] = in_ref[record, 48 + half]
            col_left[96 + 4 * s + half] = in_ref[record, 48 + half]
            col_left[96 + 4 * s + 2 + half] = in_ref[record, 48 + 4 + half]


def face_weights(flux, mass_low, mass_up):
    upwind = jnp.where(flux > 0, mass_low, mass_up)
    c = jnp.abs(flux) / jnp.maximum(upwind, 0.5)
    side = flux * c
    return flux * (1.0 - c) * (1.0 - c), side * (c - 1.0), side * (3.0 - 2.0 * c)


def write_weights(s, place_ref, weather_ref, row_lo, row_hi, col_lo, col_hi, ext_ref, put):
    tile, col = place_ref[0], place_ref[1]

    def both(ref, *index):
        return jnp.concatenate(
            [ref[index[:-1] + (index[-1],)], ref[index[:-1] + (index[-1] + 1,)]], 0
        )

    mass = both(weather_ref, s, 0)
    ext_ref[0, 0:8] = row_lo[72 + s]
    ext_ref[0, 8:24] = mass
    ext_ref[0, 24:32] = row_hi[72 + 2 * s]
    row = lax.broadcasted_iota(jnp.int32, (16, 128), 0)
    ext_ref[1, 0:16] = jnp.where((row == 0) & (tile == 0), 0.0, both(weather_ref, s, 2))
    ext_ref[1, 16:24] = row_hi[72 + 2 * s + 1]
    ext_ref[1, 24:32] = jnp.zeros((8, 128), F32)
    east = ext_ref[1, 0:24]
    for k, value in enumerate(face_weights(east, ext_ref[0, 7:31], ext_ref[0, 8:32])):
        put(XA + k, 24, value)
    shape = (16, 128)
    slot, lane = slot_of(shape), lane_of(shape)
    mass_x = jnp.where(slot < 8, roll(both(col_hi, 96 + 4 * s), 16), roll(both(col_lo, 96 + 2 * s), -16))
    south = jnp.where((slot == 0) & (col == 0), 0.0, both(weather_ref, s, 4))
    south_x = roll(both(col_hi, 96 + 4 * s + 2), 16)
    low = roll(jnp.where(slot == 15, mass_x, mass), 1)
    for k, value in enumerate(face_weights(south, low, mass)):
        put(YA + k, 16, value)
    low = roll(jnp.where(slot == 15, mass, mass_x), 1)
    for k, value in enumerate(face_weights(south_x, low, mass_x)):
        put(WA + k, 16, value)
    bottom = jnp.where(lane < 16, 0.0, both(weather_ref, s, 6))
    for k, value in enumerate(face_weights(bottom, roll(mass, 16), mass)):
        put(ZA + k, 16, value)
    new_mass = (
        mass
        - (ext_ref[1, 1:17] - ext_ref[1, 0:16])
        - (roll(jnp.where(slot == 0, south_x, south), -1) - south)
        - (roll(bottom, -16) - bottom)
    )
    put(MASS, 16, mass)
    put(INV, 16, 1.0 / new_mass)


def edge_value(low2, low1, up1, up2):
    value = (7.0 / 12.0) * (low1 + up1) - (1.0 / 12.0) * (low2 + up2)
    return jnp.minimum(
        jnp.maximum(value, jnp.minimum(low1, up1)), jnp.maximum(low1, up1)
    )


def face_flux(weights, edge, below, above, q_low, q_up):
    a, b, c = weights
    forward = c > 0
    return a * edge + b * jnp.where(forward, below, above) + c * jnp.where(forward, q_low, q_up)


def advect(q_ref, row_lo, row_hi, col_lo, col_hi, get, out_ref, conc_ref):
    shape = (8, 128)
    slot, lane = slot_of(shape), lane_of(shape)
    first, last, last_two, left_half = slot == 0, slot == 15, slot >= 14, slot < 8

    def one_group(src, tg):
        def q_row(k):
            if k < 0:
                return row_lo[src * 9 + 3 * (k + 3) + tg]
            if k >= ROWS:
                return row_hi[src * 9 + 3 * (k - ROWS) + tg]
            return q_ref[src, 3 * k + tg]

        g = src * 3 + tg
        q = {k: q_row(k) for k in (-3, -2, -1, 0)}
        edges = {}

        def x_edge(k):
            for need in (k - 2, k - 1, k, k + 1):
                if need not in q:
                    q[need] = q_row(need)
            if k not in edges:
                edges[k] = edge_value(q[k - 2], q[k - 1], q[k], q[k + 1])
            return edges[k]

        def x_flux(r):
            return face_flux(
                [get(XA + i, r) for i in range(3)],
                x_edge(r), x_edge(r - 1), x_edge(r + 1), q[r - 1], q[r],
            )

        results = []
        below = x_flux(0)
        for r in range(ROWS):
            above = x_flux(r + 1)
            here = q[r]
            block, i = r // 4, r % 4
            x = jnp.where(
                left_half,
                roll(col_hi[g * 4 + block], 16 - 4 * i),
                roll(col_lo[g * 4 + block], -4 - 4 * i),
            )
            m1 = roll(jnp.where(last, x, here), 1)
            m2 = roll(jnp.where(last_two, x, here), 2)
            p1 = roll(jnp.where(first, x, here), -1)
            edge = edge_value(m2, m1, here, p1)
            x_m1 = roll(jnp.where(last, here, x), 1)
            x_m2 = roll(jnp.where(last_two, here, x), 2)
            x_p1 = roll(jnp.where(first, here, x), -1)
            edge_x = edge_value(x_m2, x_m1, x, x_p1)
            flux_y = face_flux(
                [get(YA + i, r) for i in range(3)], edge,
                roll(jnp.where(last, edge_x, edge), 1),
                roll(jnp.where(first, edge_x, edge), -1), m1, here,
            )
            flux_w = face_flux(
                [get(WA + i, r) for i in range(3)], edge_x,
                roll(jnp.where(last, edge, edge_x), 1), roll(edge_x, -1), x_m1, x,
            )
            flux_y_up = roll(jnp.where(first, flux_w, flux_y), -1)
            m1 = jnp.where(lane >= 16, roll(here, 16), 0.0)
            m2 = jnp.where(lane >= 32, roll(here, 32), 0.0)
            p1 = jnp.where(lane < 112, roll(here, -16), 0.0)
            edge = edge_value(m2, m1, here, p1)
            top = (7.0 / 12.0) * here - (1.0 / 12.0) * m1
            top = jnp.minimum(jnp.maximum(top, jnp.minimum(here, 0.0)), jnp.maximum(here, 0.0))
            flux_z = face_flux(
                [get(ZA + i, r) for i in range(3)], edge, roll(edge, 16),
                jnp.where(lane >= 112, top, roll(edge, -16)), m1, here,
            )
            moved = (
                get(MASS, r) * here
                - (above - below)
                - (flux_y_up - flux_y)
                - (roll(flux_z, -16) - flux_z)
            ) * get(INV, r)
            out_ref[src, 3 * r + tg] = moved
            results.append(moved)
            below = above
        return results

    def pair(p, carry):
        parts = []
        for k in range(2):
            g = 2 * p + k
            src = g // 3
            parts.append(one_group(src, g - 3 * src))
        start = pl.multiple_of(16 * p, 16)
        for r in range(ROWS):
            conc_ref[pl.ds(start, 16), 128 * r : 128 * r + 128] = jnp.concatenate(
                [parts[0][r], parts[1][r]], 0
            ).astype(BF16)
        return carry

    lax.fori_loop(0, GROUPS // 2, pair, 0)


def react(conc_ref, sel_ref, net_ref, coeff_ref, rate_ref, out_ref):
    def block(n, carry):
        lanes = pl.ds(pl.multiple_of(256 * n, 256), 256)
        conc = conc_ref[:, lanes]
        for k in range(4):
            part = slice(128 * k, 128 * k + 128)
            one = jnp.dot(sel_ref[part, :], conc, preferred_element_type=F32)
            two = jnp.dot(
                sel_ref[512 + 128 * k : 640 + 128 * k, :], conc, preferred_element_type=F32
            )
            rate_ref[part, :] = (coeff_ref[part, :] * one * two).astype(BF16)
        change = jnp.dot(net_ref[...], rate_ref[...], preferred_element_type=F32)
        change = change.astype(BF16).astype(F32)
        for i in range(2):
            r = 2 * n + i
            for g in range(GROUPS):
                part = change[8 * g : 8 * g + 8, 128 * i : 128 * i + 128]
                out_ref[g // 3, 3 * r + g % 3] += part
        return carry

    lax.fori_loop(0, ROWS // 2, block, 0)


def first_kernel(
    place_ref, q_ref, weather_ref, row_lo, row_hi, col_lo, col_hi, sel_ref, net_ref, coeff_ref,
    out_ref, later_ref, row_up, row_down, col_right, col_left, now_ref, ext_ref, conc_ref, rate_ref,
):
    for s, ref in enumerate((now_ref, later_ref)):
        def put(k, rows, value, ref=ref):
            ref[k, 0:rows] = value

        write_weights(s, place_ref, weather_ref, row_lo, row_hi, col_lo, col_hi, ext_ref, put)

    def get(k, r):
        return now_ref[k, pl.ds(r, 8, stride=0), :]

    advect(q_ref, row_lo, row_hi, col_lo, col_hi, get, out_ref, conc_ref)
    react(conc_ref, sel_ref, net_ref, coeff_ref, rate_ref, out_ref)
    write_edges(out_ref, row_up, row_down, col_right, col_left)


def second_kernel(
    now_ref, q_ref, row_lo, row_hi, col_lo, col_hi, sel_ref, net_ref, coeff_ref,
    out_ref, conc_ref, rate_ref,
):
    def get(k, r):
        return now_ref[k, pl.ds(r, 8, stride=0), :]

    advect(q_ref, row_lo, row_hi, col_lo, col_hi, get, out_ref, conc_ref)
    react(conc_ref, sel_ref, net_ref, coeff_ref, rate_ref, out_ref)


def blocks(*lead):
    return jax.ShapeDtypeStruct(lead + (8, 128), F32)


def call(kernel, outs, specs, scratch=(), args=()):
    single = not isinstance(outs, (list, tuple))
    return pl.pallas_call(
        kernel,
        out_shape=outs,
        in_specs=specs,
        out_specs=VMEM if single else [VMEM] * len(outs),
        scratch_shapes=list(scratch),
        compiler_params=pltpu.CompilerParams(vmem_limit_bytes=40 * 2**20),
    )(*args)


def swap(x):
    return lax.all_to_all(x, "tracer", split_axis=0, concat_axis=0, tiled=True)


def halo(row_up, row_down, col_right, col_left):
    def shift(x, axis, step):
        count = lax.axis_size(axis)
        pairs = [(i, i + step) for i in range(count) if 0 <= i + step < count]
        return lax.ppermute(x, axis, pairs)

    return (
        shift(row_up, "tile", 1),
        shift(row_down, "tile", -1),
        shift(col_right, "tracer", 1),
        shift(col_left, "tracer", -1),
    )


def per_device(
    tracers, air_mass, flux_x, flux_y, flux_z, reactants, products, rate_coeff, record_of_step
):
    reactions, species = products.shape
    place = jnp.stack([lax.axis_index("tile"), lax.axis_index("tracer")]).astype(jnp.int32)
    ident = lax.broadcasted_iota(jnp.int32, (reactions, species), 1)
    selector = jnp.concatenate(
        [reactants[:, 0:1] == ident, reactants[:, 1:2] == ident], 0
    ).astype(BF16)
    ident = lax.broadcasted_iota(jnp.int32, (species, reactions), 0)
    net = (
        products.T
        - (reactants.T[0:1] == ident).astype(jnp.int32)
        - (reactants.T[1:2] == ident).astype(jnp.int32)
    ).astype(BF16)
    coeff = jnp.broadcast_to(rate_coeff[:, None], (reactions, 256))

    sent = call(
        pack_kernel, blocks(8, 56), [VMEM] * 5,
        args=(tracers.reshape(-1, 128), air_mass, flux_x, flux_y, flux_z),
    )
    state = swap(sent)
    weather, *edges = call(
        edge_kernel,
        [blocks(STEPS, 8), blocks(74), blocks(76), blocks(100), blocks(104)],
        [SMEM, VMEM],
        args=(record_of_step, state),
    )
    scratch = [pltpu.VMEM((species, 128 * ROWS), BF16), pltpu.VMEM((reactions, 256), BF16)]
    weights = (14, 24, 128)
    state, later, *edges = call(
        first_kernel,
        [
            blocks(8, 48), jax.ShapeDtypeStruct(weights, F32),
            blocks(72), blocks(72), blocks(96), blocks(96),
        ],
        [SMEM] + [VMEM] * 9,
        [pltpu.VMEM(weights, F32), pltpu.VMEM((2, 32, 128), F32)] + scratch,
        (place, state, weather) + halo(*edges) + (selector, net, coeff),
    )
    state = call(
        second_kernel,
        blocks(8, 48),
        [VMEM] * 9,
        scratch,
        (later, state) + halo(*edges) + (selector, net, coeff),
    )
    out = call(
        unpack_kernel, jax.ShapeDtypeStruct((tracers.size // 128, 128), F32), [VMEM],
        args=(swap(state),),
    )
    return out.reshape(tracers.shape)


def solution(mesh):
    fields = P("tracer", None, "tile", None)
    return jax.shard_map(
        per_device,
        mesh=mesh,
        in_specs=(fields,) * 5 + (P(),) * 4,
        out_specs=fields,
        check_vma=False,
    )
```

```python
import functools

import jax
import jax.numpy as jnp
from jax import lax
from jax.experimental import pallas as pl
from jax.experimental.pallas import tpu as pltpu
from jax.sharding import PartitionSpec as P

STEPS = 2
F32 = jnp.float32
BF16 = jnp.bfloat16
ROWS = 16
GROUPS = 24
BLOCK = 8
ORDER = (0, 2, 4, 6, 7, 5, 3, 1)
XA, XB, XC, YA, YB, YC, WA, WB, WC, ZA, ZB, ZC, MASS, INV = range(14)
VMEM = pl.BlockSpec(memory_space=pltpu.VMEM)
SMEM = pl.BlockSpec(memory_space=pltpu.SMEM)


def roll(x, shift):
    return pltpu.roll(x, shift % 128, axis=1)


def lane_of(shape):
    return lax.broadcasted_iota(jnp.int32, shape, 1)


def slot_of(shape):
    return lane_of(shape) & 15


def exchange_blocks(vectors):
    block = lane_of(vectors[0].shape) >> 4
    out = list(vectors)
    for bit in (1, 2, 4):
        low = (block & bit) == 0
        for i in range(8):
            if i & bit:
                continue
            first, second = out[i], out[i | bit]
            out[i] = jnp.where(low, first, roll(second, 16 * bit))
            out[i | bit] = jnp.where(low, roll(first, -16 * bit), second)
    return out


def pack_kernel(q_ref, mass_ref, fx_ref, fy_ref, fz_ref, out_ref):
    def row(r, carry):
        levels = [q_ref[pl.ds(lev * 16 + r, 24, stride=128), :] for lev in range(8)]
        for place, value in enumerate(exchange_blocks(levels)):
            out_ref[ORDER[place], pl.ds(3 * r, 3)] = value.reshape(3, 8, 128)
        return carry

    lax.fori_loop(0, ROWS, row, 0, unroll=2)
    for field, ref in enumerate((mass_ref, fx_ref, fy_ref, fz_ref)):
        levels = [ref[0, lev] for lev in range(8)]
        for place, value in enumerate(exchange_blocks(levels)):
            out_ref[ORDER[place], 48 + 2 * field : 50 + 2 * field] = value.reshape(2, 8, 128)


def unpack_kernel(in_ref, out_ref):
    def row(r, carry):
        cols = [in_ref[src, pl.ds(3 * r, 3)].reshape(24, 128) for src in ORDER]
        for lev, value in enumerate(exchange_blocks(cols)):
            out_ref[pl.ds(lev * 16 + r, 24, stride=128), :] = value
        return carry

    lax.fori_loop(0, ROWS, row, 0, unroll=2)


def write_edges(state_ref, row_up, row_down, col_right, col_left):
    slot = slot_of((32, 128)) >> 2

    def group(g, carry):
        src = g // 3
        tg = g - 3 * src
        for rr in range(3):
            row_down[src * 9 + 3 * rr + tg] = state_ref[src, 3 * rr + tg]
            row_up[src * 9 + 3 * rr + tg] = state_ref[src, 3 * (13 + rr) + tg]
        rows = [
            jnp.concatenate([state_ref[src, 3 * (4 * block + i) + tg] for block in range(4)], 0)
            for i in range(4)
        ]
        right, left = rows[3], rows[0]
        for i in range(3):
            right = jnp.where(slot == i, roll(rows[i], 4 * i - 12), right)
            left = jnp.where(slot == i + 1, roll(rows[i + 1], 4 * i + 4), left)
        col_right[pl.ds(g * 4, 4)] = right.reshape(4, 8, 128)
        col_left[pl.ds(g * 4, 4)] = left.reshape(4, 8, 128)
        return carry

    lax.fori_loop(0, GROUPS, group, 0, unroll=2)


def narrow(wide_refs, out_refs):
    for wide, out in zip(wide_refs, out_refs):
        out[...] = wide[...].reshape(out.shape).astype(BF16)


def widen(in_refs, wide_refs):
    for ref, wide in zip(in_refs, wide_refs):
        wide[...] = ref[...].astype(F32).reshape(wide.shape)


def edge_kernel(rec_ref, in_ref, weather_ref, *refs):
    out_refs, edges = refs[:4], refs[4:]
    row_up, row_down, col_right, col_left = edges
    write_edges(in_ref, *edges)
    for s in range(STEPS):
        record = rec_ref[s]
        for k in range(8):
            weather_ref[s, k] = in_ref[record, 48 + k]
        row_up[72 + s] = in_ref[record, 48 + 1]
        row_down[72 + 2 * s] = in_ref[record, 48 + 0]
        row_down[72 + 2 * s + 1] = in_ref[record, 48 + 2]
        for half in range(2):
            col_right[96 + 2 * s + half] = in_ref[record, 48 + half]
            col_left[96 + 4 * s + half] = in_ref[record, 48 + half]
            col_left[96 + 4 * s + 2 + half] = in_ref[record, 48 + 4 + half]
    narrow(edges, out_refs)


def face_weights(flux, mass_low, mass_up):
    upwind = jnp.where(flux > 0, mass_low, mass_up)
    c = jnp.abs(flux) / jnp.maximum(upwind, 0.5)
    side = flux * c
    return flux * (1.0 - c) * (1.0 - c), side * (c - 1.0), side * (3.0 - 2.0 * c)


def write_weights(s, place_ref, weather_ref, row_lo, row_hi, col_lo, col_hi, ext_ref, put):
    tile, col = place_ref[0], place_ref[1]

    def both(ref, *index):
        return jnp.concatenate(
            [ref[index[:-1] + (index[-1],)], ref[index[:-1] + (index[-1] + 1,)]], 0
        )

    mass = both(weather_ref, s, 0)
    ext_ref[0, 0:8] = row_lo[72 + s]
    ext_ref[0, 8:24] = mass
    ext_ref[0, 24:32] = row_hi[72 + 2 * s]
    row = lax.broadcasted_iota(jnp.int32, (16, 128), 0)
    ext_ref[1, 0:16] = jnp.where((row == 0) & (tile == 0), 0.0, both(weather_ref, s, 2))
    ext_ref[1, 16:24] = row_hi[72 + 2 * s + 1]
    ext_ref[1, 24:32] = jnp.zeros((8, 128), F32)
    east = ext_ref[1, 0:24]
    for k, value in enumerate(face_weights(east, ext_ref[0, 7:31], ext_ref[0, 8:32])):
        put(XA + k, 24, value)
    shape = (16, 128)
    slot, lane = slot_of(shape), lane_of(shape)
    mass_x = jnp.where(slot < 8, roll(both(col_hi, 96 + 4 * s), 16), roll(both(col_lo, 96 + 2 * s), -16))
    south = jnp.where((slot == 0) & (col == 0), 0.0, both(weather_ref, s, 4))
    south_x = roll(both(col_hi, 96 + 4 * s + 2), 16)
    low = roll(jnp.where(slot == 15, mass_x, mass), 1)
    for k, value in enumerate(face_weights(south, low, mass)):
        put(YA + k, 16, value)
    low = roll(jnp.where(slot == 15, mass, mass_x), 1)
    for k, value in enumerate(face_weights(south_x, low, mass_x)):
        put(WA + k, 16, value)
    bottom = jnp.where(lane < 16, 0.0, both(weather_ref, s, 6))
    for k, value in enumerate(face_weights(bottom, roll(mass, 16), mass)):
        put(ZA + k, 16, value)
    new_mass = (
        mass
        - (ext_ref[1, 1:17] - ext_ref[1, 0:16])
        - (roll(jnp.where(slot == 0, south_x, south), -1) - south)
        - (roll(bottom, -16) - bottom)
    )
    put(MASS, 16, mass)
    put(INV, 16, 1.0 / new_mass)


def edge_value(low2, low1, up1, up2):
    value = (7.0 / 12.0) * (low1 + up1) - (1.0 / 12.0) * (low2 + up2)
    return jnp.minimum(
        jnp.maximum(value, jnp.minimum(low1, up1)), jnp.maximum(low1, up1)
    )


def face_flux(weights, edge, below, above, q_low, q_up):
    a, b, c = weights
    forward = c > 0
    return a * edge + b * jnp.where(forward, below, above) + c * jnp.where(forward, q_low, q_up)


def advect(q_ref, row_lo, row_hi, col_lo, col_hi, get, out_ref, conc_ref):
    def x_difference(src, tg):
        def q_row(k):
            if k < 0:
                return row_lo[src * 9 + 3 * (k + 3) + tg]
            if k >= ROWS:
                return row_hi[src * 9 + 3 * (k - ROWS) + tg]
            return q_ref[src, 3 * k + tg]

        q = {k: q_row(k) for k in (-3, -2, -1, 0)}
        edges = {}

        def x_edge(k):
            for need in (k - 2, k - 1, k, k + 1):
                if need not in q:
                    q[need] = q_row(need)
            if k not in edges:
                edges[k] = edge_value(q[k - 2], q[k - 1], q[k], q[k + 1])
            return edges[k]

        def x_flux(r):
            return face_flux(
                [get(XA + i, r) for i in range(3)],
                x_edge(r), x_edge(r - 1), x_edge(r + 1), q[r - 1], q[r],
            )

        below = x_flux(0)
        for r in range(ROWS):
            above = x_flux(r + 1)
            out_ref[src, 3 * r + tg] = get(MASS, r) * q[r] - (above - below)
            below = above

    def stack(parts):
        return jnp.concatenate(parts, 0)

    def yz_part(members, rows):
        where = [(src, tg, r) for src, tg in members for r in rows]
        wide = (8 * len(where), 128)
        slot, lane = slot_of(wide), lane_of(wide)
        first, last, last_two, left_half = slot == 0, slot == 15, slot >= 14, slot < 8

        def weight(k):
            return stack([get(k, r) for _, _, r in where])

        def weights(k):
            return [weight(k + i) for i in range(3)]

        here = stack([q_ref[src, 3 * r + tg] for src, tg, r in where])
        x = jnp.where(
            left_half,
            stack([roll(col_hi[(3 * src + tg) * 4 + r // 4], 16 - 4 * (r % 4)) for src, tg, r in where]),
            stack([roll(col_lo[(3 * src + tg) * 4 + r // 4], -4 - 4 * (r % 4)) for src, tg, r in where]),
        )
        m1 = roll(jnp.where(last, x, here), 1)
        m2 = roll(jnp.where(last_two, x, here), 2)
        p1 = roll(jnp.where(first, x, here), -1)
        x_m1 = roll(jnp.where(last, here, x), 1)
        x_m2 = roll(jnp.where(last_two, here, x), 2)
        x_p1 = roll(jnp.where(first, here, x), -1)
        edge = edge_value(m2, m1, here, p1)
        edge_x = edge_value(x_m2, x_m1, x, x_p1)
        flux_y = face_flux(
            weights(YA), edge,
            roll(jnp.where(last, edge_x, edge), 1),
            roll(jnp.where(first, edge_x, edge), -1), m1, here,
        )
        flux_w = face_flux(
            weights(WA), edge_x,
            roll(jnp.where(last, edge, edge_x), 1), roll(edge_x, -1), x_m1, x,
        )
        total = roll(jnp.where(first, flux_w, flux_y), -1) - flux_y
        m1 = jnp.where(lane >= 16, roll(here, 16), 0.0)
        m2 = jnp.where(lane >= 32, roll(here, 32), 0.0)
        p1 = jnp.where(lane < 112, roll(here, -16), 0.0)
        edge = edge_value(m2, m1, here, p1)
        top = (7.0 / 12.0) * here - (1.0 / 12.0) * m1
        top = jnp.minimum(jnp.maximum(top, jnp.minimum(here, 0.0)), jnp.maximum(here, 0.0))
        flux_z = face_flux(
            weights(ZA), edge, roll(edge, 16),
            jnp.where(lane >= 112, top, roll(edge, -16)), m1, here,
        )
        total = total + (roll(flux_z, -16) - flux_z)
        partial = stack([out_ref[src, 3 * r + tg] for src, tg, r in where])
        moved = (partial - total) * weight(INV)
        result = []
        for n, (src, tg, r) in enumerate(where):
            result.append(moved[8 * n : 8 * n + 8])
            out_ref[src, 3 * r + tg] = result[-1]
        return result

    def pair(p, carry):
        members = []
        for k in range(2):
            g = 2 * p + k
            src = g // 3
            members.append((src, g - 3 * src))
        for src, tg in members:
            x_difference(src, tg)
        start = pl.multiple_of(16 * p, 16)
        for block in range(ROWS // BLOCK):
            rows = range(BLOCK * block, BLOCK * block + BLOCK)
            parts = yz_part(members, rows)
            for i, r in enumerate(rows):
                conc_ref[pl.ds(start, 16), 128 * r : 128 * r + 128] = jnp.concatenate(
                    [parts[i], parts[BLOCK + i]], 0
                ).astype(BF16)
        return carry

    lax.fori_loop(0, GROUPS // 2, pair, 0)


def react(conc_ref, sel_ref, net_ref, coeff_ref, rate_ref, out_ref):
    def block(n, carry):
        lanes = pl.ds(pl.multiple_of(256 * n, 256), 256)
        conc = conc_ref[:, lanes]
        for k in range(4):
            part = slice(128 * k, 128 * k + 128)
            one = jnp.dot(sel_ref[part, :], conc, preferred_element_type=F32)
            two = jnp.dot(
                sel_ref[512 + 128 * k : 640 + 128 * k, :], conc, preferred_element_type=F32
            )
            rate_ref[part, :] = (coeff_ref[part, :] * one * two).astype(BF16)
        change = jnp.dot(net_ref[...], rate_ref[...], preferred_element_type=F32)
        change = change.astype(BF16).astype(F32)
        for i in range(2):
            r = 2 * n + i
            for g in range(GROUPS):
                part = change[8 * g : 8 * g + 8, 128 * i : 128 * i + 128]
                out_ref[g // 3, 3 * r + g % 3] += part
        return carry

    lax.fori_loop(0, ROWS // 2, block, 0)


def first_kernel(
    place_ref, q_ref, weather_ref, lo_ref, hi_ref, left_ref, right_ref, sel_ref, net_ref, coeff_ref,
    out_ref, later_ref, up_out, down_out, right_out, left_out,
    now_ref, ext_ref, conc_ref, rate_ref, row_lo, row_hi, col_lo, col_hi,
):
    halos = (row_lo, row_hi, col_lo, col_hi)
    widen((lo_ref, hi_ref, left_ref, right_ref), halos)
    for s, ref in enumerate((now_ref, later_ref)):
        def put(k, rows, value, ref=ref):
            ref[k, 0:rows] = value

        write_weights(s, place_ref, weather_ref, *halos, ext_ref, put)

    def get(k, r):
        return now_ref[k, pl.ds(r, 8, stride=0), :]

    advect(q_ref, *halos, get, out_ref, conc_ref)
    react(conc_ref, sel_ref, net_ref, coeff_ref, rate_ref, out_ref)
    edges = (row_lo.at[0:72], row_hi.at[0:72], col_lo.at[0:96], col_hi.at[0:96])
    write_edges(out_ref, *edges)
    narrow(edges, (up_out, down_out, right_out, left_out))


def second_kernel(
    now_ref, q_ref, lo_ref, hi_ref, left_ref, right_ref, sel_ref, net_ref, coeff_ref,
    out_ref, conc_ref, rate_ref, *halos,
):
    widen((lo_ref, hi_ref, left_ref, right_ref), halos)

    def get(k, r):
        return now_ref[k, pl.ds(r, 8, stride=0), :]

    advect(q_ref, *halos, get, out_ref, conc_ref)
    react(conc_ref, sel_ref, net_ref, coeff_ref, rate_ref, out_ref)


def blocks(*lead):
    return jax.ShapeDtypeStruct(lead + (8, 128), F32)


def call(kernel, outs, specs, scratch=(), args=()):
    single = not isinstance(outs, (list, tuple))
    return pl.pallas_call(
        kernel,
        out_shape=outs,
        in_specs=specs,
        out_specs=VMEM if single else [VMEM] * len(outs),
        scratch_shapes=list(scratch),
        compiler_params=pltpu.CompilerParams(vmem_limit_bytes=40 * 2**20),
    )(*args)


def swap(x):
    return lax.all_to_all(x, "tracer", split_axis=0, concat_axis=0, tiled=True)


def halo(row_up, row_down, col_right, col_left):
    tiles = [(i, i + 1) for i in range(lax.axis_size("tile") - 1)]
    columns = list(zip(ORDER[:-1], ORDER[1:]))

    def back(pairs):
        return [(target, source) for source, target in pairs]

    return (
        lax.ppermute(row_up, "tile", tiles),
        lax.ppermute(row_down, "tile", back(tiles)),
        lax.ppermute(col_right, "tracer", columns),
        lax.ppermute(col_left, "tracer", back(columns)),
    )


def per_device(
    tracers, air_mass, flux_x, flux_y, flux_z, reactants, products, rate_coeff, record_of_step
):
    reactions, species = products.shape
    place = jnp.stack([lax.axis_index("tile"), lax.axis_index("tracer")]).astype(jnp.int32)
    ident = lax.broadcasted_iota(jnp.int32, (reactions, species), 1)
    selector = jnp.concatenate(
        [reactants[:, 0:1] == ident, reactants[:, 1:2] == ident], 0
    ).astype(BF16)
    ident = lax.broadcasted_iota(jnp.int32, (species, reactions), 0)
    net = (
        products.T
        - (reactants.T[0:1] == ident).astype(jnp.int32)
        - (reactants.T[1:2] == ident).astype(jnp.int32)
    ).astype(BF16)
    coeff = jnp.broadcast_to(rate_coeff[:, None], (reactions, 256))

    sent = call(
        pack_kernel, blocks(8, 56), [VMEM] * 5,
        args=(tracers.reshape(-1, 128), air_mass, flux_x, flux_y, flux_z),
    )
    state = swap(sent)
    def narrow_blocks(*counts):
        return [jax.ShapeDtypeStruct((8 * count, 128), BF16) for count in counts]

    def wide_blocks(*counts):
        return [pltpu.VMEM((count, 8, 128), F32) for count in counts]

    first, plain = (74, 76, 100, 104), (72, 72, 96, 96)
    weather, *edges = call(
        edge_kernel,
        [blocks(STEPS, 8)] + narrow_blocks(*first),
        [SMEM, VMEM],
        wide_blocks(*first),
        (record_of_step, state),
    )
    scratch = [pltpu.VMEM((species, 128 * ROWS), BF16), pltpu.VMEM((reactions, 256), BF16)]
    weights = (14, 24, 128)
    state, later, *edges = call(
        first_kernel,
        [blocks(8, 48), jax.ShapeDtypeStruct(weights, F32)] + narrow_blocks(*plain),
        [SMEM] + [VMEM] * 9,
        [pltpu.VMEM(weights, F32), pltpu.VMEM((2, 32, 128), F32)] + scratch + wide_blocks(*first),
        (place, state, weather) + halo(*edges) + (selector, net, coeff),
    )
    state = call(
        second_kernel,
        blocks(8, 48),
        [VMEM] * 9,
        scratch + wide_blocks(*plain),
        (later, state) + halo(*edges) + (selector, net, coeff),
    )
    out = call(
        unpack_kernel, jax.ShapeDtypeStruct((tracers.size // 128, 128), F32), [VMEM],
        args=(swap(state),),
    )
    return out.reshape(tracers.shape)


def solution(mesh):
    fields = P("tracer", None, "tile", None)
    return jax.shard_map(
        per_device,
        mesh=mesh,
        in_specs=(fields,) * 5 + (P(),) * 4,
        out_specs=fields,
        check_vma=False,
    )
```

```python
import jax
import jax.numpy as jnp
from jax import lax
from jax.experimental import pallas as pl
from jax.experimental.pallas import tpu as pltpu
from jax.sharding import PartitionSpec as P

STEPS = 2
F32 = jnp.float32
BF16 = jnp.bfloat16
ROWS = 16
COLS = 16
LANES = 256
ORDER = (0, 2, 4, 6, 7, 5, 3, 1)
XA, YA, ZA, MASS, INV, WA = 0, 3, 6, 9, 10, 11
VMEM = pl.BlockSpec(memory_space=pltpu.VMEM)
SMEM = pl.BlockSpec(memory_space=pltpu.SMEM)


def roll(x, shift):
    return pltpu.roll(x, shift % 128, axis=1)


def lane_of(shape):
    return lax.broadcasted_iota(jnp.int32, shape, 1)


def exchange_blocks(vectors):
    block = lane_of(vectors[0].shape) >> 4
    out = list(vectors)
    for bit in (1, 2, 4):
        low = (block & bit) == 0
        for i in range(8):
            if i & bit:
                continue
            first, second = out[i], out[i | bit]
            out[i] = jnp.where(low, first, roll(second, 16 * bit))
            out[i | bit] = jnp.where(low, roll(first, -16 * bit), second)
    return out


def pack_kernel(q_ref, mass_ref, fx_ref, fy_ref, fz_ref, out_ref):
    def row(r, carry):
        levels = [q_ref[pl.ds(lev * 16 + r, 24, stride=128), :] for lev in range(8)]
        for place, value in enumerate(exchange_blocks(levels)):
            out_ref[ORDER[place], pl.ds(3 * r, 3)] = value.reshape(3, 8, 128)
        return carry

    lax.fori_loop(0, ROWS, row, 0, unroll=2)
    for field, ref in enumerate((mass_ref, fx_ref, fy_ref, fz_ref)):
        for half in range(2):
            rows = [ref[pl.ds(8 * half + r, 8, stride=16), :] for r in range(8)]
            for place, value in enumerate(exchange_blocks(rows)):
                out_ref[ORDER[place], 48 + 2 * field + half] = value


def unpack_kernel(in_ref, out_ref):
    def row(r, carry):
        cols = [in_ref[src, pl.ds(3 * r, 3)].reshape(24, 128) for src in ORDER]
        for lev, value in enumerate(exchange_blocks(cols)):
            out_ref[pl.ds(lev * 16 + r, 24, stride=128), :] = value
        return carry

    lax.fori_loop(0, ROWS, row, 0, unroll=2)


def cell(c):
    return pl.ds(8 * (c + 3), 8)


def write_edges(state_ref, row_up, row_down, col_right, col_left):
    inner = pl.ds(24, 128)
    for k in range(3):
        row_up[128 * k : 128 * k + 128] = state_ref[16 + k, inner].astype(BF16)
        row_down[128 * k : 128 * k + 128] = state_ref[3 + k, inner].astype(BF16)
    for pair in range(ROWS // 2):
        for out, start in ((col_right, 128), (col_left, 24)):
            both = [state_ref[3 + 2 * pair + i, pl.ds(start, 24)] for i in range(2)]
            out[48 * pair : 48 * pair + 48] = jnp.concatenate(both, 0).astype(BF16)


def read_edges(state_ref, row_lo, row_hi, col_lo, col_hi):
    inner = pl.ds(24, 128)
    for k in range(3):
        state_ref[k, inner] = row_lo[128 * k : 128 * k + 128].astype(F32)
        state_ref[19 + k, inner] = row_hi[128 * k : 128 * k + 128].astype(F32)
    for pair in range(ROWS // 2):
        for ref, start in ((col_lo, 0), (col_hi, 152)):
            both = ref[48 * pair : 48 * pair + 48].astype(F32)
            for i in range(2):
                state_ref[3 + 2 * pair + i, pl.ds(start, 24)] = both[24 * i : 24 * i + 24]


def arrange_kernel(
    rec_ref, in_ref, state_ref, weather_ref, row_up, row_down, col_right, col_left, turn_ref
):
    def row(r, carry):
        parts = [in_ref[src, pl.ds(3 * r, 3)].reshape(24, 128) for src in range(8)]
        parts.append(jnp.zeros((LANES - 192, 128), F32))
        stacked = jnp.concatenate(parts, 0)
        for half in range(2):
            turned = stacked[128 * half : 128 * half + 128].T
            for i in range(16):
                start = 128 * (2 * (r & 1) + half) + 64 * (i % 2) + i // 2
                turn_ref[pl.ds(start, 8, stride=8), :] = turned[8 * i : 8 * i + 8]
            whole = turn_ref[pl.ds(pl.multiple_of(128 * (2 * (r & 1) + half), 128), 128), :]
            state_ref[r + 3, pl.ds(24, 128), 128 * half : 128 * half + 128] = whole
        return carry

    lax.fori_loop(0, ROWS, row, 0, unroll=2)
    write_edges(state_ref, row_up, row_down, col_right, col_left)

    def lanes(*blocks):
        return jnp.concatenate(blocks, 1)

    ups, downs, rights, lefts = [], [], [], []
    zero = jnp.zeros((8, 128), F32)
    for s in range(STEPS):
        record = rec_ref[s]
        got = [in_ref[record, 48 + k] for k in range(8)]
        for k in range(8):
            weather_ref[s, k] = got[k]
        ups.append(lanes(got[1], zero))
        downs.append(lanes(got[0], got[2]))
        rights.append(lanes(got[0], got[1]))
        lefts += [lanes(got[0], got[1]), lanes(got[4], got[5])]
    row_up[384:400] = jnp.concatenate(ups, 0).astype(BF16)
    row_down[384:400] = jnp.concatenate(downs, 0).astype(BF16)
    col_right[384:400] = jnp.concatenate(rights, 0).astype(BF16)
    col_left[384:416] = jnp.concatenate(lefts, 0).astype(BF16)


def face_weights(flux, mass_low, mass_up):
    upwind = jnp.where(flux > 0, mass_low, mass_up)
    c = jnp.abs(flux) / jnp.maximum(upwind, 0.5)
    side = flux * c
    return [flux * (1.0 - c) * (1.0 - c), side * (c - 1.0), side * (3.0 - 2.0 * c)]


def write_weights(s, place_ref, weather_ref, row_lo, row_hi, col_lo, col_hi, out_ref):
    tile, column = place_ref[0], place_ref[1]
    shape = (8, 128)
    lane = lane_of(shape)
    slot, group = lane & 15, lane >> 4
    level = lax.broadcasted_iota(jnp.int32, shape, 0)
    zero = jnp.zeros(shape, F32)

    def edge(ref, start, s):
        both = ref[384 + start : 400 + start].astype(F32)[8 * s : 8 * s + 8]
        return both[:, 0:128], both[:, 128:256]

    mass = [weather_ref[s, 0], weather_ref[s, 1]]
    east = [weather_ref[s, 2], weather_ref[s, 3]]
    south = [weather_ref[s, 4], weather_ref[s, 5]]
    bottom = [weather_ref[s, 6], weather_ref[s, 7]]
    mass_before, _ = edge(row_lo, 0, s)
    mass_after, east_after = edge(row_hi, 0, s)
    mass_left = edge(col_lo, 0, s)
    lefts = col_hi[384:416].astype(F32)[16 * s : 16 * s + 16]
    mass_right = [lefts[0:8, 128 * h : 128 * h + 128] for h in range(2)]
    south_right = [lefts[8:16, 128 * h : 128 * h + 128] for h in range(2)]
    east[0] = jnp.where((group == 0) & (tile == 0), 0.0, east[0])
    mass_rows = [mass_before] + mass + [mass_after]
    east_rows = east + [east_after]
    for h in range(2):
        here = mass[h]
        south_h = jnp.where((slot == 0) & (column == 0), 0.0, south[h])
        bottom_h = jnp.where(level == 0, 0.0, bottom[h])
        before = jnp.where(group == 0, roll(mass_rows[h], 16), roll(here, 16))
        east_up = jnp.where(group == 7, roll(east_rows[h + 1], -16), roll(east[h], -16))
        left = jnp.where(slot == 0, roll(mass_left[h], -15), roll(here, 1))
        south_up = jnp.where(slot == 15, roll(south_right[h], 15), roll(south_h, -1))
        below = jnp.concatenate([here[0:1], here[0:7]], 0)
        bottom_up = jnp.concatenate([bottom_h[1:8], zero[0:1]], 0)
        new_mass = here - (east_up - east[h]) - (south_up - south_h) - (bottom_up - bottom_h)
        fields = (
            face_weights(east[h], before, here)
            + face_weights(south_h, left, here)
            + face_weights(bottom_h, below, here)
            + [here, 1.0 / new_mass]
            + face_weights(south_right[h], roll(here, -15), mass_right[h])
            + [zero, zero]
        )
        for part in range(2):
            for r, value in enumerate(exchange_blocks(fields[8 * part : 8 * part + 8])):
                out_ref[8 * h + r, part] = value
    last = face_weights(east_after, roll(mass[1], 16), mass_after)
    out_ref[16, 0] = exchange_blocks(last + [zero] * 5)[0]


def edge_value(low2, low1, up1, up2):
    value = (7.0 / 12.0) * (low1 + up1) - (1.0 / 12.0) * (low2 + up2)
    return jnp.minimum(
        jnp.maximum(value, jnp.minimum(low1, up1)), jnp.maximum(low1, up1)
    )


def face_flux(weights, edge, below, above, q_low, q_up):
    a, b, c = weights
    forward = c > 0
    return a * edge + b * jnp.where(forward, below, above) + c * jnp.where(forward, q_low, q_up)


def advect(state, weight_ref, x_edges, x_flux, z_q, z_edge, z_flux):
    def pick(ref_value, field, c):
        lane = 16 * (field % 8) + c
        return jnp.broadcast_to(ref_value[:, lane : lane + 1], (8, LANES))

    zero = jnp.zeros((16 * COLS + 16, LANES), F32)
    z_q[...] = zero
    z_edge[...] = zero
    z_flux[...] = zero
    first = weight_ref[0, 0]
    for c in range(COLS):
        q = [state[k, cell(c)] for k in range(6)]
        edges = [edge_value(*q[k : k + 4]) for k in range(3)]
        for k in range(3):
            x_edges[k, c] = edges[k]
        weights = [pick(first, XA + i, c) for i in range(3)]
        x_flux[c] = face_flux(weights, edges[1], edges[0], edges[2], q[2], q[3])

    def row(r, carry):
        main = [weight_ref[r, 0], weight_ref[r, 1]]
        ahead = weight_ref[r + 1, 0]

        def weight(field, c):
            return pick(main[field // 8], field, c)

        def z_rows(c, shift=0):
            return pl.ds(16 * c + 8 + shift, 8)

        loaded, edges = {}, {}

        def q_at(c):
            if c not in loaded:
                loaded[c] = state[r + 3, cell(c)]
            return loaded[c]

        def y_edge(c):
            if c not in edges:
                edges[c] = edge_value(q_at(c - 2), q_at(c - 1), q_at(c), q_at(c + 1))
            return edges[c]

        def y_face(c):
            weights = [weight(YA + i, c) if c < COLS else weight(WA + i, 0) for i in range(3)]
            return face_flux(
                weights, y_edge(c), y_edge(c - 1), y_edge(c + 1), q_at(c - 1), q_at(c)
            )

        flux_y = y_face(0)
        for c in range(COLS):
            here = q_at(c)
            z_q[z_rows(c), :] = here
            flux_y_up = y_face(c + 1)
            q1, q2, q3 = [state[r + 3 + k, cell(c)] for k in (1, 2, 3)]
            new_edge = edge_value(here, q1, q2, q3)
            x_edges[r + 3, c] = new_edge
            flux_x_up = face_flux(
                [pick(ahead, XA + i, c) for i in range(3)],
                x_edges[r + 2, c], x_edges[r + 1, c], new_edge, here, q1,
            )
            flux_x = x_flux[c]
            x_flux[c] = flux_x_up
            m2, m1 = z_q[z_rows(c, -2), :], z_q[z_rows(c, -1), :]
            p1, p2 = z_q[z_rows(c, 1), :], z_q[z_rows(c, 2), :]
            edge = edge_value(m2, m1, here, p1)
            z_edge[z_rows(c), :] = edge
            flux_z = face_flux(
                [weight(ZA + i, c) for i in range(3)],
                edge, z_edge[z_rows(c, -1), :], edge_value(m1, here, p1, p2), m1, here,
            )
            z_flux[z_rows(c), :] = flux_z
            total = (flux_x_up - flux_x) + (flux_y_up - flux_y) + (z_flux[z_rows(c, 1), :] - flux_z)
            state[r + 3, cell(c)] = (weight(MASS, c) * here - total) * weight(INV, c)
            flux_y = flux_y_up
        return carry

    lax.fori_loop(0, ROWS, row, 0)


def react(state, sel_ref, net_ref, coeff_ref, rate_ref):
    def block(n, carry):
        rows = [3 + 4 * n + i for i in range(4)]
        inner = pl.ds(24, 128)
        conc = jnp.concatenate([state[r, inner] for r in rows], 0).astype(BF16)
        for k in range(2):
            part = slice(256 * k, 256 * k + 256)
            one = jnp.dot(conc, sel_ref[:, part], preferred_element_type=F32)
            two = jnp.dot(
                conc, sel_ref[:, 512 + 256 * k : 768 + 256 * k], preferred_element_type=F32
            )
            rate_ref[:, part] = (coeff_ref[:, part] * one * two).astype(BF16)
        change = jnp.dot(rate_ref[...], net_ref[...], preferred_element_type=F32)
        change = change.astype(BF16).astype(F32)
        for i, r in enumerate(rows):
            state[r, inner] += change[128 * i : 128 * i + 128]
        return carry

    lax.fori_loop(0, ROWS // 4, block, 0)


def first_kernel(
    place_ref, weather_ref, row_lo, row_hi, col_lo, col_hi, sel_ref, net_ref, coeff_ref, in_ref,
    state, later_ref, row_up, row_down, col_right, col_left, now_ref, rate_ref, *work
):
    del in_ref
    halos = (row_lo, row_hi, col_lo, col_hi)
    for s, ref in enumerate((now_ref, later_ref)):
        write_weights(s, place_ref, weather_ref, *halos, ref)
    read_edges(state, *halos)
    advect(state, now_ref, *work)
    react(state, sel_ref, net_ref, coeff_ref, rate_ref)
    write_edges(state, row_up, row_down, col_right, col_left)


def second_kernel(
    weight_ref, row_lo, row_hi, col_lo, col_hi, sel_ref, net_ref, coeff_ref, in_ref,
    state, out_ref, turn_ref, rate_ref, *work
):
    del in_ref
    read_edges(state, row_lo, row_hi, col_lo, col_hi)
    advect(state, weight_ref, *work)
    react(state, sel_ref, net_ref, coeff_ref, rate_ref)

    def row(r, carry):
        turned = []
        for half in range(2):
            base = 128 * (2 * (r & 1) + half)
            whole = state[r + 3, pl.ds(24, 128), 128 * half : 128 * half + 128]
            turn_ref[pl.ds(pl.multiple_of(base, 128), 128), :] = whole
            parts = [
                turn_ref[pl.ds(base + 64 * (i % 2) + i // 2, 8, stride=8), :] for i in range(16)
            ]
            turned.append(jnp.concatenate(parts, 0).T)
        turned = jnp.concatenate([turned[0], turned[1][0:64]], 0)
        for dest in range(8):
            out_ref[dest, pl.ds(3 * r, 3)] = turned[24 * dest : 24 * dest + 24].reshape(3, 8, 128)
        return carry

    lax.fori_loop(0, ROWS, row, 0, unroll=2)


def blocks(*lead):
    return jax.ShapeDtypeStruct(lead + (8, 128), F32)


def call(kernel, outs, specs, scratch=(), args=(), aliases=None):
    single = not isinstance(outs, (list, tuple))
    return pl.pallas_call(
        kernel,
        out_shape=outs,
        in_specs=specs,
        out_specs=VMEM if single else [VMEM] * len(outs),
        scratch_shapes=list(scratch),
        input_output_aliases=aliases or {},
        compiler_params=pltpu.CompilerParams(vmem_limit_bytes=40 * 2**20),
    )(*args)


def swap(x):
    return lax.all_to_all(x, "tracer", split_axis=0, concat_axis=0, tiled=True)


def halo(row_up, row_down, col_right, col_left):
    tiles = [(i, i + 1) for i in range(lax.axis_size("tile") - 1)]
    columns = list(zip(ORDER[:-1], ORDER[1:]))

    def back(pairs):
        return [(target, source) for source, target in pairs]

    return (
        lax.ppermute(row_up, "tile", tiles),
        lax.ppermute(row_down, "tile", back(tiles)),
        lax.ppermute(col_right, "tracer", columns),
        lax.ppermute(col_left, "tracer", back(columns)),
    )


def per_device(
    tracers, air_mass, flux_x, flux_y, flux_z, reactants, products, rate_coeff, record_of_step
):
    reactions, species = products.shape
    place = jnp.stack([lax.axis_index("tile"), lax.axis_index("tracer")]).astype(jnp.int32)
    pairs = reactants.T
    ident = lax.broadcasted_iota(jnp.int32, (LANES, reactions), 0)
    hot = [pairs[k : k + 1] == ident for k in range(2)]
    selector = jnp.concatenate(hot, 1).astype(BF16)
    ident = lax.broadcasted_iota(jnp.int32, (reactions, LANES), 1)
    net = jnp.pad(products, ((0, 0), (0, LANES - species)))
    for k in range(2):
        net = net - (reactants[:, k : k + 1] == ident).astype(jnp.int32)
    constants = (selector, net.astype(BF16), rate_coeff[None, :])

    sent = call(
        pack_kernel, blocks(8, 56), [VMEM] * 5,
        args=[x.reshape(-1, 128) for x in (tracers, air_mass, flux_x, flux_y, flux_z)],
    )

    def edge_blocks(*counts):
        return [jax.ShapeDtypeStruct((count, LANES), BF16) for count in counts]

    state_shape = jax.ShapeDtypeStruct((ROWS + 6, 8 * (COLS + 6), LANES), F32)
    turn = pltpu.VMEM((512, 128), F32)
    state, weather, *edges = call(
        arrange_kernel,
        [state_shape, blocks(STEPS, 8)] + edge_blocks(400, 400, 400, 416),
        [SMEM, VMEM],
        [turn],
        (record_of_step, swap(sent)),
    )
    column = pltpu.VMEM((16 * COLS + 16, LANES), F32)
    work = [
        pltpu.VMEM((512, reactions), BF16),
        pltpu.VMEM((19, COLS, 8, LANES), F32),
        pltpu.VMEM((COLS, 8, LANES), F32),
        column, column, column,
    ]
    weights = (ROWS + 1, 2, 8, 128)
    state, later, *edges = call(
        first_kernel,
        [state_shape, jax.ShapeDtypeStruct(weights, F32)] + edge_blocks(384, 384, 384, 384),
        [SMEM] + [VMEM] * 9,
        [pltpu.VMEM(weights, F32)] + work,
        (place, weather) + halo(*edges) + constants + (state,),
        {9: 0},
    )
    _, sent = call(
        second_kernel,
        [state_shape, blocks(8, 48)],
        [VMEM] * 9,
        [turn] + work,
        (later,) + halo(*edges) + constants + (state,),
        {8: 0},
    )
    out = call(
        unpack_kernel, jax.ShapeDtypeStruct((tracers.size // 128, 128), F32), [VMEM],
        args=(swap(sent),),
    )
    return out.reshape(tracers.shape)


def solution(mesh):
    fields = P("tracer", None, "tile", None)
    return jax.shard_map(
        per_device,
        mesh=mesh,
        in_specs=(fields,) * 5 + (P(),) * 4,
        out_specs=fields,
        check_vma=False,
    )
```

```python
import jax
import jax.numpy as jnp
from jax import lax
from jax.experimental import pallas as pl
from jax.experimental.pallas import tpu as pltpu
from jax.sharding import PartitionSpec as P

STEPS = 2
F32 = jnp.float32
BF16 = jnp.bfloat16
ROWS = 16
COLS = 16
STACK = 16
LANES = 256
ORDER = (0, 2, 4, 6, 7, 5, 3, 1)
XA, YA, ZA, MASS, INV, WA = 0, 3, 6, 9, 10, 11
VMEM = pl.BlockSpec(memory_space=pltpu.VMEM)
SMEM = pl.BlockSpec(memory_space=pltpu.SMEM)
ANY = pl.BlockSpec(memory_space=pltpu.HBM)


def roll(x, shift):
    return pltpu.roll(x, shift % 128, axis=1)


def lane_of(shape):
    return lax.broadcasted_iota(jnp.int32, shape, 1)


def exchange_blocks(vectors):
    block = lane_of(vectors[0].shape) >> 4
    out = list(vectors)
    for bit in (1, 2, 4):
        low = (block & bit) == 0
        for i in range(8):
            if i & bit:
                continue
            first, second = out[i], out[i | bit]
            out[i] = jnp.where(low, first, roll(second, 16 * bit))
            out[i | bit] = jnp.where(low, roll(first, -16 * bit), second)
    return out


def pack_kernel(
    q_hbm, mass_hbm, fx_hbm, fy_hbm, fz_hbm, out_hbm, q_ref, field_ref, out_ref, in_sem, out_sem
):
    fields = (mass_hbm, fx_hbm, fy_hbm, fz_hbm)
    loads = [
        pltpu.make_async_copy(hbm, field_ref.at[i], in_sem.at[i]) for i, hbm in enumerate(fields)
    ]
    for tg in range(3):
        part = pl.ds(1024 * tg, 1024)
        loads.append(pltpu.make_async_copy(q_hbm.at[part], q_ref.at[part], in_sem.at[4 + tg]))
    stores = []
    for i, (start, count) in enumerate(((48, 8), (0, 16), (16, 16), (32, 16))):
        part = pl.ds(start, count)
        stores.append(
            pltpu.make_async_copy(out_ref.at[:, part], out_hbm.at[:, part], out_sem.at[i])
        )
    for load in loads:
        load.start()
    for i in range(4):
        loads[i].wait()
    rows = [
        jnp.concatenate(
            [
                field_ref[i, pl.ds(8 * half + r, 8, stride=16), :]
                for i in range(4)
                for half in range(2)
            ],
            0,
        )
        for r in range(8)
    ]
    for place, value in enumerate(exchange_blocks(rows)):
        out_ref[ORDER[place], 48:56] = value.reshape(8, 8, 128)
    stores[0].start()
    for tg in range(3):
        loads[4 + tg].wait()

        def rows(k, carry, tg=tg):
            levels = [
                jnp.concatenate(
                    [
                        q_ref[pl.ds(1024 * tg + lev * 16 + STACK * k + i, 8, stride=128), :]
                        for i in range(STACK)
                    ],
                    0,
                )
                for lev in range(8)
            ]
            for place, value in enumerate(exchange_blocks(levels)):
                part = pl.ds(16 * tg + STACK * k, STACK)
                out_ref[ORDER[place], part] = value.reshape(STACK, 8, 128)
            return carry

        lax.fori_loop(0, ROWS // STACK, rows, 0)
        stores[1 + tg].start()
    for store in stores:
        store.wait()


def unpack_kernel(in_ref, out_hbm, out_ref, out_sem):
    stores = []
    for tg in range(3):
        part = pl.ds(1024 * tg, 1024)
        stores.append(pltpu.make_async_copy(out_ref.at[part], out_hbm.at[part], out_sem.at[tg]))
    for tg in range(3):

        def rows(k, carry, tg=tg):
            part = pl.ds(16 * tg + STACK * k, STACK)
            cols = [in_ref[src, part].reshape(8 * STACK, 128) for src in ORDER]
            for lev, value in enumerate(exchange_blocks(cols)):
                for i in range(STACK):
                    start = 1024 * tg + lev * 16 + STACK * k + i
                    out_ref[pl.ds(start, 8, stride=128), :] = value[8 * i : 8 * i + 8]
            return carry

        lax.fori_loop(0, ROWS // STACK, rows, 0)
        stores[tg].start()
    for store in stores:
        store.wait()


def cell(c):
    return pl.ds(8 * (c + 3), 8)


def write_edges(state_ref, row_up, row_down, col_right, col_left):
    inner = pl.ds(24, 128)
    for k in range(3):
        row_up[128 * k : 128 * k + 128] = state_ref[16 + k, inner].astype(BF16)
        row_down[128 * k : 128 * k + 128] = state_ref[3 + k, inner].astype(BF16)
    for pair in range(ROWS // 2):
        for out, start in ((col_right, 128), (col_left, 24)):
            both = [state_ref[3 + 2 * pair + i, pl.ds(start, 24)] for i in range(2)]
            out[48 * pair : 48 * pair + 48] = jnp.concatenate(both, 0).astype(BF16)


def read_edges(state_ref, row_lo, row_hi, col_lo, col_hi):
    inner = pl.ds(24, 128)
    for k in range(3):
        state_ref[k, inner] = row_lo[128 * k : 128 * k + 128].astype(F32)
        state_ref[19 + k, inner] = row_hi[128 * k : 128 * k + 128].astype(F32)
    for pair in range(ROWS // 2):
        for ref, start in ((col_lo, 0), (col_hi, 152)):
            both = ref[48 * pair : 48 * pair + 48].astype(F32)
            for i in range(2):
                state_ref[3 + 2 * pair + i, pl.ds(start, 24)] = both[24 * i : 24 * i + 24]


def arrange_kernel(
    rec_ref, in_ref, state_ref, weather_ref, row_up, row_down, col_right, col_left, turn_ref
):
    def row(r, carry):
        parts = [in_ref[src, 16 * tg + r] for src in range(8) for tg in range(3)]
        parts.append(jnp.zeros((LANES - 192, 128), F32))
        stacked = jnp.concatenate(parts, 0)
        for half in range(2):
            turned = stacked[128 * half : 128 * half + 128].T
            for i in range(16):
                start = 128 * (2 * (r & 1) + half) + 64 * (i % 2) + i // 2
                turn_ref[pl.ds(start, 8, stride=8), :] = turned[8 * i : 8 * i + 8]
            whole = turn_ref[pl.ds(pl.multiple_of(128 * (2 * (r & 1) + half), 128), 128), :]
            state_ref[r + 3, pl.ds(24, 128), 128 * half : 128 * half + 128] = whole
        return carry

    lax.fori_loop(0, ROWS, row, 0, unroll=2)
    write_edges(state_ref, row_up, row_down, col_right, col_left)

    def lanes(*blocks):
        return jnp.concatenate(blocks, 1)

    ups, downs, rights, lefts = [], [], [], []
    zero = jnp.zeros((8, 128), F32)
    for s in range(STEPS):
        record = rec_ref[s]
        got = [in_ref[record, 48 + k] for k in range(8)]
        for k in range(8):
            weather_ref[s, k] = got[k]
        ups.append(lanes(got[1], zero))
        downs.append(lanes(got[0], got[2]))
        rights.append(lanes(got[0], got[1]))
        lefts += [lanes(got[0], got[1]), lanes(got[4], got[5])]
    row_up[384:400] = jnp.concatenate(ups, 0).astype(BF16)
    row_down[384:400] = jnp.concatenate(downs, 0).astype(BF16)
    col_right[384:400] = jnp.concatenate(rights, 0).astype(BF16)
    col_left[384:416] = jnp.concatenate(lefts, 0).astype(BF16)


def face_weights(flux, mass_low, mass_up):
    upwind = jnp.where(flux > 0, mass_low, mass_up)
    c = jnp.abs(flux) / jnp.maximum(upwind, 0.5)
    side = flux * c
    return [flux * (1.0 - c) * (1.0 - c), side * (c - 1.0), side * (3.0 - 2.0 * c)]


def write_weights(s, place_ref, weather_ref, row_lo, row_hi, col_lo, col_hi, out_ref):
    tile, column = place_ref[0], place_ref[1]
    shape = (8, 128)
    lane = lane_of(shape)
    slot, group = lane & 15, lane >> 4
    level = lax.broadcasted_iota(jnp.int32, shape, 0)
    zero = jnp.zeros(shape, F32)

    def edge(ref, start, s):
        both = ref[384 + start : 400 + start].astype(F32)[8 * s : 8 * s + 8]
        return both[:, 0:128], both[:, 128:256]

    mass = [weather_ref[s, 0], weather_ref[s, 1]]
    east = [weather_ref[s, 2], weather_ref[s, 3]]
    south = [weather_ref[s, 4], weather_ref[s, 5]]
    bottom = [weather_ref[s, 6], weather_ref[s, 7]]
    mass_before, _ = edge(row_lo, 0, s)
    mass_after, east_after = edge(row_hi, 0, s)
    mass_left = edge(col_lo, 0, s)
    lefts = col_hi[384:416].astype(F32)[16 * s : 16 * s + 16]
    mass_right = [lefts[0:8, 128 * h : 128 * h + 128] for h in range(2)]
    south_right = [lefts[8:16, 128 * h : 128 * h + 128] for h in range(2)]
    east[0] = jnp.where((group == 0) & (tile == 0), 0.0, east[0])
    mass_rows = [mass_before] + mass + [mass_after]
    east_rows = east + [east_after]
    for h in range(2):
        here = mass[h]
        south_h = jnp.where((slot == 0) & (column == 0), 0.0, south[h])
        bottom_h = jnp.where(level == 0, 0.0, bottom[h])
        before = jnp.where(group == 0, roll(mass_rows[h], 16), roll(here, 16))
        east_up = jnp.where(group == 7, roll(east_rows[h + 1], -16), roll(east[h], -16))
        left = jnp.where(slot == 0, roll(mass_left[h], -15), roll(here, 1))
        south_up = jnp.where(slot == 15, roll(south_right[h], 15), roll(south_h, -1))
        below = jnp.concatenate([here[0:1], here[0:7]], 0)
        bottom_up = jnp.concatenate([bottom_h[1:8], zero[0:1]], 0)
        new_mass = here - (east_up - east[h]) - (south_up - south_h) - (bottom_up - bottom_h)
        fields = (
            face_weights(east[h], before, here)
            + face_weights(south_h, left, here)
            + face_weights(bottom_h, below, here)
            + [here, 1.0 / new_mass]
            + face_weights(south_right[h], roll(here, -15), mass_right[h])
            + [zero, zero]
        )
        for part in range(2):
            for r, value in enumerate(exchange_blocks(fields[8 * part : 8 * part + 8])):
                out_ref[8 * h + r, part] = value
    last = face_weights(east_after, roll(mass[1], 16), mass_after)
    out_ref[16, 0] = exchange_blocks(last + [zero] * 5)[0]


def edge_value(low2, low1, up1, up2):
    value = (7.0 / 12.0) * (low1 + up1) - (1.0 / 12.0) * (low2 + up2)
    return jnp.minimum(
        jnp.maximum(value, jnp.minimum(low1, up1)), jnp.maximum(low1, up1)
    )


def face_flux(weights, edge, below, above, q_low, q_up):
    a, b, c = weights
    forward = c > 0
    return a * edge + b * jnp.where(forward, below, above) + c * jnp.where(forward, q_low, q_up)


def advect(state, weight_ref, x_edges, x_flux, z_q, z_edge, z_flux):
    def pick(ref_value, field, c):
        lane = 16 * (field % 8) + c
        return jnp.broadcast_to(ref_value[:, lane : lane + 1], (8, LANES))

    zero = jnp.zeros((16 * COLS + 16, LANES), F32)
    z_q[...] = zero
    z_edge[...] = zero
    z_flux[...] = zero
    first = weight_ref[0, 0]
    for c in range(COLS):
        q = [state[k, cell(c)] for k in range(6)]
        edges = [edge_value(*q[k : k + 4]) for k in range(3)]
        for k in range(3):
            x_edges[k, c] = edges[k]
        weights = [pick(first, XA + i, c) for i in range(3)]
        x_flux[c] = face_flux(weights, edges[1], edges[0], edges[2], q[2], q[3])

    def row(r, carry):
        main = [weight_ref[r, 0], weight_ref[r, 1]]
        ahead = weight_ref[r + 1, 0]

        def weight(field, c):
            return pick(main[field // 8], field, c)

        def z_rows(c, shift=0):
            return pl.ds(16 * c + 8 + shift, 8)

        loaded, edges = {}, {}

        def q_at(c):
            if c not in loaded:
                loaded[c] = state[r + 3, cell(c)]
            return loaded[c]

        def y_edge(c):
            if c not in edges:
                edges[c] = edge_value(q_at(c - 2), q_at(c - 1), q_at(c), q_at(c + 1))
            return edges[c]

        def y_face(c):
            weights = [weight(YA + i, c) if c < COLS else weight(WA + i, 0) for i in range(3)]
            return face_flux(
                weights, y_edge(c), y_edge(c - 1), y_edge(c + 1), q_at(c - 1), q_at(c)
            )

        flux_y = y_face(0)
        for c in range(COLS):
            here = q_at(c)
            z_q[z_rows(c), :] = here
            flux_y_up = y_face(c + 1)
            q1, q2, q3 = [state[r + 3 + k, cell(c)] for k in (1, 2, 3)]
            new_edge = edge_value(here, q1, q2, q3)
            x_edges[r + 3, c] = new_edge
            flux_x_up = face_flux(
                [pick(ahead, XA + i, c) for i in range(3)],
                x_edges[r + 2, c], x_edges[r + 1, c], new_edge, here, q1,
            )
            flux_x = x_flux[c]
            x_flux[c] = flux_x_up
            m2, m1 = z_q[z_rows(c, -2), :], z_q[z_rows(c, -1), :]
            p1, p2 = z_q[z_rows(c, 1), :], z_q[z_rows(c, 2), :]
            edge = edge_value(m2, m1, here, p1)
            z_edge[z_rows(c), :] = edge
            flux_z = face_flux(
                [weight(ZA + i, c) for i in range(3)],
                edge, z_edge[z_rows(c, -1), :], edge_value(m1, here, p1, p2), m1, here,
            )
            z_flux[z_rows(c), :] = flux_z
            total = (flux_x_up - flux_x) + (flux_y_up - flux_y) + (z_flux[z_rows(c, 1), :] - flux_z)
            state[r + 3, cell(c)] = (weight(MASS, c) * here - total) * weight(INV, c)
            flux_y = flux_y_up
        return carry

    lax.fori_loop(0, ROWS, row, 0)


def react(state, sel_ref, net_ref, coeff_ref, rate_ref):
    def block(n, carry):
        rows = [3 + 4 * n + i for i in range(4)]
        inner = pl.ds(24, 128)
        conc = jnp.concatenate([state[r, inner] for r in rows], 0).astype(BF16)
        for k in range(2):
            part = slice(256 * k, 256 * k + 256)
            one = jnp.dot(conc, sel_ref[:, part], preferred_element_type=F32)
            two = jnp.dot(
                conc, sel_ref[:, 512 + 256 * k : 768 + 256 * k], preferred_element_type=F32
            )
            rate_ref[:, part] = (coeff_ref[:, part] * one * two).astype(BF16)
        change = jnp.dot(rate_ref[...], net_ref[...], preferred_element_type=F32)
        change = change.astype(BF16).astype(F32)
        for i, r in enumerate(rows):
            state[r, inner] += change[128 * i : 128 * i + 128]
        return carry

    lax.fori_loop(0, ROWS // 4, block, 0)


def first_kernel(
    place_ref, weather_ref, row_lo, row_hi, col_lo, col_hi, sel_ref, net_ref, coeff_ref, in_ref,
    state, later_ref, row_up, row_down, col_right, col_left, now_ref, rate_ref, *work
):
    del in_ref
    halos = (row_lo, row_hi, col_lo, col_hi)
    for s, ref in enumerate((now_ref, later_ref)):
        write_weights(s, place_ref, weather_ref, *halos, ref)
    read_edges(state, *halos)
    advect(state, now_ref, *work)
    react(state, sel_ref, net_ref, coeff_ref, rate_ref)
    write_edges(state, row_up, row_down, col_right, col_left)


def second_kernel(
    weight_ref, row_lo, row_hi, col_lo, col_hi, sel_ref, net_ref, coeff_ref, in_ref,
    state, out_ref, turn_ref, rate_ref, *work
):
    del in_ref
    read_edges(state, row_lo, row_hi, col_lo, col_hi)
    advect(state, weight_ref, *work)
    react(state, sel_ref, net_ref, coeff_ref, rate_ref)

    def row(r, carry):
        turned = []
        for half in range(2):
            base = 128 * (2 * (r & 1) + half)
            whole = state[r + 3, pl.ds(24, 128), 128 * half : 128 * half + 128]
            turn_ref[pl.ds(pl.multiple_of(base, 128), 128), :] = whole
            parts = [
                turn_ref[pl.ds(base + 64 * (i % 2) + i // 2, 8, stride=8), :] for i in range(16)
            ]
            turned.append(jnp.concatenate(parts, 0).T)
        turned = jnp.concatenate([turned[0], turned[1][0:64]], 0)
        for g in range(24):
            out_ref[g // 3, 16 * (g % 3) + r] = turned[8 * g : 8 * g + 8]
        return carry

    lax.fori_loop(0, ROWS, row, 0, unroll=2)


def blocks(*lead):
    return jax.ShapeDtypeStruct(lead + (8, 128), F32)


def call(kernel, outs, specs, scratch=(), args=(), aliases=None, out_spec=VMEM, grant=40 * 2**20):
    single = not isinstance(outs, (list, tuple))
    return pl.pallas_call(
        kernel,
        out_shape=outs,
        in_specs=specs,
        out_specs=out_spec if single else [VMEM] * len(outs),
        scratch_shapes=list(scratch),
        input_output_aliases=aliases or {},
        compiler_params=pltpu.CompilerParams(vmem_limit_bytes=grant),
    )(*args)


def swap(x):
    return lax.all_to_all(x, "tracer", split_axis=0, concat_axis=0, tiled=True)


def halo(row_up, row_down, col_right, col_left):
    tiles = [(i, i + 1) for i in range(lax.axis_size("tile") - 1)]
    columns = list(zip(ORDER[:-1], ORDER[1:]))

    def back(pairs):
        return [(target, source) for source, target in pairs]

    return (
        lax.ppermute(row_up, "tile", tiles),
        lax.ppermute(row_down, "tile", back(tiles)),
        lax.ppermute(col_right, "tracer", columns),
        lax.ppermute(col_left, "tracer", back(columns)),
    )


def per_device(
    tracers, air_mass, flux_x, flux_y, flux_z, reactants, products, rate_coeff, record_of_step
):
    reactions, species = products.shape
    place = jnp.stack([lax.axis_index("tile"), lax.axis_index("tracer")]).astype(jnp.int32)
    pairs = reactants.T
    ident = lax.broadcasted_iota(jnp.int32, (LANES, reactions), 0)
    hot = [pairs[k : k + 1] == ident for k in range(2)]
    selector = jnp.concatenate(hot, 1).astype(BF16)
    ident = lax.broadcasted_iota(jnp.int32, (reactions, LANES), 1)
    net = jnp.pad(products, ((0, 0), (0, LANES - species)))
    for k in range(2):
        net = net - (reactants[:, k : k + 1] == ident).astype(jnp.int32)
    constants = (selector, net.astype(BF16), rate_coeff[None, :])

    sent = call(
        pack_kernel,
        blocks(8, 56),
        [ANY] * 5,
        [
            pltpu.VMEM((3072, 128), F32),
            pltpu.VMEM((4, 128, 128), F32),
            pltpu.VMEM((8, 56, 8, 128), F32),
            pltpu.SemaphoreType.DMA((7,)),
            pltpu.SemaphoreType.DMA((4,)),
        ],
        [x.reshape(-1, 128) for x in (tracers, air_mass, flux_x, flux_y, flux_z)],
        out_spec=ANY,
        grant=63 * 2**20,
    )

    def edge_blocks(*counts):
        return [jax.ShapeDtypeStruct((count, LANES), BF16) for count in counts]

    state_shape = jax.ShapeDtypeStruct((ROWS + 6, 8 * (COLS + 6), LANES), F32)
    turn = pltpu.VMEM((512, 128), F32)
    state, weather, *edges = call(
        arrange_kernel,
        [state_shape, blocks(STEPS, 8)] + edge_blocks(400, 400, 400, 416),
        [SMEM, VMEM],
        [turn],
        (record_of_step, swap(sent)),
    )
    column = pltpu.VMEM((16 * COLS + 16, LANES), F32)
    work = [
        pltpu.VMEM((512, reactions), BF16),
        pltpu.VMEM((19, COLS, 8, LANES), F32),
        pltpu.VMEM((COLS, 8, LANES), F32),
        column, column, column,
    ]
    weights = (ROWS + 1, 2, 8, 128)
    state, later, *edges = call(
        first_kernel,
        [state_shape, jax.ShapeDtypeStruct(weights, F32)] + edge_blocks(384, 384, 384, 384),
        [SMEM] + [VMEM] * 9,
        [pltpu.VMEM(weights, F32)] + work,
        (place, weather) + halo(*edges) + constants + (state,),
        {9: 0},
    )
    _, sent = call(
        second_kernel,
        [state_shape, blocks(8, 48)],
        [VMEM] * 9,
        [turn] + work,
        (later,) + halo(*edges) + constants + (state,),
        {8: 0},
    )
    out = call(
        unpack_kernel,
        jax.ShapeDtypeStruct((tracers.size // 128, 128), F32),
        [VMEM],
        [pltpu.VMEM((3072, 128), F32), pltpu.SemaphoreType.DMA((3,))],
        (swap(sent),),
        out_spec=ANY,
    )
    return out.reshape(tracers.shape)


def solution(mesh):
    fields = P("tracer", None, "tile", None)
    return jax.shard_map(
        per_device,
        mesh=mesh,
        in_specs=(fields,) * 5 + (P(),) * 4,
        out_specs=fields,
        check_vma=False,
    )
```

```python
import jax
import jax.numpy as jnp
from jax import lax
from jax.experimental import pallas as pl
from jax.experimental.pallas import tpu as pltpu
from jax.sharding import PartitionSpec as P

STEPS = 2
F32 = jnp.float32
BF16 = jnp.bfloat16
ROWS = 16
COLS = 16
STACK = 16
LANES = 256
ORDER = (0, 2, 4, 6, 7, 5, 3, 1)
XA, YA, ZA, MASS, INV, WA = 0, 3, 6, 9, 10, 11
VMEM = pl.BlockSpec(memory_space=pltpu.VMEM)
SMEM = pl.BlockSpec(memory_space=pltpu.SMEM)
ANY = pl.BlockSpec(memory_space=pltpu.HBM)


def roll(x, shift):
    return pltpu.roll(x, shift % 128, axis=1)


def lane_of(shape):
    return lax.broadcasted_iota(jnp.int32, shape, 1)


def exchange_blocks(vectors):
    block = lane_of(vectors[0].shape) >> 4
    out = list(vectors)
    for bit in (1, 2, 4):
        low = (block & bit) == 0
        for i in range(8):
            if i & bit:
                continue
            first, second = out[i], out[i | bit]
            out[i] = jnp.where(low, first, roll(second, 16 * bit))
            out[i | bit] = jnp.where(low, roll(first, -16 * bit), second)
    return out


def pack_kernel(
    q_hbm, mass_hbm, fx_hbm, fy_hbm, fz_hbm, out_hbm, q_ref, field_ref, out_ref, in_sem, out_sem
):
    fields = (mass_hbm, fx_hbm, fy_hbm, fz_hbm)
    loads = [
        pltpu.make_async_copy(hbm, field_ref.at[i], in_sem.at[i]) for i, hbm in enumerate(fields)
    ]
    for tg in range(3):
        part = pl.ds(1024 * tg, 1024)
        loads.append(pltpu.make_async_copy(q_hbm.at[part], q_ref.at[part], in_sem.at[4 + tg]))
    stores = []
    for i, (start, count) in enumerate(((48, 8), (0, 16), (16, 16), (32, 16))):
        part = pl.ds(start, count)
        stores.append(
            pltpu.make_async_copy(out_ref.at[:, part], out_hbm.at[:, part], out_sem.at[i])
        )
    for load in loads:
        load.start()
    for i in range(4):
        loads[i].wait()
    rows = [
        jnp.concatenate(
            [
                field_ref[i, pl.ds(8 * half + r, 8, stride=16), :]
                for i in range(4)
                for half in range(2)
            ],
            0,
        )
        for r in range(8)
    ]
    for place, value in enumerate(exchange_blocks(rows)):
        out_ref[ORDER[place], 48:56] = value.reshape(8, 8, 128)
    stores[0].start()
    for tg in range(3):
        loads[4 + tg].wait()

        def rows(k, carry, tg=tg):
            levels = [
                jnp.concatenate(
                    [
                        q_ref[pl.ds(1024 * tg + lev * 16 + STACK * k + i, 8, stride=128), :]
                        for i in range(STACK)
                    ],
                    0,
                )
                for lev in range(8)
            ]
            for place, value in enumerate(exchange_blocks(levels)):
                part = pl.ds(16 * tg + STACK * k, STACK)
                out_ref[ORDER[place], part] = value.reshape(STACK, 8, 128)
            return carry

        lax.fori_loop(0, ROWS // STACK, rows, 0)
        stores[1 + tg].start()
    for store in stores:
        store.wait()


def unpack_kernel(in_ref, out_hbm, out_ref, out_sem):
    stores = []
    for tg in range(3):
        part = pl.ds(1024 * tg, 1024)
        stores.append(pltpu.make_async_copy(out_ref.at[part], out_hbm.at[part], out_sem.at[tg]))
    for tg in range(3):

        def rows(k, carry, tg=tg):
            part = pl.ds(16 * tg + STACK * k, STACK)
            cols = [in_ref[src, part].reshape(8 * STACK, 128) for src in ORDER]
            for lev, value in enumerate(exchange_blocks(cols)):
                for i in range(STACK):
                    start = 1024 * tg + lev * 16 + STACK * k + i
                    out_ref[pl.ds(start, 8, stride=128), :] = value[8 * i : 8 * i + 8]
            return carry

        lax.fori_loop(0, ROWS // STACK, rows, 0)
        stores[tg].start()
    for store in stores:
        store.wait()


def cell(c):
    return pl.ds(8 * (c + 3), 8)


def write_edges(state_ref, row_up, row_down, col_right, col_left):
    inner = pl.ds(24, 128)
    for k in range(3):
        row_up[128 * k : 128 * k + 128] = state_ref[16 + k, inner].astype(BF16)
        row_down[128 * k : 128 * k + 128] = state_ref[3 + k, inner].astype(BF16)
    for pair in range(ROWS // 2):
        for out, start in ((col_right, 128), (col_left, 24)):
            both = [state_ref[3 + 2 * pair + i, pl.ds(start, 24)] for i in range(2)]
            out[48 * pair : 48 * pair + 48] = jnp.concatenate(both, 0).astype(BF16)


def read_edges(state_ref, row_lo, row_hi, col_lo, col_hi):
    inner = pl.ds(24, 128)
    for k in range(3):
        state_ref[k, inner] = row_lo[128 * k : 128 * k + 128].astype(F32)
        state_ref[19 + k, inner] = row_hi[128 * k : 128 * k + 128].astype(F32)
    for pair in range(ROWS // 2):
        for ref, start in ((col_lo, 0), (col_hi, 152)):
            both = ref[48 * pair : 48 * pair + 48].astype(F32)
            for i in range(2):
                state_ref[3 + 2 * pair + i, pl.ds(start, 24)] = both[24 * i : 24 * i + 24]


def arrange_kernel(
    rec_ref, in_ref, state_ref, weather_ref, row_up, row_down, col_right, col_left, turn_ref
):
    def row(r, carry):
        parts = [in_ref[src, 16 * tg + r] for src in range(8) for tg in range(3)]
        parts.append(jnp.zeros((LANES - 192, 128), F32))
        stacked = jnp.concatenate(parts, 0)
        for half in range(2):
            turned = stacked[128 * half : 128 * half + 128].T
            for i in range(16):
                start = 128 * (2 * (r & 1) + half) + 64 * (i % 2) + i // 2
                turn_ref[pl.ds(start, 8, stride=8), :] = turned[8 * i : 8 * i + 8]
            whole = turn_ref[pl.ds(pl.multiple_of(128 * (2 * (r & 1) + half), 128), 128), :]
            state_ref[r + 3, pl.ds(24, 128), 128 * half : 128 * half + 128] = whole
        return carry

    lax.fori_loop(0, ROWS, row, 0, unroll=2)
    write_edges(state_ref, row_up, row_down, col_right, col_left)

    def lanes(*blocks):
        return jnp.concatenate(blocks, 1)

    ups, downs, rights, lefts = [], [], [], []
    zero = jnp.zeros((8, 128), F32)
    for s in range(STEPS):
        record = rec_ref[s]
        got = [in_ref[record, 48 + k] for k in range(8)]
        for k in range(8):
            weather_ref[s, k] = got[k]
        ups.append(lanes(got[1], zero))
        downs.append(lanes(got[0], got[2]))
        rights.append(lanes(got[0], got[1]))
        lefts += [lanes(got[0], got[1]), lanes(got[4], got[5])]
    row_up[384:400] = jnp.concatenate(ups, 0).astype(BF16)
    row_down[384:400] = jnp.concatenate(downs, 0).astype(BF16)
    col_right[384:400] = jnp.concatenate(rights, 0).astype(BF16)
    col_left[384:416] = jnp.concatenate(lefts, 0).astype(BF16)


def face_weights(flux, mass_low, mass_up):
    upwind = jnp.where(flux > 0, mass_low, mass_up)
    c = jnp.abs(flux) / jnp.maximum(upwind, 0.5)
    side = flux * c
    return [flux * (1.0 - c) * (1.0 - c), side * (c - 1.0), side * (3.0 - 2.0 * c)]


def write_weights(s, place_ref, weather_ref, row_lo, row_hi, col_lo, col_hi, out_ref):
    tile, column = place_ref[0], place_ref[1]
    shape = (8, 128)
    lane = lane_of(shape)
    slot, group = lane & 15, lane >> 4
    level = lax.broadcasted_iota(jnp.int32, shape, 0)
    zero = jnp.zeros(shape, F32)

    def edge(ref, start, s):
        both = ref[384 + start : 400 + start].astype(F32)[8 * s : 8 * s + 8]
        return both[:, 0:128], both[:, 128:256]

    mass = [weather_ref[s, 0], weather_ref[s, 1]]
    east = [weather_ref[s, 2], weather_ref[s, 3]]
    south = [weather_ref[s, 4], weather_ref[s, 5]]
    bottom = [weather_ref[s, 6], weather_ref[s, 7]]
    mass_before, _ = edge(row_lo, 0, s)
    mass_after, east_after = edge(row_hi, 0, s)
    mass_left = edge(col_lo, 0, s)
    lefts = col_hi[384:416].astype(F32)[16 * s : 16 * s + 16]
    mass_right = [lefts[0:8, 128 * h : 128 * h + 128] for h in range(2)]
    south_right = [lefts[8:16, 128 * h : 128 * h + 128] for h in range(2)]
    east[0] = jnp.where((group == 0) & (tile == 0), 0.0, east[0])
    mass_rows = [mass_before] + mass + [mass_after]
    east_rows = east + [east_after]
    for h in range(2):
        here = mass[h]
        south_h = jnp.where((slot == 0) & (column == 0), 0.0, south[h])
        bottom_h = jnp.where(level == 0, 0.0, bottom[h])
        before = jnp.where(group == 0, roll(mass_rows[h], 16), roll(here, 16))
        east_up = jnp.where(group == 7, roll(east_rows[h + 1], -16), roll(east[h], -16))
        left = jnp.where(slot == 0, roll(mass_left[h], -15), roll(here, 1))
        south_up = jnp.where(slot == 15, roll(south_right[h], 15), roll(south_h, -1))
        below = jnp.concatenate([here[0:1], here[0:7]], 0)
        bottom_up = jnp.concatenate([bottom_h[1:8], zero[0:1]], 0)
        new_mass = here - (east_up - east[h]) - (south_up - south_h) - (bottom_up - bottom_h)
        fields = (
            face_weights(east[h], before, here)
            + face_weights(south_h, left, here)
            + face_weights(bottom_h, below, here)
            + [here, 1.0 / new_mass]
            + face_weights(south_right[h], roll(here, -15), mass_right[h])
            + [zero, zero]
        )
        for part in range(2):
            for r, value in enumerate(exchange_blocks(fields[8 * part : 8 * part + 8])):
                out_ref[8 * h + r, part] = value
    last = face_weights(east_after, roll(mass[1], 16), mass_after)
    out_ref[16, 0] = exchange_blocks(last + [zero] * 5)[0]


def edge_value(low2, low1, up1, up2):
    value = (7.0 / 12.0) * (low1 + up1) - (1.0 / 12.0) * (low2 + up2)
    return jnp.minimum(
        jnp.maximum(value, jnp.minimum(low1, up1)), jnp.maximum(low1, up1)
    )


def face_flux(weights, edge, below, above, q_low, q_up):
    a, b, c = weights
    forward = c > 0
    return a * edge + b * jnp.where(forward, below, above) + c * jnp.where(forward, q_low, q_up)


def advect(state, weight_ref, x_edges, x_flux, z_q, z_edge, z_flux):
    def pick(ref_value, field, c):
        lane = 16 * (field % 8) + c
        return jnp.broadcast_to(ref_value[:, lane : lane + 1], (8, LANES))

    for ref in (z_q, z_edge, z_flux):
        ref[...] = jnp.zeros_like(ref)
    first = weight_ref[0, 0]
    for c in range(COLS):
        q = [state[k, cell(c)] for k in range(6)]
        edges = [edge_value(*q[k : k + 4]) for k in range(3)]
        for k in range(3):
            x_edges[k, c] = edges[k]
        weights = [pick(first, XA + i, c) for i in range(3)]
        x_flux[c] = face_flux(weights, edges[1], edges[0], edges[2], q[2], q[3])

    def row(r, carry):
        main = [weight_ref[r, 0], weight_ref[r, 1]]
        ahead = weight_ref[r + 1, 0]

        def weight(field, c):
            return pick(main[field // 8], field, c)

        def z_put(ref, c, value):
            for half in range(2):
                ref[half, pl.ds(16 * c + 8, 8), :] = value[:, 128 * half : 128 * half + 128]

        def z_get(ref, c, shift):
            rows = pl.ds(16 * c + 8 + shift, 8)
            return jnp.concatenate([ref[half, rows, :] for half in range(2)], 1)

        loaded, edges = {}, {}

        def q_at(c):
            if c not in loaded:
                loaded[c] = state[r + 3, cell(c)]
            return loaded[c]

        def y_edge(c):
            if c not in edges:
                edges[c] = edge_value(q_at(c - 2), q_at(c - 1), q_at(c), q_at(c + 1))
            return edges[c]

        def y_face(c):
            weights = [weight(YA + i, c) if c < COLS else weight(WA + i, 0) for i in range(3)]
            return face_flux(
                weights, y_edge(c), y_edge(c - 1), y_edge(c + 1), q_at(c - 1), q_at(c)
            )

        flux_y = y_face(0)
        for c in range(COLS):
            here = q_at(c)
            z_put(z_q, c, here)
            flux_y_up = y_face(c + 1)
            q1, q2, q3 = [state[r + 3 + k, cell(c)] for k in (1, 2, 3)]
            new_edge = edge_value(here, q1, q2, q3)
            x_edges[r + 3, c] = new_edge
            flux_x_up = face_flux(
                [pick(ahead, XA + i, c) for i in range(3)],
                x_edges[r + 2, c], x_edges[r + 1, c], new_edge, here, q1,
            )
            flux_x = x_flux[c]
            x_flux[c] = flux_x_up
            m2, m1, p1, p2 = [z_get(z_q, c, shift) for shift in (-2, -1, 1, 2)]
            edge = edge_value(m2, m1, here, p1)
            z_put(z_edge, c, edge)
            flux_z = face_flux(
                [weight(ZA + i, c) for i in range(3)],
                edge, z_get(z_edge, c, -1), edge_value(m1, here, p1, p2), m1, here,
            )
            z_put(z_flux, c, flux_z)
            flux_z_up = z_get(z_flux, c, 1)
            total = (flux_x_up - flux_x) + (flux_y_up - flux_y) + (flux_z_up - flux_z)
            state[r + 3, cell(c)] = (weight(MASS, c) * here - total) * weight(INV, c)
            flux_y = flux_y_up
        return carry

    lax.fori_loop(0, ROWS, row, 0)


def react(state, sel_ref, net_ref, coeff_ref, rate_ref):
    def block(n, carry):
        rows = [3 + 4 * n + i for i in range(4)]
        inner = pl.ds(24, 128)
        conc = jnp.concatenate([state[r, inner] for r in rows], 0).astype(BF16)
        for k in range(2):
            part = slice(256 * k, 256 * k + 256)
            one = jnp.dot(conc, sel_ref[:, part], preferred_element_type=F32)
            two = jnp.dot(
                conc, sel_ref[:, 512 + 256 * k : 768 + 256 * k], preferred_element_type=F32
            )
            rate_ref[:, part] = (coeff_ref[:, part] * one * two).astype(BF16)
        change = jnp.dot(rate_ref[...], net_ref[...], preferred_element_type=F32)
        change = change.astype(BF16).astype(F32)
        for i, r in enumerate(rows):
            state[r, inner] += change[128 * i : 128 * i + 128]
        return carry

    lax.fori_loop(0, ROWS // 4, block, 0)


def first_kernel(
    place_ref, weather_ref, row_lo, row_hi, col_lo, col_hi, sel_ref, net_ref, coeff_ref, in_ref,
    state, later_ref, row_up, row_down, col_right, col_left, now_ref, rate_ref, *work
):
    del in_ref
    halos = (row_lo, row_hi, col_lo, col_hi)
    for s, ref in enumerate((now_ref, later_ref)):
        write_weights(s, place_ref, weather_ref, *halos, ref)
    read_edges(state, *halos)
    advect(state, now_ref, *work)
    react(state, sel_ref, net_ref, coeff_ref, rate_ref)
    write_edges(state, row_up, row_down, col_right, col_left)


def second_kernel(
    weight_ref, row_lo, row_hi, col_lo, col_hi, sel_ref, net_ref, coeff_ref, in_ref,
    state, out_ref, turn_ref, rate_ref, *work
):
    del in_ref
    read_edges(state, row_lo, row_hi, col_lo, col_hi)
    advect(state, weight_ref, *work)
    react(state, sel_ref, net_ref, coeff_ref, rate_ref)

    def row(r, carry):
        turned = []
        for half in range(2):
            base = 128 * (2 * (r & 1) + half)
            whole = state[r + 3, pl.ds(24, 128), 128 * half : 128 * half + 128]
            turn_ref[pl.ds(pl.multiple_of(base, 128), 128), :] = whole
            parts = [
                turn_ref[pl.ds(base + 64 * (i % 2) + i // 2, 8, stride=8), :] for i in range(16)
            ]
            turned.append(jnp.concatenate(parts, 0).T)
        turned = jnp.concatenate([turned[0], turned[1][0:64]], 0)
        for g in range(24):
            out_ref[g // 3, 16 * (g % 3) + r] = turned[8 * g : 8 * g + 8]
        return carry

    lax.fori_loop(0, ROWS, row, 0, unroll=2)


def blocks(*lead):
    return jax.ShapeDtypeStruct(lead + (8, 128), F32)


def call(kernel, outs, specs, scratch=(), args=(), aliases=None, out_spec=VMEM, grant=40 * 2**20):
    single = not isinstance(outs, (list, tuple))
    return pl.pallas_call(
        kernel,
        out_shape=outs,
        in_specs=specs,
        out_specs=out_spec if single else [VMEM] * len(outs),
        scratch_shapes=list(scratch),
        input_output_aliases=aliases or {},
        compiler_params=pltpu.CompilerParams(vmem_limit_bytes=grant),
    )(*args)


def swap(x):
    return lax.all_to_all(x, "tracer", split_axis=0, concat_axis=0, tiled=True)


def halo(row_up, row_down, col_right, col_left):
    tiles = [(i, i + 1) for i in range(lax.axis_size("tile") - 1)]
    columns = list(zip(ORDER[:-1], ORDER[1:]))

    def back(pairs):
        return [(target, source) for source, target in pairs]

    return (
        lax.ppermute(row_up, "tile", tiles),
        lax.ppermute(row_down, "tile", back(tiles)),
        lax.ppermute(col_right, "tracer", columns),
        lax.ppermute(col_left, "tracer", back(columns)),
    )


def per_device(
    tracers, air_mass, flux_x, flux_y, flux_z, reactants, products, rate_coeff, record_of_step
):
    reactions, species = products.shape
    place = jnp.stack([lax.axis_index("tile"), lax.axis_index("tracer")]).astype(jnp.int32)
    pairs = reactants.T
    ident = lax.broadcasted_iota(jnp.int32, (LANES, reactions), 0)
    hot = [pairs[k : k + 1] == ident for k in range(2)]
    selector = jnp.concatenate(hot, 1).astype(BF16)
    ident = lax.broadcasted_iota(jnp.int32, (reactions, LANES), 1)
    net = jnp.pad(products, ((0, 0), (0, LANES - species)))
    for k in range(2):
        net = net - (reactants[:, k : k + 1] == ident).astype(jnp.int32)
    constants = (selector, net.astype(BF16), rate_coeff[None, :])

    sent = call(
        pack_kernel,
        blocks(8, 56),
        [ANY] * 5,
        [
            pltpu.VMEM((3072, 128), F32),
            pltpu.VMEM((4, 128, 128), F32),
            pltpu.VMEM((8, 56, 8, 128), F32),
            pltpu.SemaphoreType.DMA((7,)),
            pltpu.SemaphoreType.DMA((4,)),
        ],
        [x.reshape(-1, 128) for x in (tracers, air_mass, flux_x, flux_y, flux_z)],
        out_spec=ANY,
        grant=63 * 2**20,
    )

    def edge_blocks(*counts):
        return [jax.ShapeDtypeStruct((count, LANES), BF16) for count in counts]

    state_shape = jax.ShapeDtypeStruct((ROWS + 6, 8 * (COLS + 6), LANES), F32)
    turn = pltpu.VMEM((512, 128), F32)
    state, weather, *edges = call(
        arrange_kernel,
        [state_shape, blocks(STEPS, 8)] + edge_blocks(400, 400, 400, 416),
        [SMEM, VMEM],
        [turn],
        (record_of_step, swap(sent)),
    )
    column = pltpu.VMEM((2, 16 * COLS + 16, 128), F32)
    work = [
        pltpu.VMEM((512, reactions), BF16),
        pltpu.VMEM((19, COLS, 8, LANES), F32),
        pltpu.VMEM((COLS, 8, LANES), F32),
        column, column, column,
    ]
    weights = (ROWS + 1, 2, 8, 128)
    state, later, *edges = call(
        first_kernel,
        [state_shape, jax.ShapeDtypeStruct(weights, F32)] + edge_blocks(384, 384, 384, 384),
        [SMEM] + [VMEM] * 9,
        [pltpu.VMEM(weights, F32)] + work,
        (place, weather) + halo(*edges) + constants + (state,),
        {9: 0},
    )
    _, sent = call(
        second_kernel,
        [state_shape, blocks(8, 48)],
        [VMEM] * 9,
        [turn] + work,
        (later,) + halo(*edges) + constants + (state,),
        {8: 0},
    )
    out = call(
        unpack_kernel,
        jax.ShapeDtypeStruct((tracers.size // 128, 128), F32),
        [VMEM],
        [pltpu.VMEM((3072, 128), F32), pltpu.SemaphoreType.DMA((3,))],
        (swap(sent),),
        out_spec=ANY,
    )
    return out.reshape(tracers.shape)


def solution(mesh):
    fields = P("tracer", None, "tile", None)
    return jax.shard_map(
        per_device,
        mesh=mesh,
        in_specs=(fields,) * 5 + (P(),) * 4,
        out_specs=fields,
        check_vma=False,
    )
```

```python
import functools

import jax
import jax.numpy as jnp
from jax import lax
from jax.experimental import pallas as pl
from jax.experimental.pallas import tpu as pltpu
from jax.sharding import PartitionSpec as P

STEPS = 2
F32 = jnp.float32
BF16 = jnp.bfloat16
ROWS = 16
COLS = 16
STACK = 16
LANES = 256
ORDER = (0, 2, 4, 6, 7, 5, 3, 1)
XA, YA, ZA, MASS, INV, WA = 0, 3, 6, 9, 10, 11
COST = pl.CostEstimate(flops=60_000_000, bytes_accessed=8_000_000, transcendentals=0)
VMEM = pl.BlockSpec(memory_space=pltpu.VMEM)
SMEM = pl.BlockSpec(memory_space=pltpu.SMEM)
ANY = pl.BlockSpec(memory_space=pltpu.HBM)


def roll(x, shift):
    return pltpu.roll(x, shift % 128, axis=1)


def lane_of(shape):
    return lax.broadcasted_iota(jnp.int32, shape, 1)


def exchange_blocks(vectors):
    block = lane_of(vectors[0].shape) >> 4
    out = list(vectors)
    for bit in (1, 2, 4):
        low = (block & bit) == 0
        for i in range(8):
            if i & bit:
                continue
            first, second = out[i], out[i | bit]
            out[i] = jnp.where(low, first, roll(second, 16 * bit))
            out[i | bit] = jnp.where(low, roll(first, -16 * bit), second)
    return out


def pack_kernel(
    q_hbm, mass_hbm, fx_hbm, fy_hbm, fz_hbm, out_hbm, q_ref, field_ref, out_ref, in_sem, out_sem
):
    fields = (mass_hbm, fx_hbm, fy_hbm, fz_hbm)
    loads = [
        pltpu.make_async_copy(hbm, field_ref.at[i], in_sem.at[i]) for i, hbm in enumerate(fields)
    ]
    for tg in range(3):
        part = pl.ds(1024 * tg, 1024)
        loads.append(pltpu.make_async_copy(q_hbm.at[part], q_ref.at[part], in_sem.at[4 + tg]))
    stores = []
    for i, (start, count) in enumerate(((48, 8), (0, 16), (16, 16), (32, 16))):
        part = pl.ds(start, count)
        stores.append(
            pltpu.make_async_copy(out_ref.at[:, part], out_hbm.at[:, part], out_sem.at[i])
        )
    for load in loads:
        load.start()
    for i in range(4):
        loads[i].wait()
    rows = [
        jnp.concatenate(
            [
                field_ref[i, pl.ds(8 * half + r, 8, stride=16), :]
                for i in range(4)
                for half in range(2)
            ],
            0,
        )
        for r in range(8)
    ]
    for place, value in enumerate(exchange_blocks(rows)):
        out_ref[ORDER[place], 48:56] = value.reshape(8, 8, 128)
    stores[0].start()
    for tg in range(3):
        loads[4 + tg].wait()

        def rows(k, carry, tg=tg):
            levels = [
                jnp.concatenate(
                    [
                        q_ref[pl.ds(1024 * tg + lev * 16 + STACK * k + i, 8, stride=128), :]
                        for i in range(STACK)
                    ],
                    0,
                )
                for lev in range(8)
            ]
            for place, value in enumerate(exchange_blocks(levels)):
                part = pl.ds(16 * tg + STACK * k, STACK)
                out_ref[ORDER[place], part] = value.reshape(STACK, 8, 128)
            return carry

        lax.fori_loop(0, ROWS // STACK, rows, 0)
        stores[1 + tg].start()
    for store in stores:
        store.wait()


def unpack_kernel(in_ref, out_hbm, out_ref, out_sem):
    stores = []
    for tg in range(3):
        part = pl.ds(1024 * tg, 1024)
        stores.append(pltpu.make_async_copy(out_ref.at[part], out_hbm.at[part], out_sem.at[tg]))
    for tg in range(3):

        def rows(k, carry, tg=tg):
            part = pl.ds(16 * tg + STACK * k, STACK)
            cols = [in_ref[src, part].reshape(8 * STACK, 128) for src in ORDER]
            for lev, value in enumerate(exchange_blocks(cols)):
                for i in range(STACK):
                    start = 1024 * tg + lev * 16 + STACK * k + i
                    out_ref[pl.ds(start, 8, stride=128), :] = value[8 * i : 8 * i + 8]
            return carry

        lax.fori_loop(0, ROWS // STACK, rows, 0)
        stores[tg].start()
    for store in stores:
        store.wait()


def cell(c):
    return pl.ds(8 * (c + 3), 8)


def write_edges(state_ref, row_up, row_down, col_right, col_left):
    inner = pl.ds(24, 128)
    for k in range(3):
        row_up[128 * k : 128 * k + 128] = state_ref[16 + k, inner].astype(BF16)
        row_down[128 * k : 128 * k + 128] = state_ref[3 + k, inner].astype(BF16)
    for pair in range(ROWS // 2):
        for out, start in ((col_right, 128), (col_left, 24)):
            both = [state_ref[3 + 2 * pair + i, pl.ds(start, 24)] for i in range(2)]
            out[48 * pair : 48 * pair + 48] = jnp.concatenate(both, 0).astype(BF16)


def read_edges(state_ref, row_lo, row_hi, col_lo, col_hi):
    inner = pl.ds(24, 128)
    for k in range(3):
        state_ref[k, inner] = row_lo[128 * k : 128 * k + 128].astype(F32)
        state_ref[19 + k, inner] = row_hi[128 * k : 128 * k + 128].astype(F32)
    for pair in range(ROWS // 2):
        for ref, start in ((col_lo, 0), (col_hi, 152)):
            both = ref[48 * pair : 48 * pair + 48].astype(F32)
            for i in range(2):
                state_ref[3 + 2 * pair + i, pl.ds(start, 24)] = both[24 * i : 24 * i + 24]


def arrange_kernel(
    rec_ref, in_ref, state_ref, weather_ref, row_up, row_down, col_right, col_left, turn_ref
):
    def row(r, carry):
        parts = [in_ref[src, 16 * tg + r] for src in range(8) for tg in range(3)]
        parts.append(jnp.zeros((LANES - 192, 128), F32))
        stacked = jnp.concatenate(parts, 0)
        for half in range(2):
            turned = stacked[128 * half : 128 * half + 128].T
            for i in range(16):
                start = 128 * (2 * (r & 1) + half) + 64 * (i % 2) + i // 2
                turn_ref[pl.ds(start, 8, stride=8), :] = turned[8 * i : 8 * i + 8]
            whole = turn_ref[pl.ds(pl.multiple_of(128 * (2 * (r & 1) + half), 128), 128), :]
            state_ref[r + 3, pl.ds(24, 128), 128 * half : 128 * half + 128] = whole
        return carry

    lax.fori_loop(0, ROWS, row, 0, unroll=2)
    write_edges(state_ref, row_up, row_down, col_right, col_left)

    def lanes(*blocks):
        return jnp.concatenate(blocks, 1)

    ups, downs, rights, lefts = [], [], [], []
    zero = jnp.zeros((8, 128), F32)
    for s in range(STEPS):
        record = rec_ref[s]
        got = [in_ref[record, 48 + k] for k in range(8)]
        for k in range(8):
            weather_ref[s, k] = got[k]
        ups.append(lanes(got[1], zero))
        downs.append(lanes(got[0], got[2]))
        rights.append(lanes(got[0], got[1]))
        lefts += [lanes(got[0], got[1]), lanes(got[4], got[5])]
    row_up[384:400] = jnp.concatenate(ups, 0).astype(BF16)
    row_down[384:400] = jnp.concatenate(downs, 0).astype(BF16)
    col_right[384:400] = jnp.concatenate(rights, 0).astype(BF16)
    col_left[384:416] = jnp.concatenate(lefts, 0).astype(BF16)


def face_weights(flux, mass_low, mass_up):
    upwind = jnp.where(flux > 0, mass_low, mass_up)
    c = jnp.abs(flux) / jnp.maximum(upwind, 0.5)
    side = flux * c
    return [flux * (1.0 - c) * (1.0 - c), side * (c - 1.0), side * (3.0 - 2.0 * c)]


def write_weights(s, place_ref, weather_ref, halos, out_ref):
    tile, column = place_ref[0], place_ref[1]
    shape = (8, 128)
    lane = lane_of(shape)
    slot, group = lane & 15, lane >> 4
    level = lax.broadcasted_iota(jnp.int32, shape, 0)
    zero = jnp.zeros(shape, F32)

    def edge(ref, size):
        both = ref[384 : 384 + 2 * size].astype(F32)[size * s : size * s + size]
        return [
            both[8 * k : 8 * k + 8, 128 * h : 128 * h + 128]
            for k in range(size // 8)
            for h in range(2)
        ]

    mass = [weather_ref[s, 0], weather_ref[s, 1]]
    east = [weather_ref[s, 2], weather_ref[s, 3]]
    south = [weather_ref[s, 4], weather_ref[s, 5]]
    bottom = [weather_ref[s, 6], weather_ref[s, 7]]
    if halos is None:
        mass_before = mass_after = east_after = zero
        mass_left = mass_right = south_right = [zero, zero]
    else:
        row_lo, row_hi, col_lo, col_hi = halos
        mass_before = edge(row_lo, 8)[0]
        mass_after, east_after = edge(row_hi, 8)
        mass_left = edge(col_lo, 8)
        mass_right = edge(col_hi, 16)
        mass_right, south_right = mass_right[0:2], mass_right[2:4]
    east[0] = jnp.where((group == 0) & (tile == 0), 0.0, east[0])
    mass_rows = [mass_before] + mass + [mass_after]
    east_rows = east + [east_after]
    for h in range(2):
        here = mass[h]
        south_h = jnp.where((slot == 0) & (column == 0), 0.0, south[h])
        bottom_h = jnp.where(level == 0, 0.0, bottom[h])
        before = jnp.where(group == 0, roll(mass_rows[h], 16), roll(here, 16))
        east_up = jnp.where(group == 7, roll(east_rows[h + 1], -16), roll(east[h], -16))
        left = jnp.where(slot == 0, roll(mass_left[h], -15), roll(here, 1))
        south_up = jnp.where(slot == 15, roll(south_right[h], 15), roll(south_h, -1))
        below = jnp.concatenate([here[0:1], here[0:7]], 0)
        bottom_up = jnp.concatenate([bottom_h[1:8], zero[0:1]], 0)
        new_mass = here - (east_up - east[h]) - (south_up - south_h) - (bottom_up - bottom_h)
        fields = (
            face_weights(east[h], before, here)
            + face_weights(south_h, left, here)
            + face_weights(bottom_h, below, here)
            + [here, 1.0 / new_mass]
            + face_weights(south_right[h], roll(here, -15), mass_right[h])
            + [zero, zero]
        )
        for part in range(2):
            for r, value in enumerate(exchange_blocks(fields[8 * part : 8 * part + 8])):
                out_ref[8 * h + r, part] = value
    last = face_weights(east_after, roll(mass[1], 16), mass_after)
    out_ref[16, 0] = exchange_blocks(last + [zero] * 5)[0]


def edge_value(low2, low1, up1, up2):
    value = (7.0 / 12.0) * (low1 + up1) - (1.0 / 12.0) * (low2 + up2)
    return jnp.minimum(
        jnp.maximum(value, jnp.minimum(low1, up1)), jnp.maximum(low1, up1)
    )


def face_flux(weights, edge, below, above, q_low, q_up):
    a, b, c = weights
    forward = c > 0
    return a * edge + b * jnp.where(forward, below, above) + c * jnp.where(forward, q_low, q_up)


def pick(vector, field, c):
    lane = 16 * (field % 8) + c
    return jnp.broadcast_to(vector[:, lane : lane + 1], (8, LANES))


def advect_inner(state, weight_ref, partial, x_edges, x_flux, z_q, z_edge, z_flux):
    for ref in (z_q, z_edge, z_flux):
        ref[...] = jnp.zeros_like(ref)

    def row(with_x, r, carry):
        main = [weight_ref[r, 0], weight_ref[r, 1]]
        ahead = weight_ref[r + 1, 0]

        def weights(field, c):
            return [pick(main[(field + i) // 8], field + i, c) for i in range(3)]

        def z_put(ref, c, value):
            for half in range(2):
                ref[half, pl.ds(16 * c + 8, 8), :] = value[:, 128 * half : 128 * half + 128]

        def z_get(ref, c, shift):
            rows = pl.ds(16 * c + 8 + shift, 8)
            return jnp.concatenate([ref[half, rows, :] for half in range(2)], 1)

        loaded, edges = {}, {}

        def q_at(c):
            if c not in loaded:
                loaded[c] = state[r + 3, cell(c)]
            return loaded[c]

        def y_edge(c):
            if c not in edges:
                edges[c] = edge_value(q_at(c - 2), q_at(c - 1), q_at(c), q_at(c + 1))
            return edges[c]

        def y_face(c):
            return face_flux(
                weights(YA, c), y_edge(c), y_edge(c - 1), y_edge(c + 1), q_at(c - 1), q_at(c)
            )

        flux_y = None
        for c in range(COLS):
            here = q_at(c)
            z_put(z_q, c, here)
            m2, m1, p1, p2 = [z_get(z_q, c, shift) for shift in (-2, -1, 1, 2)]
            edge = edge_value(m2, m1, here, p1)
            z_put(z_edge, c, edge)
            flux_z = face_flux(
                weights(ZA, c), edge, z_get(z_edge, c, -1), edge_value(m1, here, p1, p2), m1, here
            )
            z_put(z_flux, c, flux_z)
            total = z_get(z_flux, c, 1) - flux_z
            if 3 <= c <= 12:
                flux_y = y_face(3) if c == 3 else flux_y
                flux_y_up = y_face(c + 1)
                total = total + (flux_y_up - flux_y)
                flux_y = flux_y_up
            if with_x:
                q1, q2, q3 = [state[r + 3 + k, cell(c)] for k in (1, 2, 3)]
                new_edge = edge_value(here, q1, q2, q3)
                x_edges[r + 3, c] = new_edge
                flux_x_up = face_flux(
                    [pick(ahead, XA + i, c) for i in range(3)],
                    x_edges[r + 2, c], x_edges[r + 1, c], new_edge, here, q1,
                )
                total = total + (flux_x_up - x_flux[c])
                x_flux[c] = flux_x_up
            partial[r, c] = pick(main[MASS // 8], MASS, c) * here - total
        return carry

    third = weight_ref[3, 0]
    for c in range(COLS):
        q = [state[3 + k, cell(c)] for k in range(6)]
        edges = [edge_value(*q[k : k + 4]) for k in range(3)]
        for k in range(3):
            x_edges[3 + k, c] = edges[k]
        weights = [pick(third, XA + i, c) for i in range(3)]
        x_flux[c] = face_flux(weights, edges[1], edges[0], edges[2], q[2], q[3])
    lax.fori_loop(3, 13, functools.partial(row, True), 0)
    lax.fori_loop(0, 6, lambda k, carry: row(False, jnp.where(k < 3, k, k + 10), carry), 0)


def four_faces(q, weights):
    edges = [edge_value(*q[k : k + 4]) for k in range(6)]
    flux = [
        face_flux(weights[k], edges[k + 1], edges[k], edges[k + 2], q[k + 2], q[k + 3])
        for k in range(4)
    ]
    return [flux[k + 1] - flux[k] for k in range(3)]


def advect_outer(state, weight_ref, partial):
    def x_side(side, carry):
        base = 13 * side
        vectors = [weight_ref[base + k, 0] for k in range(4)]
        for c in range(COLS):
            q = [state[base + k, cell(c)] for k in range(9)]
            weights = [[pick(vector, XA + i, c) for i in range(3)] for vector in vectors]
            for k, value in enumerate(four_faces(q, weights)):
                partial[base + k, c] -= value
        return carry

    lax.fori_loop(0, 2, x_side, 0)

    def row(r, carry):
        main = [weight_ref[r, 0], weight_ref[r, 1]]

        def weights(c):
            field, place = (YA, c) if c < COLS else (WA, 0)
            return [pick(main[(field + i) // 8], field + i, place) for i in range(3)]

        found = {}
        for base in (0, 13):
            q = [state[r + 3, cell(base - 3 + k)] for k in range(9)]
            for k, value in enumerate(four_faces(q, [weights(base + j) for j in range(4)])):
                found[base + k] = value
        for c in range(COLS):
            value = partial[r, c]
            if c in found:
                value = value - found[c]
            state[r + 3, cell(c)] = value * pick(main[INV // 8], INV, c)
        return carry

    lax.fori_loop(0, ROWS, row, 0)


def react(state, sel_ref, net_ref, coeff_ref, rate_ref):
    def block(n, carry):
        rows = [3 + 4 * n + i for i in range(4)]
        inner = pl.ds(24, 128)
        conc = jnp.concatenate([state[r, inner] for r in rows], 0).astype(BF16)
        for k in range(2):
            part = slice(256 * k, 256 * k + 256)
            one = jnp.dot(conc, sel_ref[:, part], preferred_element_type=F32)
            two = jnp.dot(
                conc, sel_ref[:, 512 + 256 * k : 768 + 256 * k], preferred_element_type=F32
            )
            rate_ref[:, part] = (coeff_ref[:, part] * one * two).astype(BF16)
        change = jnp.dot(rate_ref[...], net_ref[...], preferred_element_type=F32)
        change = change.astype(BF16).astype(F32)
        for i, r in enumerate(rows):
            state[r, inner] += change[128 * i : 128 * i + 128]
        return carry

    lax.fori_loop(0, ROWS // 4, block, 0)


def first_inner_kernel(place_ref, weather_ref, state, partial, weight_ref, *work):
    write_weights(0, place_ref, weather_ref, None, weight_ref)
    advect_inner(state, weight_ref, partial, *work)


def second_inner_kernel(weight_ref, state, partial, *work):
    advect_inner(state, weight_ref, partial, *work)


def first_kernel(
    place_ref, weather_ref, row_lo, row_hi, col_lo, col_hi, sel_ref, net_ref, coeff_ref,
    in_ref, partial_ref,
    state, partial, later_ref, row_up, row_down, col_right, col_left, now_ref, rate_ref,
):
    del in_ref, partial_ref
    halos = (row_lo, row_hi, col_lo, col_hi)
    for s, ref in enumerate((now_ref, later_ref)):
        write_weights(s, place_ref, weather_ref, halos, ref)
    read_edges(state, *halos)
    advect_outer(state, now_ref, partial)
    react(state, sel_ref, net_ref, coeff_ref, rate_ref)
    write_edges(state, row_up, row_down, col_right, col_left)


def second_kernel(
    weight_ref, row_lo, row_hi, col_lo, col_hi, sel_ref, net_ref, coeff_ref, in_ref, partial_ref,
    state, partial, out_ref, turn_ref, rate_ref,
):
    del in_ref, partial_ref
    read_edges(state, row_lo, row_hi, col_lo, col_hi)
    advect_outer(state, weight_ref, partial)
    react(state, sel_ref, net_ref, coeff_ref, rate_ref)

    def row(r, carry):
        turned = []
        for half in range(2):
            base = 128 * (2 * (r & 1) + half)
            whole = state[r + 3, pl.ds(24, 128), 128 * half : 128 * half + 128]
            turn_ref[pl.ds(pl.multiple_of(base, 128), 128), :] = whole
            parts = [
                turn_ref[pl.ds(base + 64 * (i % 2) + i // 2, 8, stride=8), :] for i in range(16)
            ]
            turned.append(jnp.concatenate(parts, 0).T)
        turned = jnp.concatenate([turned[0], turned[1][0:64]], 0)
        for g in range(24):
            out_ref[g // 3, 16 * (g % 3) + r] = turned[8 * g : 8 * g + 8]
        return carry

    lax.fori_loop(0, ROWS, row, 0, unroll=2)


def blocks(*lead):
    return jax.ShapeDtypeStruct(lead + (8, 128), F32)


def call(kernel, outs, specs, scratch=(), args=(), aliases=None, out_spec=VMEM, grant=40 * 2**20, cost=None):
    single = not isinstance(outs, (list, tuple))
    return pl.pallas_call(
        kernel,
        out_shape=outs,
        in_specs=specs,
        out_specs=out_spec if single else [VMEM] * len(outs),
        scratch_shapes=list(scratch),
        input_output_aliases=aliases or {},
        cost_estimate=cost,
        compiler_params=pltpu.CompilerParams(vmem_limit_bytes=grant),
    )(*args)


def swap(x):
    return lax.all_to_all(x, "tracer", split_axis=0, concat_axis=0, tiled=True)


def halo(row_up, row_down, col_right, col_left):
    tiles = [(i, i + 1) for i in range(lax.axis_size("tile") - 1)]
    columns = list(zip(ORDER[:-1], ORDER[1:]))

    def back(pairs):
        return [(target, source) for source, target in pairs]

    return (
        lax.ppermute(row_up, "tile", tiles),
        lax.ppermute(row_down, "tile", back(tiles)),
        lax.ppermute(col_right, "tracer", columns),
        lax.ppermute(col_left, "tracer", back(columns)),
    )


def per_device(
    tracers, air_mass, flux_x, flux_y, flux_z, reactants, products, rate_coeff, record_of_step
):
    reactions, species = products.shape
    place = jnp.stack([lax.axis_index("tile"), lax.axis_index("tracer")]).astype(jnp.int32)
    pairs = reactants.T
    ident = lax.broadcasted_iota(jnp.int32, (LANES, reactions), 0)
    hot = [pairs[k : k + 1] == ident for k in range(2)]
    selector = jnp.concatenate(hot, 1).astype(BF16)
    ident = lax.broadcasted_iota(jnp.int32, (reactions, LANES), 1)
    net = jnp.pad(products, ((0, 0), (0, LANES - species)))
    for k in range(2):
        net = net - (reactants[:, k : k + 1] == ident).astype(jnp.int32)
    constants = (selector, net.astype(BF16), rate_coeff[None, :])

    sent = call(
        pack_kernel,
        blocks(8, 56),
        [ANY] * 5,
        [
            pltpu.VMEM((3072, 128), F32),
            pltpu.VMEM((4, 128, 128), F32),
            pltpu.VMEM((8, 56, 8, 128), F32),
            pltpu.SemaphoreType.DMA((7,)),
            pltpu.SemaphoreType.DMA((4,)),
        ],
        [x.reshape(-1, 128) for x in (tracers, air_mass, flux_x, flux_y, flux_z)],
        out_spec=ANY,
        grant=63 * 2**20,
    )

    def edge_blocks(*counts):
        return [jax.ShapeDtypeStruct((count, LANES), BF16) for count in counts]

    state_shape = jax.ShapeDtypeStruct((ROWS + 6, 8 * (COLS + 6), LANES), F32)
    turn = pltpu.VMEM((512, 128), F32)
    state, weather, *edges = call(
        arrange_kernel,
        [state_shape, blocks(STEPS, 8)] + edge_blocks(400, 400, 400, 416),
        [SMEM, VMEM],
        [turn],
        (record_of_step, swap(sent)),
    )
    column = pltpu.VMEM((2, 16 * COLS + 16, 128), F32)
    work = [
        pltpu.VMEM((19, COLS, 8, LANES), F32),
        pltpu.VMEM((COLS, 8, LANES), F32),
        column, column, column,
    ]
    rates = pltpu.VMEM((512, reactions), BF16)
    weights = (ROWS + 1, 2, 8, 128)
    partial_shape = jax.ShapeDtypeStruct((ROWS, COLS, 8, LANES), F32)
    halos = halo(*edges)
    partial = call(
        first_inner_kernel, partial_shape, [SMEM] + [VMEM] * 2,
        [pltpu.VMEM(weights, F32)] + work, (place, weather, state), cost=COST,
    )
    state, _, later, *edges = call(
        first_kernel,
        [state_shape, partial_shape, jax.ShapeDtypeStruct(weights, F32)]
        + edge_blocks(384, 384, 384, 384),
        [SMEM] + [VMEM] * 10,
        [pltpu.VMEM(weights, F32), rates],
        (place, weather) + halos + constants + (state, partial),
        {9: 0, 10: 1},
    )
    halos = halo(*edges)
    partial = call(
        second_inner_kernel, partial_shape, [VMEM] * 2, work, (later, state), cost=COST
    )
    _, _, sent = call(
        second_kernel,
        [state_shape, partial_shape, blocks(8, 48)],
        [VMEM] * 10,
        [turn, rates],
        (later,) + halos + constants + (state, partial),
        {8: 0, 9: 1},
    )
    out = call(
        unpack_kernel,
        jax.ShapeDtypeStruct((tracers.size // 128, 128), F32),
        [VMEM],
        [pltpu.VMEM((3072, 128), F32), pltpu.SemaphoreType.DMA((3,))],
        (swap(sent),),
        out_spec=ANY,
    )
    return out.reshape(tracers.shape)


def solution(mesh):
    fields = P("tracer", None, "tile", None)
    return jax.shard_map(
        per_device,
        mesh=mesh,
        in_specs=(fields,) * 5 + (P(),) * 4,
        out_specs=fields,
        check_vma=False,
    )
```

```python
import functools

import jax
import jax.numpy as jnp
from jax import lax
from jax.experimental import pallas as pl
from jax.experimental.pallas import tpu as pltpu
from jax.sharding import PartitionSpec as P

STEPS = 2
F32 = jnp.float32
BF16 = jnp.bfloat16
ROWS = 16
COLS = 16
STACK = 16
LANES = 256
ORDER = (0, 2, 4, 6, 7, 5, 3, 1)
XA, YA, ZA, MASS, INV, WA = 0, 3, 6, 9, 10, 11
COST = pl.CostEstimate(flops=60_000_000, bytes_accessed=8_000_000, transcendentals=0)
VMEM = pl.BlockSpec(memory_space=pltpu.VMEM)
SMEM = pl.BlockSpec(memory_space=pltpu.SMEM)
ANY = pl.BlockSpec(memory_space=pltpu.HBM)


def roll(x, shift):
    return pltpu.roll(x, shift % 128, axis=1)


def lane_of(shape):
    return lax.broadcasted_iota(jnp.int32, shape, 1)


def exchange_blocks(vectors):
    block = lane_of(vectors[0].shape) >> 4
    out = list(vectors)
    for bit in (1, 2, 4):
        low = (block & bit) == 0
        for i in range(8):
            if i & bit:
                continue
            first, second = out[i], out[i | bit]
            out[i] = jnp.where(low, first, roll(second, 16 * bit))
            out[i | bit] = jnp.where(low, roll(first, -16 * bit), second)
    return out


def pack_kernel(
    q_hbm, mass_hbm, fx_hbm, fy_hbm, fz_hbm, out_hbm, q_ref, field_ref, out_ref, in_sem, out_sem
):
    fields = (mass_hbm, fx_hbm, fy_hbm, fz_hbm)
    loads = [
        pltpu.make_async_copy(hbm, field_ref.at[i], in_sem.at[i]) for i, hbm in enumerate(fields)
    ]
    for tg in range(3):
        part = pl.ds(1024 * tg, 1024)
        loads.append(pltpu.make_async_copy(q_hbm.at[part], q_ref.at[part], in_sem.at[4 + tg]))
    stores = []
    for i, (start, count) in enumerate(((48, 8), (0, 16), (16, 16), (32, 16))):
        part = pl.ds(start, count)
        stores.append(
            pltpu.make_async_copy(out_ref.at[:, part], out_hbm.at[:, part], out_sem.at[i])
        )
    for load in loads:
        load.start()
    for i in range(4):
        loads[i].wait()
    rows = [
        jnp.concatenate(
            [
                field_ref[i, pl.ds(8 * half + r, 8, stride=16), :]
                for i in range(4)
                for half in range(2)
            ],
            0,
        )
        for r in range(8)
    ]
    for place, value in enumerate(exchange_blocks(rows)):
        out_ref[ORDER[place], 48:56] = value.reshape(8, 8, 128)
    stores[0].start()
    for tg in range(3):
        loads[4 + tg].wait()

        def rows(k, carry, tg=tg):
            levels = [
                jnp.concatenate(
                    [
                        q_ref[pl.ds(1024 * tg + lev * 16 + STACK * k + i, 8, stride=128), :]
                        for i in range(STACK)
                    ],
                    0,
                )
                for lev in range(8)
            ]
            for place, value in enumerate(exchange_blocks(levels)):
                part = pl.ds(16 * tg + STACK * k, STACK)
                out_ref[ORDER[place], part] = value.reshape(STACK, 8, 128)
            return carry

        lax.fori_loop(0, ROWS // STACK, rows, 0)
        stores[1 + tg].start()
    for store in stores:
        store.wait()


def unpack_kernel(in_ref, out_hbm, out_ref, out_sem):
    stores = []
    for tg in range(3):
        part = pl.ds(1024 * tg, 1024)
        stores.append(pltpu.make_async_copy(out_ref.at[part], out_hbm.at[part], out_sem.at[tg]))
    for tg in range(3):

        def rows(k, carry, tg=tg):
            part = pl.ds(16 * tg + STACK * k, STACK)
            cols = [in_ref[src, part].reshape(8 * STACK, 128) for src in ORDER]
            for lev, value in enumerate(exchange_blocks(cols)):
                for i in range(STACK):
                    start = 1024 * tg + lev * 16 + STACK * k + i
                    out_ref[pl.ds(start, 8, stride=128), :] = value[8 * i : 8 * i + 8]
            return carry

        lax.fori_loop(0, ROWS // STACK, rows, 0)
        stores[tg].start()
    for store in stores:
        store.wait()


def cell(c):
    return pl.ds(8 * (c + 3), 8)


def write_edges(state_ref, row_up, row_down, col_right, col_left):
    inner = pl.ds(24, 128)
    for k in range(3):
        row_up[128 * k : 128 * k + 128] = state_ref[16 + k, inner].astype(BF16)
        row_down[128 * k : 128 * k + 128] = state_ref[3 + k, inner].astype(BF16)
    for pair in range(ROWS // 2):
        for out, start in ((col_right, 128), (col_left, 24)):
            both = [state_ref[3 + 2 * pair + i, pl.ds(start, 24)] for i in range(2)]
            out[48 * pair : 48 * pair + 48] = jnp.concatenate(both, 0).astype(BF16)


def read_edges(state_ref, row_lo, row_hi, col_lo, col_hi):
    inner = pl.ds(24, 128)
    for k in range(3):
        state_ref[k, inner] = row_lo[128 * k : 128 * k + 128].astype(F32)
        state_ref[19 + k, inner] = row_hi[128 * k : 128 * k + 128].astype(F32)
    for pair in range(ROWS // 2):
        for ref, start in ((col_lo, 0), (col_hi, 152)):
            both = ref[48 * pair : 48 * pair + 48].astype(F32)
            for i in range(2):
                state_ref[3 + 2 * pair + i, pl.ds(start, 24)] = both[24 * i : 24 * i + 24]


def arrange_kernel(
    rec_ref, place_ref, in_ref,
    state_ref, weather_ref, weight_ref, row_up, row_down, col_right, col_left, turn_ref,
):
    def row(r, carry):
        parts = [in_ref[src, 16 * tg + r] for src in range(8) for tg in range(3)]
        parts.append(jnp.zeros((LANES - 192, 128), F32))
        stacked = jnp.concatenate(parts, 0)
        for half in range(2):
            turned = stacked[128 * half : 128 * half + 128].T
            for i in range(16):
                start = 128 * (2 * (r & 1) + half) + 64 * (i % 2) + i // 2
                turn_ref[pl.ds(start, 8, stride=8), :] = turned[8 * i : 8 * i + 8]
            whole = turn_ref[pl.ds(pl.multiple_of(128 * (2 * (r & 1) + half), 128), 128), :]
            state_ref[r + 3, pl.ds(24, 128), 128 * half : 128 * half + 128] = whole
        return carry

    lax.fori_loop(0, ROWS, row, 0, unroll=8)
    write_edges(state_ref, row_up, row_down, col_right, col_left)

    def lanes(*blocks):
        return jnp.concatenate(blocks, 1)

    ups, downs, rights, lefts = [], [], [], []
    zero = jnp.zeros((8, 128), F32)
    for s in range(STEPS):
        record = rec_ref[s]
        got = [in_ref[record, 48 + k] for k in range(8)]
        for k in range(8):
            weather_ref[s, k] = got[k]
        ups.append(lanes(got[1], zero))
        downs.append(lanes(got[0], got[2]))
        rights.append(lanes(got[0], got[1]))
        lefts += [lanes(got[0], got[1]), lanes(got[4], got[5])]
    row_up[384:400] = jnp.concatenate(ups, 0).astype(BF16)
    row_down[384:400] = jnp.concatenate(downs, 0).astype(BF16)
    col_right[384:400] = jnp.concatenate(rights, 0).astype(BF16)
    col_left[384:416] = jnp.concatenate(lefts, 0).astype(BF16)
    write_weights(0, place_ref, weather_ref, None, weight_ref)


def face_weights(flux, mass_low, mass_up):
    upwind = jnp.where(flux > 0, mass_low, mass_up)
    c = jnp.abs(flux) / jnp.maximum(upwind, 0.5)
    side = flux * c
    return [flux * (1.0 - c) * (1.0 - c), side * (c - 1.0), side * (3.0 - 2.0 * c)]


def write_weights(s, place_ref, weather_ref, halos, out_ref):
    tile, column = place_ref[0], place_ref[1]
    shape = (8, 128)
    lane = lane_of(shape)
    slot, group = lane & 15, lane >> 4
    level = lax.broadcasted_iota(jnp.int32, shape, 0)
    zero = jnp.zeros(shape, F32)

    def edge(ref, size):
        both = ref[384 : 384 + 2 * size].astype(F32)[size * s : size * s + size]
        return [
            both[8 * k : 8 * k + 8, 128 * h : 128 * h + 128]
            for k in range(size // 8)
            for h in range(2)
        ]

    mass = [weather_ref[s, 0], weather_ref[s, 1]]
    east = [weather_ref[s, 2], weather_ref[s, 3]]
    south = [weather_ref[s, 4], weather_ref[s, 5]]
    bottom = [weather_ref[s, 6], weather_ref[s, 7]]
    if halos is None:
        mass_before = mass_after = east_after = zero
        mass_left = mass_right = south_right = [zero, zero]
    else:
        row_lo, row_hi, col_lo, col_hi = halos
        mass_before = edge(row_lo, 8)[0]
        mass_after, east_after = edge(row_hi, 8)
        mass_left = edge(col_lo, 8)
        mass_right = edge(col_hi, 16)
        mass_right, south_right = mass_right[0:2], mass_right[2:4]
    east[0] = jnp.where((group == 0) & (tile == 0), 0.0, east[0])
    mass_rows = [mass_before] + mass + [mass_after]
    east_rows = east + [east_after]
    for h in range(2):
        here = mass[h]
        south_h = jnp.where((slot == 0) & (column == 0), 0.0, south[h])
        bottom_h = jnp.where(level == 0, 0.0, bottom[h])
        before = jnp.where(group == 0, roll(mass_rows[h], 16), roll(here, 16))
        east_up = jnp.where(group == 7, roll(east_rows[h + 1], -16), roll(east[h], -16))
        left = jnp.where(slot == 0, roll(mass_left[h], -15), roll(here, 1))
        south_up = jnp.where(slot == 15, roll(south_right[h], 15), roll(south_h, -1))
        below = jnp.concatenate([here[0:1], here[0:7]], 0)
        bottom_up = jnp.concatenate([bottom_h[1:8], zero[0:1]], 0)
        new_mass = here - (east_up - east[h]) - (south_up - south_h) - (bottom_up - bottom_h)
        fields = (
            face_weights(east[h], before, here)
            + face_weights(south_h, left, here)
            + face_weights(bottom_h, below, here)
            + [here, 1.0 / new_mass]
            + face_weights(south_right[h], roll(here, -15), mass_right[h])
            + [zero, zero]
        )
        for part in range(2):
            for r, value in enumerate(exchange_blocks(fields[8 * part : 8 * part + 8])):
                out_ref[8 * h + r, part] = value
    last = face_weights(east_after, roll(mass[1], 16), mass_after)
    out_ref[16, 0] = exchange_blocks(last + [zero] * 5)[0]


def edge_value(low2, low1, up1, up2):
    value = (7.0 / 12.0) * (low1 + up1) - (1.0 / 12.0) * (low2 + up2)
    return jnp.minimum(
        jnp.maximum(value, jnp.minimum(low1, up1)), jnp.maximum(low1, up1)
    )


def face_flux(weights, edge, below, above, q_low, q_up):
    a, b, c = weights
    forward = c > 0
    return a * edge + b * jnp.where(forward, below, above) + c * jnp.where(forward, q_low, q_up)


def pick(vector, field, c):
    lane = 16 * (field % 8) + c
    return jnp.broadcast_to(vector[:, lane : lane + 1], (8, LANES))


def advect_inner(state, weight_ref, partial, x_edges, x_flux, z_q, z_edge, z_flux):
    for ref in (z_q, z_edge, z_flux):
        ref[...] = jnp.zeros_like(ref)

    def row(with_x, r, carry):
        main = [weight_ref[r, 0], weight_ref[r, 1]]
        ahead = weight_ref[r + 1, 0]

        def weights(field, c):
            return [pick(main[(field + i) // 8], field + i, c) for i in range(3)]

        def z_put(ref, c, value, shift=0):
            for half in range(2):
                ref[half, pl.ds(16 * c + 8 + shift, 8), :] = value[:, 128 * half : 128 * half + 128]

        def z_get(ref, c, shift):
            rows = pl.ds(16 * c + 8 + shift, 8)
            return jnp.concatenate([ref[half, rows, :] for half in range(2)], 1)

        loaded, edges = {}, {}

        def q_at(c):
            if c not in loaded:
                loaded[c] = state[r + 3, cell(c)]
            return loaded[c]

        def y_edge(c):
            if c not in edges:
                edges[c] = edge_value(q_at(c - 2), q_at(c - 1), q_at(c), q_at(c + 1))
            return edges[c]

        def y_face(c):
            return face_flux(
                weights(YA, c), y_edge(c), y_edge(c - 1), y_edge(c + 1), q_at(c - 1), q_at(c)
            )

        for c in range(COLS):
            z_put(z_q, c, q_at(c))
        for half in range(2):
            low = [z_q[half, pl.ds(8 + k, COLS, stride=16), :] for k in range(2)]
            none = jnp.zeros_like(low[0])
            z_edge[half, pl.ds(8, COLS, stride=16), :] = edge_value(none, none, *low)
        flux_y = None
        for c in range(COLS):
            here = q_at(c)
            m1, p1, p2 = [z_get(z_q, c, shift) for shift in (-1, 1, 2)]
            edge_up = edge_value(m1, here, p1, p2)
            z_put(z_edge, c, edge_up, 1)
            flux_z = face_flux(
                weights(ZA, c), z_get(z_edge, c, 0), z_get(z_edge, c, -1), edge_up, m1, here
            )
            z_put(z_flux, c, flux_z)
            total = z_get(z_flux, c, 1) - flux_z
            if 3 <= c <= 12:
                flux_y = y_face(3) if c == 3 else flux_y
                flux_y_up = y_face(c + 1)
                total = total + (flux_y_up - flux_y)
                flux_y = flux_y_up
            if with_x:
                q1, q2, q3 = [state[r + 3 + k, cell(c)] for k in (1, 2, 3)]
                new_edge = edge_value(here, q1, q2, q3)
                x_edges[r + 3, c] = new_edge
                flux_x_up = face_flux(
                    [pick(ahead, XA + i, c) for i in range(3)],
                    x_edges[r + 2, c], x_edges[r + 1, c], new_edge, here, q1,
                )
                total = total + (flux_x_up - x_flux[c])
                x_flux[c] = flux_x_up
            partial[r, c] = pick(main[MASS // 8], MASS, c) * here - total
        return carry

    third = weight_ref[3, 0]
    for c in range(COLS):
        q = [state[3 + k, cell(c)] for k in range(6)]
        edges = [edge_value(*q[k : k + 4]) for k in range(3)]
        for k in range(3):
            x_edges[3 + k, c] = edges[k]
        weights = [pick(third, XA + i, c) for i in range(3)]
        x_flux[c] = face_flux(weights, edges[1], edges[0], edges[2], q[2], q[3])
    lax.fori_loop(3, 13, functools.partial(row, True), 0)
    lax.fori_loop(0, 6, lambda k, carry: row(False, jnp.where(k < 3, k, k + 10), carry), 0)


def four_faces(q, weights):
    edges = [edge_value(*q[k : k + 4]) for k in range(6)]
    flux = [
        face_flux(weights[k], edges[k + 1], edges[k], edges[k + 2], q[k + 2], q[k + 3])
        for k in range(4)
    ]
    return [flux[k + 1] - flux[k] for k in range(3)]


def advect_outer(state, weight_ref, partial):
    def x_side(side, carry):
        base = 13 * side
        vectors = [weight_ref[base + k, 0] for k in range(4)]
        for c in range(COLS):
            q = [state[base + k, cell(c)] for k in range(9)]
            weights = [[pick(vector, XA + i, c) for i in range(3)] for vector in vectors]
            for k, value in enumerate(four_faces(q, weights)):
                partial[base + k, c] -= value
        return carry

    lax.fori_loop(0, 2, x_side, 0)

    def row(r, carry):
        main = [weight_ref[r, 0], weight_ref[r, 1]]

        def weights(c):
            field, place = (YA, c) if c < COLS else (WA, 0)
            return [pick(main[(field + i) // 8], field + i, place) for i in range(3)]

        found = {}
        for base in (0, 13):
            q = [state[r + 3, cell(base - 3 + k)] for k in range(9)]
            for k, value in enumerate(four_faces(q, [weights(base + j) for j in range(4)])):
                found[base + k] = value
        for c in range(COLS):
            value = partial[r, c]
            if c in found:
                value = value - found[c]
            state[r + 3, cell(c)] = value * pick(main[INV // 8], INV, c)
        return carry

    lax.fori_loop(0, ROWS, row, 0)


def react(state, sel_ref, net_ref, coeff_ref, rate_ref):
    def block(n, carry):
        rows = [3 + 16 * n + i for i in range(16)]
        inner = pl.ds(24, 128)
        conc = jnp.concatenate([state[r, inner] for r in rows], 0).astype(BF16)
        for k in range(2):
            part = slice(256 * k, 256 * k + 256)
            one = jnp.dot(conc, sel_ref[:, part], preferred_element_type=F32)
            two = jnp.dot(
                conc, sel_ref[:, 512 + 256 * k : 768 + 256 * k], preferred_element_type=F32
            )
            rate_ref[:, part] = (coeff_ref[:, part] * one * two).astype(BF16)
        change = jnp.dot(rate_ref[...], net_ref[...], preferred_element_type=F32)
        change = change.astype(BF16).astype(F32)
        for i, r in enumerate(rows):
            state[r, inner] += change[128 * i : 128 * i + 128]
        return carry

    lax.fori_loop(0, ROWS // 16, block, 0)


def inner_kernel(weight_ref, state, partial, *work):
    advect_inner(state, weight_ref, partial, *work)


def first_kernel(
    place_ref, weather_ref, row_lo, row_hi, col_lo, col_hi, sel_ref, net_ref, coeff_ref,
    in_ref, partial_ref,
    state, partial, later_ref, row_up, row_down, col_right, col_left, now_ref, rate_ref,
):
    del in_ref, partial_ref
    halos = (row_lo, row_hi, col_lo, col_hi)
    for s, ref in enumerate((now_ref, later_ref)):
        write_weights(s, place_ref, weather_ref, halos, ref)
    read_edges(state, *halos)
    advect_outer(state, now_ref, partial)
    react(state, sel_ref, net_ref, coeff_ref, rate_ref)
    write_edges(state, row_up, row_down, col_right, col_left)


def second_kernel(
    weight_ref, row_lo, row_hi, col_lo, col_hi, sel_ref, net_ref, coeff_ref, in_ref, partial_ref,
    state, partial, out_ref, turn_ref, rate_ref,
):
    del in_ref, partial_ref
    read_edges(state, row_lo, row_hi, col_lo, col_hi)
    advect_outer(state, weight_ref, partial)
    react(state, sel_ref, net_ref, coeff_ref, rate_ref)

    def row(r, carry):
        turned = []
        for half in range(2):
            base = 128 * (2 * (r & 1) + half)
            whole = state[r + 3, pl.ds(24, 128), 128 * half : 128 * half + 128]
            turn_ref[pl.ds(pl.multiple_of(base, 128), 128), :] = whole
            parts = [
                turn_ref[pl.ds(base + 64 * (i % 2) + i // 2, 8, stride=8), :] for i in range(16)
            ]
            turned.append(jnp.concatenate(parts, 0).T)
        turned = jnp.concatenate([turned[0], turned[1][0:64]], 0)
        for g in range(24):
            out_ref[g // 3, 16 * (g % 3) + r] = turned[8 * g : 8 * g + 8]
        return carry

    lax.fori_loop(0, ROWS, row, 0, unroll=8)


def blocks(*lead):
    return jax.ShapeDtypeStruct(lead + (8, 128), F32)


def call(kernel, outs, specs, scratch=(), args=(), aliases=None, out_spec=VMEM, grant=40 * 2**20, cost=None):
    single = not isinstance(outs, (list, tuple))
    return pl.pallas_call(
        kernel,
        out_shape=outs,
        in_specs=specs,
        out_specs=out_spec if single else [VMEM] * len(outs),
        scratch_shapes=list(scratch),
        input_output_aliases=aliases or {},
        cost_estimate=cost,
        compiler_params=pltpu.CompilerParams(vmem_limit_bytes=grant),
    )(*args)


def swap(x):
    return lax.all_to_all(x, "tracer", split_axis=0, concat_axis=0, tiled=True)


def halo(row_up, row_down, col_right, col_left):
    tiles = [(i, i + 1) for i in range(lax.axis_size("tile") - 1)]
    columns = list(zip(ORDER[:-1], ORDER[1:]))

    def back(pairs):
        return [(target, source) for source, target in pairs]

    return (
        lax.ppermute(row_up, "tile", tiles),
        lax.ppermute(row_down, "tile", back(tiles)),
        lax.ppermute(col_right, "tracer", columns),
        lax.ppermute(col_left, "tracer", back(columns)),
    )


def per_device(
    tracers, air_mass, flux_x, flux_y, flux_z, reactants, products, rate_coeff, record_of_step
):
    reactions, species = products.shape
    place = jnp.stack([lax.axis_index("tile"), lax.axis_index("tracer")]).astype(jnp.int32)
    pairs = reactants.T
    ident = lax.broadcasted_iota(jnp.int32, (LANES, reactions), 0)
    hot = [pairs[k : k + 1] == ident for k in range(2)]
    selector = jnp.concatenate(hot, 1).astype(BF16)
    ident = lax.broadcasted_iota(jnp.int32, (reactions, LANES), 1)
    net = jnp.pad(products, ((0, 0), (0, LANES - species)))
    for k in range(2):
        net = net - (reactants[:, k : k + 1] == ident).astype(jnp.int32)
    constants = (selector, net.astype(BF16), rate_coeff[None, :])

    sent = call(
        pack_kernel,
        blocks(8, 56),
        [ANY] * 5,
        [
            pltpu.VMEM((3072, 128), F32),
            pltpu.VMEM((4, 128, 128), F32),
            pltpu.VMEM((8, 56, 8, 128), F32),
            pltpu.SemaphoreType.DMA((7,)),
            pltpu.SemaphoreType.DMA((4,)),
        ],
        [x.reshape(-1, 128) for x in (tracers, air_mass, flux_x, flux_y, flux_z)],
        out_spec=ANY,
        grant=63 * 2**20,
    )

    def edge_blocks(*counts):
        return [jax.ShapeDtypeStruct((count, LANES), BF16) for count in counts]

    state_shape = jax.ShapeDtypeStruct((ROWS + 6, 8 * (COLS + 6), LANES), F32)
    turn = pltpu.VMEM((512, 128), F32)
    weights = (ROWS + 1, 2, 8, 128)
    weights_shape = jax.ShapeDtypeStruct(weights, F32)
    state, weather, early, *edges = call(
        arrange_kernel,
        [state_shape, blocks(STEPS, 8), weights_shape] + edge_blocks(400, 400, 400, 416),
        [SMEM, SMEM, VMEM],
        [turn],
        (record_of_step, place, swap(sent)),
    )
    column = pltpu.VMEM((2, 16 * COLS + 16, 128), F32)
    work = [
        pltpu.VMEM((19, COLS, 8, LANES), F32),
        pltpu.VMEM((COLS, 8, LANES), F32),
        column, column, column,
    ]
    rates = pltpu.VMEM((2048, reactions), BF16)
    partial_shape = jax.ShapeDtypeStruct((ROWS, COLS, 8, LANES), F32)
    halos = halo(*edges)
    partial = call(
        inner_kernel, partial_shape, [VMEM] * 2, work, (early, state), cost=COST
    )
    state, _, later, *edges = call(
        first_kernel,
        [state_shape, partial_shape, weights_shape]
        + edge_blocks(384, 384, 384, 384),
        [SMEM] + [VMEM] * 10,
        [pltpu.VMEM(weights, F32), rates],
        (place, weather) + halos + constants + (state, partial),
        {9: 0, 10: 1},
    )
    halos = halo(*edges)
    partial = call(
        inner_kernel, partial_shape, [VMEM] * 2, work, (later, state), cost=COST
    )
    _, _, sent = call(
        second_kernel,
        [state_shape, partial_shape, blocks(8, 48)],
        [VMEM] * 10,
        [turn, rates],
        (later,) + halos + constants + (state, partial),
        {8: 0, 9: 1},
    )
    out = call(
        unpack_kernel,
        jax.ShapeDtypeStruct((tracers.size // 128, 128), F32),
        [VMEM],
        [pltpu.VMEM((3072, 128), F32), pltpu.SemaphoreType.DMA((3,))],
        (swap(sent),),
        out_spec=ANY,
    )
    return out.reshape(tracers.shape)


def solution(mesh):
    fields = P("tracer", None, "tile", None)
    return jax.shard_map(
        per_device,
        mesh=mesh,
        in_specs=(fields,) * 5 + (P(),) * 4,
        out_specs=fields,
        check_vma=False,
    )
```

```python
import functools

import jax
import jax.numpy as jnp
from jax import lax
from jax.experimental import pallas as pl
from jax.experimental.pallas import tpu as pltpu
from jax.sharding import PartitionSpec as P

STEPS = 2
F32 = jnp.float32
BF16 = jnp.bfloat16
ROWS = 16
COLS = 16
STACK = 16
LANES = 256
ORDER = (0, 2, 4, 6, 7, 5, 3, 1)
XA, YA, ZA, MASS, INV, WA = 0, 3, 6, 9, 10, 11
COST = pl.CostEstimate(flops=60_000_000, bytes_accessed=8_000_000, transcendentals=0)
VMEM = pl.BlockSpec(memory_space=pltpu.VMEM)
SMEM = pl.BlockSpec(memory_space=pltpu.SMEM)
ANY = pl.BlockSpec(memory_space=pltpu.HBM)


def roll(x, shift):
    return pltpu.roll(x, shift % 128, axis=1)


def lane_of(shape):
    return lax.broadcasted_iota(jnp.int32, shape, 1)


def exchange_blocks(vectors):
    block = lane_of(vectors[0].shape) >> 4
    out = list(vectors)
    for bit in (1, 2, 4):
        low = (block & bit) == 0
        for i in range(8):
            if i & bit:
                continue
            first, second = out[i], out[i | bit]
            out[i] = jnp.where(low, first, roll(second, 16 * bit))
            out[i | bit] = jnp.where(low, roll(first, -16 * bit), second)
    return out


def pack_kernel(
    q_hbm, mass_hbm, fx_hbm, fy_hbm, fz_hbm, out_hbm, q_ref, field_ref, out_ref, in_sem, out_sem
):
    fields = (mass_hbm, fx_hbm, fy_hbm, fz_hbm)
    loads = [
        pltpu.make_async_copy(hbm, field_ref.at[i], in_sem.at[i]) for i, hbm in enumerate(fields)
    ]
    for tg in range(3):
        part = pl.ds(1024 * tg, 1024)
        loads.append(pltpu.make_async_copy(q_hbm.at[part], q_ref.at[part], in_sem.at[4 + tg]))
    stores = []
    for i, (start, count) in enumerate(((48, 8), (0, 16), (16, 16), (32, 16))):
        part = pl.ds(start, count)
        stores.append(
            pltpu.make_async_copy(out_ref.at[:, part], out_hbm.at[:, part], out_sem.at[i])
        )
    for load in loads:
        load.start()
    for i in range(4):
        loads[i].wait()
    rows = [
        jnp.concatenate(
            [
                field_ref[i, pl.ds(8 * half + r, 8, stride=16), :]
                for i in range(4)
                for half in range(2)
            ],
            0,
        )
        for r in range(8)
    ]
    for place, value in enumerate(exchange_blocks(rows)):
        out_ref[ORDER[place], 48:56] = value.reshape(8, 8, 128)
    stores[0].start()
    for tg in range(3):
        loads[4 + tg].wait()

        def rows(k, carry, tg=tg):
            levels = [
                jnp.concatenate(
                    [
                        q_ref[pl.ds(1024 * tg + lev * 16 + STACK * k + i, 8, stride=128), :]
                        for i in range(STACK)
                    ],
                    0,
                )
                for lev in range(8)
            ]
            for place, value in enumerate(exchange_blocks(levels)):
                part = pl.ds(16 * tg + STACK * k, STACK)
                out_ref[ORDER[place], part] = value.reshape(STACK, 8, 128)
            return carry

        lax.fori_loop(0, ROWS // STACK, rows, 0)
        stores[1 + tg].start()
    for store in stores:
        store.wait()


def unpack_kernel(in_ref, out_hbm, out_ref, out_sem):
    stores = []
    for tg in range(3):
        part = pl.ds(1024 * tg, 1024)
        stores.append(pltpu.make_async_copy(out_ref.at[part], out_hbm.at[part], out_sem.at[tg]))
    for tg in range(3):

        def rows(k, carry, tg=tg):
            part = pl.ds(16 * tg + STACK * k, STACK)
            cols = [in_ref[src, part].reshape(8 * STACK, 128) for src in ORDER]
            for lev, value in enumerate(exchange_blocks(cols)):
                for i in range(STACK):
                    start = 1024 * tg + lev * 16 + STACK * k + i
                    out_ref[pl.ds(start, 8, stride=128), :] = value[8 * i : 8 * i + 8]
            return carry

        lax.fori_loop(0, ROWS // STACK, rows, 0)
        stores[tg].start()
    for store in stores:
        store.wait()


def cell(c):
    return pl.ds(8 * (c + 3), 8)


def write_edges(state_ref, row_up, row_down, col_right, col_left):
    inner = pl.ds(24, 128)
    for k in range(3):
        row_up[128 * k : 128 * k + 128] = state_ref[16 + k, inner].astype(BF16)
        row_down[128 * k : 128 * k + 128] = state_ref[3 + k, inner].astype(BF16)
    for pair in range(ROWS // 2):
        for out, start in ((col_right, 128), (col_left, 24)):
            both = [state_ref[3 + 2 * pair + i, pl.ds(start, 24)] for i in range(2)]
            out[48 * pair : 48 * pair + 48] = jnp.concatenate(both, 0).astype(BF16)


def read_edges(state_ref, row_lo, row_hi, col_lo, col_hi):
    inner = pl.ds(24, 128)
    for k in range(3):
        state_ref[k, inner] = row_lo[128 * k : 128 * k + 128].astype(F32)
        state_ref[19 + k, inner] = row_hi[128 * k : 128 * k + 128].astype(F32)
    for pair in range(ROWS // 2):
        for ref, start in ((col_lo, 0), (col_hi, 152)):
            both = ref[48 * pair : 48 * pair + 48].astype(F32)
            for i in range(2):
                state_ref[3 + 2 * pair + i, pl.ds(start, 24)] = both[24 * i : 24 * i + 24]


def arrange_kernel(
    rec_ref, place_ref, in_ref,
    state_ref, weather_ref, weight_ref, row_up, row_down, col_right, col_left, turn_ref,
):
    def row(r, carry):
        parts = [in_ref[src, 16 * tg + r] for src in range(8) for tg in range(3)]
        parts.append(jnp.zeros((LANES - 192, 128), F32))
        stacked = jnp.concatenate(parts, 0)
        for half in range(2):
            turned = stacked[128 * half : 128 * half + 128].T
            for i in range(16):
                start = 128 * (2 * (r & 1) + half) + 64 * (i % 2) + i // 2
                turn_ref[pl.ds(start, 8, stride=8), :] = turned[8 * i : 8 * i + 8]
            whole = turn_ref[pl.ds(pl.multiple_of(128 * (2 * (r & 1) + half), 128), 128), :]
            state_ref[r + 3, pl.ds(24, 128), 128 * half : 128 * half + 128] = whole
        return carry

    lax.fori_loop(0, ROWS, row, 0, unroll=8)
    write_edges(state_ref, row_up, row_down, col_right, col_left)

    def lanes(*blocks):
        return jnp.concatenate(blocks, 1)

    ups, downs, rights, lefts = [], [], [], []
    zero = jnp.zeros((8, 128), F32)
    for s in range(STEPS):
        record = rec_ref[s]
        got = [in_ref[record, 48 + k] for k in range(8)]
        for k in range(8):
            weather_ref[s, k] = got[k]
        ups.append(lanes(got[1], zero))
        downs.append(lanes(got[0], got[2]))
        rights.append(lanes(got[0], got[1]))
        lefts += [lanes(got[0], got[1]), lanes(got[4], got[5])]
    row_up[384:400] = jnp.concatenate(ups, 0).astype(BF16)
    row_down[384:400] = jnp.concatenate(downs, 0).astype(BF16)
    col_right[384:400] = jnp.concatenate(rights, 0).astype(BF16)
    col_left[384:416] = jnp.concatenate(lefts, 0).astype(BF16)
    write_weights(0, place_ref, weather_ref, None, weight_ref)


def face_weights(flux, mass_low, mass_up):
    upwind = jnp.where(flux > 0, mass_low, mass_up)
    c = jnp.abs(flux) / jnp.maximum(upwind, 0.5)
    side = flux * c
    return [flux * (1.0 - c) * (1.0 - c), side * (c - 1.0), side * (3.0 - 2.0 * c)]


def write_weights(s, place_ref, weather_ref, halos, out_ref):
    tile, column = place_ref[0], place_ref[1]
    shape = (8, 128)
    lane = lane_of(shape)
    slot, group = lane & 15, lane >> 4
    level = lax.broadcasted_iota(jnp.int32, shape, 0)
    zero = jnp.zeros(shape, F32)

    def edge(ref, size):
        both = ref[384 : 384 + 2 * size].astype(F32)[size * s : size * s + size]
        return [
            both[8 * k : 8 * k + 8, 128 * h : 128 * h + 128]
            for k in range(size // 8)
            for h in range(2)
        ]

    mass = [weather_ref[s, 0], weather_ref[s, 1]]
    east = [weather_ref[s, 2], weather_ref[s, 3]]
    south = [weather_ref[s, 4], weather_ref[s, 5]]
    bottom = [weather_ref[s, 6], weather_ref[s, 7]]
    if halos is None:
        mass_before = mass_after = east_after = zero
        mass_left = mass_right = south_right = [zero, zero]
    else:
        row_lo, row_hi, col_lo, col_hi = halos
        mass_before = edge(row_lo, 8)[0]
        mass_after, east_after = edge(row_hi, 8)
        mass_left = edge(col_lo, 8)
        mass_right = edge(col_hi, 16)
        mass_right, south_right = mass_right[0:2], mass_right[2:4]
    east[0] = jnp.where((group == 0) & (tile == 0), 0.0, east[0])
    mass_rows = [mass_before] + mass + [mass_after]
    east_rows = east + [east_after]
    for h in range(2):
        here = mass[h]
        south_h = jnp.where((slot == 0) & (column == 0), 0.0, south[h])
        bottom_h = jnp.where(level == 0, 0.0, bottom[h])
        before = jnp.where(group == 0, roll(mass_rows[h], 16), roll(here, 16))
        east_up = jnp.where(group == 7, roll(east_rows[h + 1], -16), roll(east[h], -16))
        left = jnp.where(slot == 0, roll(mass_left[h], -15), roll(here, 1))
        south_up = jnp.where(slot == 15, roll(south_right[h], 15), roll(south_h, -1))
        below = jnp.concatenate([here[0:1], here[0:7]], 0)
        bottom_up = jnp.concatenate([bottom_h[1:8], zero[0:1]], 0)
        new_mass = here - (east_up - east[h]) - (south_up - south_h) - (bottom_up - bottom_h)
        fields = (
            face_weights(east[h], before, here)
            + face_weights(south_h, left, here)
            + face_weights(bottom_h, below, here)
            + [here, 1.0 / new_mass]
            + face_weights(south_right[h], roll(here, -15), mass_right[h])
            + [zero, zero]
        )
        for part in range(2):
            for r, value in enumerate(exchange_blocks(fields[8 * part : 8 * part + 8])):
                out_ref[8 * h + r, part] = value
    last = face_weights(east_after, roll(mass[1], 16), mass_after)
    out_ref[16, 0] = exchange_blocks(last + [zero] * 5)[0]


def edge_value(low2, low1, up1, up2):
    value = (7.0 / 12.0) * (low1 + up1) - (1.0 / 12.0) * (low2 + up2)
    return jnp.minimum(
        jnp.maximum(value, jnp.minimum(low1, up1)), jnp.maximum(low1, up1)
    )


def face_flux(weights, edge, below, above, q_low, q_up):
    a, b, c = weights
    forward = c > 0
    return a * edge + b * jnp.where(forward, below, above) + c * jnp.where(forward, q_low, q_up)


def pick(vector, field, c):
    lane = 16 * (field % 8) + c
    return jnp.broadcast_to(vector[:, lane : lane + 1], (8, LANES))


def advect_inner(state, weight_ref, partial, x_edges, x_flux, z_q, z_edge, z_flux):
    for ref in (z_q, z_edge, z_flux):
        ref[...] = jnp.zeros_like(ref)

    def row(with_x, r, carry):
        main = [weight_ref[r, 0], weight_ref[r, 1]]
        ahead = weight_ref[r + 1, 0]

        def weights(field, c):
            return [pick(main[(field + i) // 8], field + i, c) for i in range(3)]

        def z_put(ref, c, value, shift=0):
            for half in range(2):
                ref[half, pl.ds(16 * c + 8 + shift, 8), :] = value[:, 128 * half : 128 * half + 128]

        def z_get(ref, c, shift):
            rows = pl.ds(16 * c + 8 + shift, 8)
            return jnp.concatenate([ref[half, rows, :] for half in range(2)], 1)

        loaded, edges = {}, {}

        def q_at(c):
            if c not in loaded:
                loaded[c] = state[r + 3, cell(c)]
            return loaded[c]

        def y_edge(c):
            if c not in edges:
                edges[c] = edge_value(q_at(c - 2), q_at(c - 1), q_at(c), q_at(c + 1))
            return edges[c]

        def y_face(c):
            return face_flux(
                weights(YA, c), y_edge(c), y_edge(c - 1), y_edge(c + 1), q_at(c - 1), q_at(c)
            )

        for c in range(COLS):
            z_put(z_q, c, q_at(c))
        for half in range(2):
            low = [z_q[half, pl.ds(8 + k, COLS, stride=16), :] for k in range(2)]
            none = jnp.zeros_like(low[0])
            z_edge[half, pl.ds(8, COLS, stride=16), :] = edge_value(none, none, *low)
        flux_y = None
        for c in range(COLS):
            here = q_at(c)
            m1, p1, p2 = [z_get(z_q, c, shift) for shift in (-1, 1, 2)]
            edge_up = edge_value(m1, here, p1, p2)
            z_put(z_edge, c, edge_up, 1)
            flux_z = face_flux(
                weights(ZA, c), z_get(z_edge, c, 0), z_get(z_edge, c, -1), edge_up, m1, here
            )
            z_put(z_flux, c, flux_z)
            total = z_get(z_flux, c, 1) - flux_z
            if 3 <= c <= 12:
                flux_y = y_face(3) if c == 3 else flux_y
                flux_y_up = y_face(c + 1)
                total = total + (flux_y_up - flux_y)
                flux_y = flux_y_up
            if with_x:
                q1, q2, q3 = [state[r + 3 + k, cell(c)] for k in (1, 2, 3)]
                new_edge = edge_value(here, q1, q2, q3)
                x_edges[r + 3, c] = new_edge
                flux_x_up = face_flux(
                    [pick(ahead, XA + i, c) for i in range(3)],
                    x_edges[r + 2, c], x_edges[r + 1, c], new_edge, here, q1,
                )
                total = total + (flux_x_up - x_flux[c])
                x_flux[c] = flux_x_up
            partial[r, c] = pick(main[MASS // 8], MASS, c) * here - total
        return carry

    third = weight_ref[3, 0]
    for c in range(COLS):
        q = [state[3 + k, cell(c)] for k in range(6)]
        edges = [edge_value(*q[k : k + 4]) for k in range(3)]
        for k in range(3):
            x_edges[3 + k, c] = edges[k]
        weights = [pick(third, XA + i, c) for i in range(3)]
        x_flux[c] = face_flux(weights, edges[1], edges[0], edges[2], q[2], q[3])
    lax.fori_loop(3, 13, functools.partial(row, True), 0, unroll=2)
    lax.fori_loop(0, 6, lambda k, carry: row(False, jnp.where(k < 3, k, k + 10), carry), 0, unroll=2)


def four_faces(q, weights):
    edges = [edge_value(*q[k : k + 4]) for k in range(6)]
    flux = [
        face_flux(weights[k], edges[k + 1], edges[k], edges[k + 2], q[k + 2], q[k + 3])
        for k in range(4)
    ]
    return [flux[k + 1] - flux[k] for k in range(3)]


def advect_outer(state, weight_ref, partial):
    def x_side(side, carry):
        base = 13 * side
        vectors = [weight_ref[base + k, 0] for k in range(4)]
        for c in range(COLS):
            q = [state[base + k, cell(c)] for k in range(9)]
            weights = [[pick(vector, XA + i, c) for i in range(3)] for vector in vectors]
            for k, value in enumerate(four_faces(q, weights)):
                partial[base + k, c] -= value
        return carry

    lax.fori_loop(0, 2, x_side, 0)

    def row(r, carry):
        main = [weight_ref[r, 0], weight_ref[r, 1]]

        def weights(c):
            field, place = (YA, c) if c < COLS else (WA, 0)
            return [pick(main[(field + i) // 8], field + i, place) for i in range(3)]

        found = {}
        for base in (0, 13):
            q = [state[r + 3, cell(base - 3 + k)] for k in range(9)]
            for k, value in enumerate(four_faces(q, [weights(base + j) for j in range(4)])):
                found[base + k] = value
        for c in range(COLS):
            value = partial[r, c]
            if c in found:
                value = value - found[c]
            state[r + 3, cell(c)] = value * pick(main[INV // 8], INV, c)
        return carry

    lax.fori_loop(0, ROWS, row, 0, unroll=16)


def react(state, sel_ref, net_ref, coeff_ref, rate_ref):
    def block(n, carry):
        rows = [3 + 16 * n + i for i in range(16)]
        inner = pl.ds(24, 128)
        conc = jnp.concatenate([state[r, inner] for r in rows], 0).astype(BF16)
        for k in range(2):
            part = slice(256 * k, 256 * k + 256)
            one = jnp.dot(conc, sel_ref[:, part], preferred_element_type=F32)
            two = jnp.dot(
                conc, sel_ref[:, 512 + 256 * k : 768 + 256 * k], preferred_element_type=F32
            )
            rate_ref[:, part] = (coeff_ref[:, part] * one * two).astype(BF16)
        change = jnp.dot(rate_ref[...], net_ref[...], preferred_element_type=F32)
        change = change.astype(BF16).astype(F32)
        for i, r in enumerate(rows):
            state[r, inner] += change[128 * i : 128 * i + 128]
        return carry

    lax.fori_loop(0, ROWS // 16, block, 0)


def inner_kernel(weight_ref, state, partial, *work):
    advect_inner(state, weight_ref, partial, *work)


def first_kernel(
    place_ref, weather_ref, row_lo, row_hi, col_lo, col_hi, sel_ref, net_ref, coeff_ref,
    in_ref, partial_ref,
    state, partial, later_ref, row_up, row_down, col_right, col_left, now_ref, rate_ref,
):
    del in_ref, partial_ref
    halos = (row_lo, row_hi, col_lo, col_hi)
    for s, ref in enumerate((now_ref, later_ref)):
        write_weights(s, place_ref, weather_ref, halos, ref)
    read_edges(state, *halos)
    advect_outer(state, now_ref, partial)
    react(state, sel_ref, net_ref, coeff_ref, rate_ref)
    write_edges(state, row_up, row_down, col_right, col_left)


def second_kernel(
    weight_ref, row_lo, row_hi, col_lo, col_hi, sel_ref, net_ref, coeff_ref, in_ref, partial_ref,
    state, partial, out_ref, turn_ref, rate_ref,
):
    del in_ref, partial_ref
    read_edges(state, row_lo, row_hi, col_lo, col_hi)
    advect_outer(state, weight_ref, partial)
    react(state, sel_ref, net_ref, coeff_ref, rate_ref)

    def row(r, carry):
        turned = []
        for half in range(2):
            base = 128 * (2 * (r & 1) + half)
            whole = state[r + 3, pl.ds(24, 128), 128 * half : 128 * half + 128]
            turn_ref[pl.ds(pl.multiple_of(base, 128), 128), :] = whole
            parts = [
                turn_ref[pl.ds(base + 64 * (i % 2) + i // 2, 8, stride=8), :] for i in range(16)
            ]
            turned.append(jnp.concatenate(parts, 0).T)
        turned = jnp.concatenate([turned[0], turned[1][0:64]], 0)
        for g in range(24):
            out_ref[g // 3, 16 * (g % 3) + r] = turned[8 * g : 8 * g + 8]
        return carry

    lax.fori_loop(0, ROWS, row, 0, unroll=8)


def blocks(*lead):
    return jax.ShapeDtypeStruct(lead + (8, 128), F32)


def call(kernel, outs, specs, scratch=(), args=(), aliases=None, out_spec=VMEM, grant=40 * 2**20, cost=None):
    single = not isinstance(outs, (list, tuple))
    return pl.pallas_call(
        kernel,
        out_shape=outs,
        in_specs=specs,
        out_specs=out_spec if single else [VMEM] * len(outs),
        scratch_shapes=list(scratch),
        input_output_aliases=aliases or {},
        cost_estimate=cost,
        compiler_params=pltpu.CompilerParams(vmem_limit_bytes=grant),
    )(*args)


def swap(x):
    return lax.all_to_all(x, "tracer", split_axis=0, concat_axis=0, tiled=True)


def halo(row_up, row_down, col_right, col_left):
    tiles = [(i, i + 1) for i in range(lax.axis_size("tile") - 1)]
    columns = list(zip(ORDER[:-1], ORDER[1:]))

    def back(pairs):
        return [(target, source) for source, target in pairs]

    return (
        lax.ppermute(row_up, "tile", tiles),
        lax.ppermute(row_down, "tile", back(tiles)),
        lax.ppermute(col_right, "tracer", columns),
        lax.ppermute(col_left, "tracer", back(columns)),
    )


def per_device(
    tracers, air_mass, flux_x, flux_y, flux_z, reactants, products, rate_coeff, record_of_step
):
    reactions, species = products.shape
    place = jnp.stack([lax.axis_index("tile"), lax.axis_index("tracer")]).astype(jnp.int32)
    pairs = reactants.T
    ident = lax.broadcasted_iota(jnp.int32, (LANES, reactions), 0)
    hot = [pairs[k : k + 1] == ident for k in range(2)]
    selector = jnp.concatenate(hot, 1).astype(BF16)
    ident = lax.broadcasted_iota(jnp.int32, (reactions, LANES), 1)
    net = jnp.pad(products, ((0, 0), (0, LANES - species)))
    for k in range(2):
        net = net - (reactants[:, k : k + 1] == ident).astype(jnp.int32)
    constants = (selector, net.astype(BF16), rate_coeff[None, :])

    sent = call(
        pack_kernel,
        blocks(8, 56),
        [ANY] * 5,
        [
            pltpu.VMEM((3072, 128), F32),
            pltpu.VMEM((4, 128, 128), F32),
            pltpu.VMEM((8, 56, 8, 128), F32),
            pltpu.SemaphoreType.DMA((7,)),
            pltpu.SemaphoreType.DMA((4,)),
        ],
        [x.reshape(-1, 128) for x in (tracers, air_mass, flux_x, flux_y, flux_z)],
        out_spec=ANY,
        grant=63 * 2**20,
    )

    def edge_blocks(*counts):
        return [jax.ShapeDtypeStruct((count, LANES), BF16) for count in counts]

    state_shape = jax.ShapeDtypeStruct((ROWS + 6, 8 * (COLS + 6), LANES), F32)
    turn = pltpu.VMEM((512, 128), F32)
    weights = (ROWS + 1, 2, 8, 128)
    weights_shape = jax.ShapeDtypeStruct(weights, F32)
    state, weather, early, *edges = call(
        arrange_kernel,
        [state_shape, blocks(STEPS, 8), weights_shape] + edge_blocks(400, 400, 400, 416),
        [SMEM, SMEM, VMEM],
        [turn],
        (record_of_step, place, swap(sent)),
    )
    column = pltpu.VMEM((2, 16 * COLS + 16, 128), F32)
    work = [
        pltpu.VMEM((19, COLS, 8, LANES), F32),
        pltpu.VMEM((COLS, 8, LANES), F32),
        column, column, column,
    ]
    rates = pltpu.VMEM((2048, reactions), BF16)
    partial_shape = jax.ShapeDtypeStruct((ROWS, COLS, 8, LANES), F32)
    halos = halo(*edges)
    partial = call(
        inner_kernel, partial_shape, [VMEM] * 2, work, (early, state), cost=COST
    )
    state, _, later, *edges = call(
        first_kernel,
        [state_shape, partial_shape, weights_shape]
        + edge_blocks(384, 384, 384, 384),
        [SMEM] + [VMEM] * 10,
        [pltpu.VMEM(weights, F32), rates],
        (place, weather) + halos + constants + (state, partial),
        {9: 0, 10: 1},
    )
    halos = halo(*edges)
    partial = call(
        inner_kernel, partial_shape, [VMEM] * 2, work, (later, state), cost=COST
    )
    _, _, sent = call(
        second_kernel,
        [state_shape, partial_shape, blocks(8, 48)],
        [VMEM] * 10,
        [turn, rates],
        (later,) + halos + constants + (state, partial),
        {8: 0, 9: 1},
    )
    out = call(
        unpack_kernel,
        jax.ShapeDtypeStruct((tracers.size // 128, 128), F32),
        [VMEM],
        [pltpu.VMEM((3072, 128), F32), pltpu.SemaphoreType.DMA((3,))],
        (swap(sent),),
        out_spec=ANY,
    )
    return out.reshape(tracers.shape)


def solution(mesh):
    fields = P("tracer", None, "tile", None)
    return jax.shard_map(
        per_device,
        mesh=mesh,
        in_specs=(fields,) * 5 + (P(),) * 4,
        out_specs=fields,
        check_vma=False,
    )
```

```python
import functools

import jax
import jax.numpy as jnp
from jax import lax
from jax.experimental import pallas as pl
from jax.experimental.pallas import tpu as pltpu
from jax.sharding import PartitionSpec as P

STEPS = 2
F32 = jnp.float32
BF16 = jnp.bfloat16
ROWS = 16
COLS = 16
STACK = 16
LANES = 256
ORDER = (0, 2, 4, 6, 7, 5, 3, 1)
XA, YA, ZA, MASS, INV, WA = 0, 3, 6, 9, 10, 11
COST = pl.CostEstimate(flops=60_000_000, bytes_accessed=8_000_000, transcendentals=0)
VMEM = pl.BlockSpec(memory_space=pltpu.VMEM)
SMEM = pl.BlockSpec(memory_space=pltpu.SMEM)
ANY = pl.BlockSpec(memory_space=pltpu.HBM)


def roll(x, shift):
    return pltpu.roll(x, shift % 128, axis=1)


def lane_of(shape):
    return lax.broadcasted_iota(jnp.int32, shape, 1)


def exchange_blocks(vectors):
    block = lane_of(vectors[0].shape) >> 4
    out = list(vectors)
    for bit in (1, 2, 4):
        low = (block & bit) == 0
        for i in range(8):
            if i & bit:
                continue
            first, second = out[i], out[i | bit]
            out[i] = jnp.where(low, first, roll(second, 16 * bit))
            out[i | bit] = jnp.where(low, roll(first, -16 * bit), second)
    return out


def pack_kernel(
    q_hbm, mass_hbm, fx_hbm, fy_hbm, fz_hbm, out_hbm, q_ref, field_ref, out_ref, in_sem, out_sem
):
    fields = (mass_hbm, fx_hbm, fy_hbm, fz_hbm)
    loads = [
        pltpu.make_async_copy(hbm, field_ref.at[i], in_sem.at[i]) for i, hbm in enumerate(fields)
    ]
    for tg in range(3):
        part = pl.ds(1024 * tg, 1024)
        loads.append(pltpu.make_async_copy(q_hbm.at[part], q_ref.at[part], in_sem.at[4 + tg]))
    stores = []
    for i, (start, count) in enumerate(((48, 8), (0, 16), (16, 16), (32, 16))):
        part = pl.ds(start, count)
        stores.append(
            pltpu.make_async_copy(out_ref.at[:, part], out_hbm.at[:, part], out_sem.at[i])
        )
    for load in loads:
        load.start()
    for i in range(4):
        loads[i].wait()
    rows = [
        jnp.concatenate(
            [
                field_ref[i, pl.ds(8 * half + r, 8, stride=16), :]
                for i in range(4)
                for half in range(2)
            ],
            0,
        )
        for r in range(8)
    ]
    for place, value in enumerate(exchange_blocks(rows)):
        out_ref[ORDER[place], 48:56] = value.reshape(8, 8, 128)
    stores[0].start()
    for tg in range(3):
        loads[4 + tg].wait()

        def rows(k, carry, tg=tg):
            levels = [
                jnp.concatenate(
                    [
                        q_ref[pl.ds(1024 * tg + lev * 16 + STACK * k + i, 8, stride=128), :]
                        for i in range(STACK)
                    ],
                    0,
                )
                for lev in range(8)
            ]
            for place, value in enumerate(exchange_blocks(levels)):
                part = pl.ds(16 * tg + STACK * k, STACK)
                out_ref[ORDER[place], part] = value.reshape(STACK, 8, 128)
            return carry

        lax.fori_loop(0, ROWS // STACK, rows, 0)
        stores[1 + tg].start()
    for store in stores:
        store.wait()


def unpack_kernel(in_ref, out_hbm, out_ref, out_sem):
    stores = []
    for tg in range(3):
        part = pl.ds(1024 * tg, 1024)
        stores.append(pltpu.make_async_copy(out_ref.at[part], out_hbm.at[part], out_sem.at[tg]))
    for tg in range(3):

        def rows(k, carry, tg=tg):
            part = pl.ds(16 * tg + STACK * k, STACK)
            cols = [in_ref[src, part].reshape(8 * STACK, 128) for src in ORDER]
            for lev, value in enumerate(exchange_blocks(cols)):
                for i in range(STACK):
                    start = 1024 * tg + lev * 16 + STACK * k + i
                    out_ref[pl.ds(start, 8, stride=128), :] = value[8 * i : 8 * i + 8]
            return carry

        lax.fori_loop(0, ROWS // STACK, rows, 0)
        stores[tg].start()
    for store in stores:
        store.wait()


def cell(c):
    return pl.ds(8 * (c + 3), 8)


def write_edges(state_ref, row_up, row_down, col_right, col_left):
    inner = pl.ds(24, 128)
    for k in range(3):
        row_up[128 * k : 128 * k + 128] = state_ref[16 + k, inner].astype(BF16)
        row_down[128 * k : 128 * k + 128] = state_ref[3 + k, inner].astype(BF16)
    for pair in range(ROWS // 2):
        for out, start in ((col_right, 128), (col_left, 24)):
            both = [state_ref[3 + 2 * pair + i, pl.ds(start, 24)] for i in range(2)]
            out[48 * pair : 48 * pair + 48] = jnp.concatenate(both, 0).astype(BF16)


def read_edges(state_ref, row_lo, row_hi, col_lo, col_hi):
    inner = pl.ds(24, 128)
    for k in range(3):
        state_ref[k, inner] = row_lo[128 * k : 128 * k + 128].astype(F32)
        state_ref[19 + k, inner] = row_hi[128 * k : 128 * k + 128].astype(F32)
    for pair in range(ROWS // 2):
        for ref, start in ((col_lo, 0), (col_hi, 152)):
            both = ref[48 * pair : 48 * pair + 48].astype(F32)
            for i in range(2):
                state_ref[3 + 2 * pair + i, pl.ds(start, 24)] = both[24 * i : 24 * i + 24]


def arrange_kernel(
    rec_ref, place_ref, in_ref,
    state_ref, weather_ref, weight_ref, row_up, row_down, col_right, col_left, turn_ref,
):
    def row(r, carry):
        parts = [in_ref[src, 16 * tg + r] for src in range(8) for tg in range(3)]
        parts.append(jnp.zeros((LANES - 192, 128), F32))
        stacked = jnp.concatenate(parts, 0)
        for half in range(2):
            turned = stacked[128 * half : 128 * half + 128].T
            for i in range(16):
                start = 128 * (2 * (r & 1) + half) + 64 * (i % 2) + i // 2
                turn_ref[pl.ds(start, 8, stride=8), :] = turned[8 * i : 8 * i + 8]
            whole = turn_ref[pl.ds(pl.multiple_of(128 * (2 * (r & 1) + half), 128), 128), :]
            state_ref[r + 3, pl.ds(24, 128), 128 * half : 128 * half + 128] = whole
        return carry

    lax.fori_loop(0, ROWS, row, 0, unroll=16)
    write_edges(state_ref, row_up, row_down, col_right, col_left)

    def lanes(*blocks):
        return jnp.concatenate(blocks, 1)

    ups, downs, rights, lefts = [], [], [], []
    zero = jnp.zeros((8, 128), F32)
    for s in range(STEPS):
        record = rec_ref[s]
        got = [in_ref[record, 48 + k] for k in range(8)]
        for k in range(8):
            weather_ref[s, k] = got[k]
        ups.append(lanes(got[1], zero))
        downs.append(lanes(got[0], got[2]))
        rights.append(lanes(got[0], got[1]))
        lefts += [lanes(got[0], got[1]), lanes(got[4], got[5])]
    row_up[384:400] = jnp.concatenate(ups, 0).astype(BF16)
    row_down[384:400] = jnp.concatenate(downs, 0).astype(BF16)
    col_right[384:400] = jnp.concatenate(rights, 0).astype(BF16)
    col_left[384:416] = jnp.concatenate(lefts, 0).astype(BF16)
    write_weights(0, place_ref, weather_ref, None, weight_ref)


def face_weights(flux, mass_low, mass_up):
    upwind = jnp.where(flux > 0, mass_low, mass_up)
    c = jnp.abs(flux) / jnp.maximum(upwind, 0.5)
    side = flux * c
    return [flux * (1.0 - c) * (1.0 - c), side * (c - 1.0), side * (3.0 - 2.0 * c)]


def write_weights(s, place_ref, weather_ref, halos, out_ref):
    tile, column = place_ref[0], place_ref[1]
    shape = (8, 128)
    lane = lane_of(shape)
    slot, group = lane & 15, lane >> 4
    level = lax.broadcasted_iota(jnp.int32, shape, 0)
    zero = jnp.zeros(shape, F32)

    def edge(ref, size):
        both = ref[384 : 384 + 2 * size].astype(F32)[size * s : size * s + size]
        return [
            both[8 * k : 8 * k + 8, 128 * h : 128 * h + 128]
            for k in range(size // 8)
            for h in range(2)
        ]

    mass = [weather_ref[s, 0], weather_ref[s, 1]]
    east = [weather_ref[s, 2], weather_ref[s, 3]]
    south = [weather_ref[s, 4], weather_ref[s, 5]]
    bottom = [weather_ref[s, 6], weather_ref[s, 7]]
    if halos is None:
        mass_before = mass_after = east_after = zero
        mass_left = mass_right = south_right = [zero, zero]
    else:
        row_lo, row_hi, col_lo, col_hi = halos
        mass_before = edge(row_lo, 8)[0]
        mass_after, east_after = edge(row_hi, 8)
        mass_left = edge(col_lo, 8)
        mass_right = edge(col_hi, 16)
        mass_right, south_right = mass_right[0:2], mass_right[2:4]
    east[0] = jnp.where((group == 0) & (tile == 0), 0.0, east[0])
    mass_rows = [mass_before] + mass + [mass_after]
    east_rows = east + [east_after]
    for h in range(2):
        here = mass[h]
        south_h = jnp.where((slot == 0) & (column == 0), 0.0, south[h])
        bottom_h = jnp.where(level == 0, 0.0, bottom[h])
        before = jnp.where(group == 0, roll(mass_rows[h], 16), roll(here, 16))
        east_up = jnp.where(group == 7, roll(east_rows[h + 1], -16), roll(east[h], -16))
        left = jnp.where(slot == 0, roll(mass_left[h], -15), roll(here, 1))
        south_up = jnp.where(slot == 15, roll(south_right[h], 15), roll(south_h, -1))
        below = jnp.concatenate([here[0:1], here[0:7]], 0)
        bottom_up = jnp.concatenate([bottom_h[1:8], zero[0:1]], 0)
        new_mass = here - (east_up - east[h]) - (south_up - south_h) - (bottom_up - bottom_h)
        fields = (
            face_weights(east[h], before, here)
            + face_weights(south_h, left, here)
            + face_weights(bottom_h, below, here)
            + [here, 1.0 / new_mass]
            + face_weights(south_right[h], roll(here, -15), mass_right[h])
            + [zero, zero]
        )
        for part in range(2):
            for r, value in enumerate(exchange_blocks(fields[8 * part : 8 * part + 8])):
                out_ref[8 * h + r, part] = value
    last = face_weights(east_after, roll(mass[1], 16), mass_after)
    out_ref[16, 0] = exchange_blocks(last + [zero] * 5)[0]


def edge_value(low2, low1, up1, up2):
    value = (7.0 / 12.0) * (low1 + up1) - (1.0 / 12.0) * (low2 + up2)
    return jnp.minimum(
        jnp.maximum(value, jnp.minimum(low1, up1)), jnp.maximum(low1, up1)
    )


def face_flux(weights, edge, below, above, q_low, q_up):
    a, b, c = weights
    forward = c > 0
    return a * edge + b * jnp.where(forward, below, above) + c * jnp.where(forward, q_low, q_up)


def pick(vector, field, c):
    lane = 16 * (field % 8) + c
    return jnp.broadcast_to(vector[:, lane : lane + 1], (8, LANES))


def advect_inner(state, weight_ref, partial, x_edges, x_flux, z_q, z_edge, z_flux):
    for ref in (z_q, z_edge, z_flux):
        ref[...] = jnp.zeros_like(ref)

    def row(with_x, r, carry):
        main = [weight_ref[r, 0], weight_ref[r, 1]]
        ahead = weight_ref[r + 1, 0]

        def weights(field, c):
            return [pick(main[(field + i) // 8], field + i, c) for i in range(3)]

        def z_put(ref, c, value, shift=0):
            for half in range(2):
                ref[half, pl.ds(16 * c + 8 + shift, 8), :] = value[:, 128 * half : 128 * half + 128]

        def z_get(ref, c, shift):
            rows = pl.ds(16 * c + 8 + shift, 8)
            return jnp.concatenate([ref[half, rows, :] for half in range(2)], 1)

        loaded, edges = {}, {}

        def q_at(c):
            if c not in loaded:
                loaded[c] = state[r + 3, cell(c)]
            return loaded[c]

        def y_edge(c):
            if c not in edges:
                edges[c] = edge_value(q_at(c - 2), q_at(c - 1), q_at(c), q_at(c + 1))
            return edges[c]

        def y_face(c):
            return face_flux(
                weights(YA, c), y_edge(c), y_edge(c - 1), y_edge(c + 1), q_at(c - 1), q_at(c)
            )

        for c in range(COLS):
            z_put(z_q, c, q_at(c))
        for half in range(2):
            low = [z_q[half, pl.ds(8 + k, COLS, stride=16), :] for k in range(2)]
            none = jnp.zeros_like(low[0])
            z_edge[half, pl.ds(8, COLS, stride=16), :] = edge_value(none, none, *low)
        flux_y = None
        for c in range(COLS):
            here = q_at(c)
            m1, p1, p2 = [z_get(z_q, c, shift) for shift in (-1, 1, 2)]
            edge_up = edge_value(m1, here, p1, p2)
            z_put(z_edge, c, edge_up, 1)
            flux_z = face_flux(
                weights(ZA, c), z_get(z_edge, c, 0), z_get(z_edge, c, -1), edge_up, m1, here
            )
            z_put(z_flux, c, flux_z)
            total = z_get(z_flux, c, 1) - flux_z
            if 3 <= c <= 12:
                flux_y = y_face(3) if c == 3 else flux_y
                flux_y_up = y_face(c + 1)
                total = total + (flux_y_up - flux_y)
                flux_y = flux_y_up
            if with_x:
                q1, q2, q3 = [state[r + 3 + k, cell(c)] for k in (1, 2, 3)]
                new_edge = edge_value(here, q1, q2, q3)
                x_edges[r + 3, c] = new_edge
                flux_x_up = face_flux(
                    [pick(ahead, XA + i, c) for i in range(3)],
                    x_edges[r + 2, c], x_edges[r + 1, c], new_edge, here, q1,
                )
                total = total + (flux_x_up - x_flux[c])
                x_flux[c] = flux_x_up
            partial[r, c] = pick(main[MASS // 8], MASS, c) * here - total
        return carry

    third = weight_ref[3, 0]
    for c in range(COLS):
        q = [state[3 + k, cell(c)] for k in range(6)]
        edges = [edge_value(*q[k : k + 4]) for k in range(3)]
        for k in range(3):
            x_edges[3 + k, c] = edges[k]
        weights = [pick(third, XA + i, c) for i in range(3)]
        x_flux[c] = face_flux(weights, edges[1], edges[0], edges[2], q[2], q[3])
    lax.fori_loop(3, 13, functools.partial(row, True), 0, unroll=2)
    lax.fori_loop(0, 6, lambda k, carry: row(False, jnp.where(k < 3, k, k + 10), carry), 0, unroll=2)


def four_faces(q, weights):
    edges = [edge_value(*q[k : k + 4]) for k in range(6)]
    flux = [
        face_flux(weights[k], edges[k + 1], edges[k], edges[k + 2], q[k + 2], q[k + 3])
        for k in range(4)
    ]
    return [flux[k + 1] - flux[k] for k in range(3)]


def advect_outer(state, weight_ref, partial):
    def x_side(side, carry):
        base = 13 * side
        vectors = [weight_ref[base + k, 0] for k in range(4)]
        for c in range(COLS):
            q = [state[base + k, cell(c)] for k in range(9)]
            weights = [[pick(vector, XA + i, c) for i in range(3)] for vector in vectors]
            for k, value in enumerate(four_faces(q, weights)):
                partial[base + k, c] -= value
        return carry

    lax.fori_loop(0, 2, x_side, 0)

    def row(r, carry):
        main = [weight_ref[r, 0], weight_ref[r, 1]]

        def weights(c):
            field, place = (YA, c) if c < COLS else (WA, 0)
            return [pick(main[(field + i) // 8], field + i, place) for i in range(3)]

        found = {}
        for base in (0, 13):
            q = [state[r + 3, cell(base - 3 + k)] for k in range(9)]
            for k, value in enumerate(four_faces(q, [weights(base + j) for j in range(4)])):
                found[base + k] = value
        for c in range(COLS):
            value = partial[r, c]
            if c in found:
                value = value - found[c]
            state[r + 3, cell(c)] = value * pick(main[INV // 8], INV, c)
        return carry

    lax.fori_loop(0, ROWS, row, 0, unroll=16)


def react(state, sel_ref, net_ref, coeff_ref, rate_ref):
    def block(n, carry):
        rows = [3 + 16 * n + i for i in range(16)]
        inner = pl.ds(24, 128)
        conc = jnp.concatenate([state[r, inner] for r in rows], 0).astype(BF16)
        for k in range(2):
            part = slice(256 * k, 256 * k + 256)
            one = jnp.dot(conc, sel_ref[:, part], preferred_element_type=F32)
            two = jnp.dot(
                conc, sel_ref[:, 512 + 256 * k : 768 + 256 * k], preferred_element_type=F32
            )
            rate_ref[:, part] = (coeff_ref[:, part] * one * two).astype(BF16)
        change = jnp.dot(rate_ref[...], net_ref[...], preferred_element_type=F32)
        change = change.astype(BF16).astype(F32)
        for i, r in enumerate(rows):
            state[r, inner] += change[128 * i : 128 * i + 128]
        return carry

    lax.fori_loop(0, ROWS // 16, block, 0)


def inner_kernel(weight_ref, state, partial, *work):
    advect_inner(state, weight_ref, partial, *work)


def first_kernel(
    place_ref, weather_ref, row_lo, row_hi, col_lo, col_hi, sel_ref, net_ref, coeff_ref,
    in_ref, partial_ref,
    state, partial, later_ref, row_up, row_down, col_right, col_left, now_ref, rate_ref,
):
    del in_ref, partial_ref
    halos = (row_lo, row_hi, col_lo, col_hi)
    for s, ref in enumerate((now_ref, later_ref)):
        write_weights(s, place_ref, weather_ref, halos, ref)
    read_edges(state, *halos)
    advect_outer(state, now_ref, partial)
    react(state, sel_ref, net_ref, coeff_ref, rate_ref)
    write_edges(state, row_up, row_down, col_right, col_left)


def second_kernel(
    weight_ref, row_lo, row_hi, col_lo, col_hi, sel_ref, net_ref, coeff_ref, in_ref, partial_ref,
    state, partial, out_ref, turn_ref, rate_ref,
):
    del in_ref, partial_ref
    read_edges(state, row_lo, row_hi, col_lo, col_hi)
    advect_outer(state, weight_ref, partial)
    react(state, sel_ref, net_ref, coeff_ref, rate_ref)

    def row(r, carry):
        turned = []
        for half in range(2):
            base = 128 * (2 * (r & 1) + half)
            whole = state[r + 3, pl.ds(24, 128), 128 * half : 128 * half + 128]
            turn_ref[pl.ds(pl.multiple_of(base, 128), 128), :] = whole
            parts = [
                turn_ref[pl.ds(base + 64 * (i % 2) + i // 2, 8, stride=8), :] for i in range(16)
            ]
            turned.append(jnp.concatenate(parts, 0).T)
        turned = jnp.concatenate([turned[0], turned[1][0:64]], 0)
        for g in range(24):
            out_ref[g // 3, 16 * (g % 3) + r] = turned[8 * g : 8 * g + 8]
        return carry

    lax.fori_loop(0, ROWS, row, 0, unroll=16)


def blocks(*lead):
    return jax.ShapeDtypeStruct(lead + (8, 128), F32)


def call(kernel, outs, specs, scratch=(), args=(), aliases=None, out_spec=VMEM, grant=40 * 2**20, cost=None):
    single = not isinstance(outs, (list, tuple))
    return pl.pallas_call(
        kernel,
        out_shape=outs,
        in_specs=specs,
        out_specs=out_spec if single else [VMEM] * len(outs),
        scratch_shapes=list(scratch),
        input_output_aliases=aliases or {},
        cost_estimate=cost,
        compiler_params=pltpu.CompilerParams(vmem_limit_bytes=grant),
    )(*args)


def swap(x):
    return lax.all_to_all(x, "tracer", split_axis=0, concat_axis=0, tiled=True)


def halo(row_up, row_down, col_right, col_left):
    tiles = [(i, i + 1) for i in range(lax.axis_size("tile") - 1)]
    columns = list(zip(ORDER[:-1], ORDER[1:]))

    def back(pairs):
        return [(target, source) for source, target in pairs]

    return (
        lax.ppermute(row_up, "tile", tiles),
        lax.ppermute(row_down, "tile", back(tiles)),
        lax.ppermute(col_right, "tracer", columns),
        lax.ppermute(col_left, "tracer", back(columns)),
    )


def per_device(
    tracers, air_mass, flux_x, flux_y, flux_z, reactants, products, rate_coeff, record_of_step
):
    reactions, species = products.shape
    place = jnp.stack([lax.axis_index("tile"), lax.axis_index("tracer")]).astype(jnp.int32)
    pairs = reactants.T
    ident = lax.broadcasted_iota(jnp.int32, (LANES, reactions), 0)
    hot = [pairs[k : k + 1] == ident for k in range(2)]
    selector = jnp.concatenate(hot, 1).astype(BF16)
    ident = lax.broadcasted_iota(jnp.int32, (reactions, LANES), 1)
    net = jnp.pad(products, ((0, 0), (0, LANES - species)))
    for k in range(2):
        net = net - (reactants[:, k : k + 1] == ident).astype(jnp.int32)
    constants = (selector, net.astype(BF16), rate_coeff[None, :])

    sent = call(
        pack_kernel,
        blocks(8, 56),
        [ANY] * 5,
        [
            pltpu.VMEM((3072, 128), F32),
            pltpu.VMEM((4, 128, 128), F32),
            pltpu.VMEM((8, 56, 8, 128), F32),
            pltpu.SemaphoreType.DMA((7,)),
            pltpu.SemaphoreType.DMA((4,)),
        ],
        [x.reshape(-1, 128) for x in (tracers, air_mass, flux_x, flux_y, flux_z)],
        out_spec=ANY,
        grant=63 * 2**20,
    )

    def edge_blocks(*counts):
        return [jax.ShapeDtypeStruct((count, LANES), BF16) for count in counts]

    state_shape = jax.ShapeDtypeStruct((ROWS + 6, 8 * (COLS + 6), LANES), F32)
    turn = pltpu.VMEM((512, 128), F32)
    weights = (ROWS + 1, 2, 8, 128)
    weights_shape = jax.ShapeDtypeStruct(weights, F32)
    state, weather, early, *edges = call(
        arrange_kernel,
        [state_shape, blocks(STEPS, 8), weights_shape] + edge_blocks(400, 400, 400, 416),
        [SMEM, SMEM, VMEM],
        [turn],
        (record_of_step, place, swap(sent)),
    )
    column = pltpu.VMEM((2, 16 * COLS + 16, 128), F32)
    work = [
        pltpu.VMEM((19, COLS, 8, LANES), F32),
        pltpu.VMEM((COLS, 8, LANES), F32),
        column, column, column,
    ]
    rates = pltpu.VMEM((2048, reactions), BF16)
    partial_shape = jax.ShapeDtypeStruct((ROWS, COLS, 8, LANES), F32)
    halos = halo(*edges)
    partial = call(
        inner_kernel, partial_shape, [VMEM] * 2, work, (early, state), cost=COST
    )
    state, _, later, *edges = call(
        first_kernel,
        [state_shape, partial_shape, weights_shape]
        + edge_blocks(384, 384, 384, 384),
        [SMEM] + [VMEM] * 10,
        [pltpu.VMEM(weights, F32), rates],
        (place, weather) + halos + constants + (state, partial),
        {9: 0, 10: 1},
    )
    halos = halo(*edges)
    partial = call(
        inner_kernel, partial_shape, [VMEM] * 2, work, (later, state), cost=COST
    )
    _, _, sent = call(
        second_kernel,
        [state_shape, partial_shape, blocks(8, 48)],
        [VMEM] * 10,
        [turn, rates],
        (later,) + halos + constants + (state, partial),
        {8: 0, 9: 1},
    )
    out = call(
        unpack_kernel,
        jax.ShapeDtypeStruct((tracers.size // 128, 128), F32),
        [VMEM],
        [pltpu.VMEM((3072, 128), F32), pltpu.SemaphoreType.DMA((3,))],
        (swap(sent),),
        out_spec=ANY,
    )
    return out.reshape(tracers.shape)


def solution(mesh):
    fields = P("tracer", None, "tile", None)
    return jax.shard_map(
        per_device,
        mesh=mesh,
        in_specs=(fields,) * 5 + (P(),) * 4,
        out_specs=fields,
        check_vma=False,
    )
```

```python
import functools

import jax
import jax.numpy as jnp
from jax import lax
from jax.experimental import pallas as pl
from jax.experimental.pallas import tpu as pltpu
from jax.sharding import PartitionSpec as P

STEPS = 2
F32 = jnp.float32
BF16 = jnp.bfloat16
ROWS = 16
COLS = 16
STACK = 16
LANES = 256
ORDER = (0, 2, 4, 6, 7, 5, 3, 1)
XA, YA, ZA, MASS, INV, WA = 0, 3, 6, 9, 10, 11
COST = pl.CostEstimate(flops=60_000_000, bytes_accessed=8_000_000, transcendentals=0)
VMEM = pl.BlockSpec(memory_space=pltpu.VMEM)
SMEM = pl.BlockSpec(memory_space=pltpu.SMEM)
ANY = pl.BlockSpec(memory_space=pltpu.HBM)


def roll(x, shift):
    return pltpu.roll(x, shift % 128, axis=1)


def lane_of(shape):
    return lax.broadcasted_iota(jnp.int32, shape, 1)


def exchange_blocks(vectors):
    block = lane_of(vectors[0].shape) >> 4
    out = list(vectors)
    for bit in (1, 2, 4):
        low = (block & bit) == 0
        for i in range(8):
            if i & bit:
                continue
            first, second = out[i], out[i | bit]
            out[i] = jnp.where(low, first, roll(second, 16 * bit))
            out[i | bit] = jnp.where(low, roll(first, -16 * bit), second)
    return out


def pack_kernel(
    q_hbm, mass_hbm, fx_hbm, fy_hbm, fz_hbm, out_hbm, q_ref, field_ref, out_ref, in_sem, out_sem
):
    fields = (mass_hbm, fx_hbm, fy_hbm, fz_hbm)
    loads = [
        pltpu.make_async_copy(hbm, field_ref.at[i], in_sem.at[i]) for i, hbm in enumerate(fields)
    ]
    for tg in range(3):
        part = pl.ds(1024 * tg, 1024)
        loads.append(pltpu.make_async_copy(q_hbm.at[part], q_ref.at[part], in_sem.at[4 + tg]))
    stores = []
    for i, (start, count) in enumerate(((48, 8), (0, 16), (16, 16), (32, 16))):
        part = pl.ds(start, count)
        stores.append(
            pltpu.make_async_copy(out_ref.at[:, part], out_hbm.at[:, part], out_sem.at[i])
        )
    for load in loads:
        load.start()
    for i in range(4):
        loads[i].wait()
    rows = [
        jnp.concatenate(
            [
                field_ref[i, pl.ds(8 * half + r, 8, stride=16), :]
                for i in range(4)
                for half in range(2)
            ],
            0,
        )
        for r in range(8)
    ]
    for place, value in enumerate(exchange_blocks(rows)):
        out_ref[ORDER[place], 48:56] = value.reshape(8, 8, 128)
    stores[0].start()
    for tg in range(3):
        loads[4 + tg].wait()

        def rows(k, carry, tg=tg):
            levels = [
                jnp.concatenate(
                    [
                        q_ref[pl.ds(1024 * tg + lev * 16 + STACK * k + i, 8, stride=128), :]
                        for i in range(STACK)
                    ],
                    0,
                )
                for lev in range(8)
            ]
            for place, value in enumerate(exchange_blocks(levels)):
                part = pl.ds(16 * tg + STACK * k, STACK)
                out_ref[ORDER[place], part] = value.reshape(STACK, 8, 128)
            return carry

        lax.fori_loop(0, ROWS // STACK, rows, 0)
        stores[1 + tg].start()
    for store in stores:
        store.wait()


def unpack_kernel(in_ref, out_hbm, out_ref, out_sem):
    stores = []
    for tg in range(3):
        part = pl.ds(1024 * tg, 1024)
        stores.append(pltpu.make_async_copy(out_ref.at[part], out_hbm.at[part], out_sem.at[tg]))
    for tg in range(3):

        def rows(k, carry, tg=tg):
            part = pl.ds(16 * tg + STACK * k, STACK)
            cols = [in_ref[src, part].reshape(8 * STACK, 128) for src in ORDER]
            for lev, value in enumerate(exchange_blocks(cols)):
                for i in range(STACK):
                    start = 1024 * tg + lev * 16 + STACK * k + i
                    out_ref[pl.ds(start, 8, stride=128), :] = value[8 * i : 8 * i + 8]
            return carry

        lax.fori_loop(0, ROWS // STACK, rows, 0)
        stores[tg].start()
    for store in stores:
        store.wait()


def cell(c):
    return pl.ds(8 * (c + 3), 8)


def write_edges(state_ref, row_up, row_down, col_right, col_left):
    inner = pl.ds(24, 128)
    for k in range(3):
        row_up[128 * k : 128 * k + 128] = state_ref[16 + k, inner].astype(BF16)
        row_down[128 * k : 128 * k + 128] = state_ref[3 + k, inner].astype(BF16)
    for pair in range(ROWS // 2):
        for out, start in ((col_right, 128), (col_left, 24)):
            both = [state_ref[3 + 2 * pair + i, pl.ds(start, 24)] for i in range(2)]
            out[48 * pair : 48 * pair + 48] = jnp.concatenate(both, 0).astype(BF16)


def read_edges(state_ref, row_lo, row_hi, col_lo, col_hi):
    inner = pl.ds(24, 128)
    for k in range(3):
        state_ref[k, inner] = row_lo[128 * k : 128 * k + 128].astype(F32)
        state_ref[19 + k, inner] = row_hi[128 * k : 128 * k + 128].astype(F32)
    for pair in range(ROWS // 2):
        for ref, start in ((col_lo, 0), (col_hi, 152)):
            both = ref[48 * pair : 48 * pair + 48].astype(F32)
            for i in range(2):
                state_ref[3 + 2 * pair + i, pl.ds(start, 24)] = both[24 * i : 24 * i + 24]


def arrange_kernel(
    rec_ref, place_ref, in_ref,
    state_ref, weather_ref, weight_ref, row_up, row_down, col_right, col_left, turn_ref,
):
    def row(r, carry):
        parts = [in_ref[src, 16 * tg + r] for src in range(8) for tg in range(3)]
        parts.append(jnp.zeros((LANES - 192, 128), F32))
        stacked = jnp.concatenate(parts, 0)
        for half in range(2):
            turned = stacked[128 * half : 128 * half + 128].T
            for i in range(16):
                start = 128 * (2 * (r & 1) + half) + 64 * (i % 2) + i // 2
                turn_ref[pl.ds(start, 8, stride=8), :] = turned[8 * i : 8 * i + 8]
            whole = turn_ref[pl.ds(pl.multiple_of(128 * (2 * (r & 1) + half), 128), 128), :]
            state_ref[r + 3, pl.ds(24, 128), 128 * half : 128 * half + 128] = whole
        return carry

    lax.fori_loop(0, ROWS, row, 0, unroll=16)
    write_edges(state_ref, row_up, row_down, col_right, col_left)

    def lanes(*blocks):
        return jnp.concatenate(blocks, 1)

    ups, downs, rights, lefts = [], [], [], []
    zero = jnp.zeros((8, 128), F32)
    for s in range(STEPS):
        record = rec_ref[s]
        got = [in_ref[record, 48 + k] for k in range(8)]
        for k in range(8):
            weather_ref[s, k] = got[k]
        ups.append(lanes(got[1], zero))
        downs.append(lanes(got[0], got[2]))
        rights.append(lanes(got[0], got[1]))
        lefts += [lanes(got[0], got[1]), lanes(got[4], got[5])]
    row_up[384:400] = jnp.concatenate(ups, 0).astype(BF16)
    row_down[384:400] = jnp.concatenate(downs, 0).astype(BF16)
    col_right[384:400] = jnp.concatenate(rights, 0).astype(BF16)
    col_left[384:416] = jnp.concatenate(lefts, 0).astype(BF16)
    write_weights(0, place_ref, weather_ref, None, weight_ref)


def face_weights(flux, mass_low, mass_up):
    upwind = jnp.where(flux > 0, mass_low, mass_up)
    c = jnp.abs(flux) / jnp.maximum(upwind, 0.5)
    side = flux * c
    return [flux * (1.0 - c) * (1.0 - c), side * (c - 1.0), side * (3.0 - 2.0 * c)]


def write_weights(s, place_ref, weather_ref, halos, out_ref):
    tile, column = place_ref[0], place_ref[1]
    shape = (8, 128)
    lane = lane_of(shape)
    slot, group = lane & 15, lane >> 4
    level = lax.broadcasted_iota(jnp.int32, shape, 0)
    zero = jnp.zeros(shape, F32)

    def edge(ref, size):
        both = ref[384 : 384 + 2 * size].astype(F32)[size * s : size * s + size]
        return [
            both[8 * k : 8 * k + 8, 128 * h : 128 * h + 128]
            for k in range(size // 8)
            for h in range(2)
        ]

    mass = [weather_ref[s, 0], weather_ref[s, 1]]
    east = [weather_ref[s, 2], weather_ref[s, 3]]
    south = [weather_ref[s, 4], weather_ref[s, 5]]
    bottom = [weather_ref[s, 6], weather_ref[s, 7]]
    if halos is None:
        mass_before = mass_after = east_after = zero
        mass_left = mass_right = south_right = [zero, zero]
    else:
        row_lo, row_hi, col_lo, col_hi = halos
        mass_before = edge(row_lo, 8)[0]
        mass_after, east_after = edge(row_hi, 8)
        mass_left = edge(col_lo, 8)
        mass_right = edge(col_hi, 16)
        mass_right, south_right = mass_right[0:2], mass_right[2:4]
    east[0] = jnp.where((group == 0) & (tile == 0), 0.0, east[0])
    mass_rows = [mass_before] + mass + [mass_after]
    east_rows = east + [east_after]
    for h in range(2):
        here = mass[h]
        south_h = jnp.where((slot == 0) & (column == 0), 0.0, south[h])
        bottom_h = jnp.where(level == 0, 0.0, bottom[h])
        before = jnp.where(group == 0, roll(mass_rows[h], 16), roll(here, 16))
        east_up = jnp.where(group == 7, roll(east_rows[h + 1], -16), roll(east[h], -16))
        left = jnp.where(slot == 0, roll(mass_left[h], -15), roll(here, 1))
        south_up = jnp.where(slot == 15, roll(south_right[h], 15), roll(south_h, -1))
        below = jnp.concatenate([here[0:1], here[0:7]], 0)
        bottom_up = jnp.concatenate([bottom_h[1:8], zero[0:1]], 0)
        new_mass = here - (east_up - east[h]) - (south_up - south_h) - (bottom_up - bottom_h)
        fields = (
            face_weights(east[h], before, here)
            + face_weights(south_h, left, here)
            + face_weights(bottom_h, below, here)
            + [here, 1.0 / new_mass]
            + face_weights(south_right[h], roll(here, -15), mass_right[h])
            + [zero, zero]
        )
        for part in range(2):
            for r, value in enumerate(exchange_blocks(fields[8 * part : 8 * part + 8])):
                out_ref[8 * h + r, part] = value
    last = face_weights(east_after, roll(mass[1], 16), mass_after)
    out_ref[16, 0] = exchange_blocks(last + [zero] * 5)[0]


def edge_value(low2, low1, up1, up2):
    value = (7.0 / 12.0) * (low1 + up1) - (1.0 / 12.0) * (low2 + up2)
    return jnp.minimum(
        jnp.maximum(value, jnp.minimum(low1, up1)), jnp.maximum(low1, up1)
    )


def face_flux(weights, edge, below, above, q_low, q_up):
    a, b, c = weights
    forward = c > 0
    return a * edge + b * jnp.where(forward, below, above) + c * jnp.where(forward, q_low, q_up)


def pick(vector, field, c):
    lane = 16 * (field % 8) + c
    return jnp.broadcast_to(vector[:, lane : lane + 1], (8, LANES))


def advect_inner(state, weight_ref, partial, x_edges, x_flux, z_q, z_edge, z_flux):
    for ref in (z_q, z_edge, z_flux):
        ref[...] = jnp.zeros_like(ref)

    def row(with_x, r, carry):
        main = [weight_ref[r, 0], weight_ref[r, 1]]
        ahead = weight_ref[r + 1, 0]

        def weights(field, c):
            return [pick(main[(field + i) // 8], field + i, c) for i in range(3)]

        def z_put(ref, c, value, shift=0):
            for half in range(2):
                ref[half, pl.ds(16 * c + 8 + shift, 8), :] = value[:, 128 * half : 128 * half + 128]

        def z_get(ref, c, shift):
            rows = pl.ds(16 * c + 8 + shift, 8)
            return jnp.concatenate([ref[half, rows, :] for half in range(2)], 1)

        loaded, edges = {}, {}

        def q_at(c):
            if c not in loaded:
                loaded[c] = state[r + 3, cell(c)]
            return loaded[c]

        def y_edge(c):
            if c not in edges:
                edges[c] = edge_value(q_at(c - 2), q_at(c - 1), q_at(c), q_at(c + 1))
            return edges[c]

        def y_face(c):
            return face_flux(
                weights(YA, c), y_edge(c), y_edge(c - 1), y_edge(c + 1), q_at(c - 1), q_at(c)
            )

        for c in range(COLS):
            z_put(z_q, c, q_at(c))
        for half in range(2):
            low = [z_q[half, pl.ds(8 + k, COLS, stride=16), :] for k in range(2)]
            none = jnp.zeros_like(low[0])
            z_edge[half, pl.ds(8, COLS, stride=16), :] = edge_value(none, none, *low)
        flux_y = None
        for c in range(COLS):
            here = q_at(c)
            m1, p1, p2 = [z_get(z_q, c, shift) for shift in (-1, 1, 2)]
            edge_up = edge_value(m1, here, p1, p2)
            z_put(z_edge, c, edge_up, 1)
            flux_z = face_flux(
                weights(ZA, c), z_get(z_edge, c, 0), z_get(z_edge, c, -1), edge_up, m1, here
            )
            z_put(z_flux, c, flux_z)
            total = z_get(z_flux, c, 1) - flux_z
            if 3 <= c <= 12:
                flux_y = y_face(3) if c == 3 else flux_y
                flux_y_up = y_face(c + 1)
                total = total + (flux_y_up - flux_y)
                flux_y = flux_y_up
            if with_x:
                q1, q2, q3 = [state[r + 3 + k, cell(c)] for k in (1, 2, 3)]
                new_edge = edge_value(here, q1, q2, q3)
                x_edges[r + 3, c] = new_edge
                flux_x_up = face_flux(
                    [pick(ahead, XA + i, c) for i in range(3)],
                    x_edges[r + 2, c], x_edges[r + 1, c], new_edge, here, q1,
                )
                total = total + (flux_x_up - x_flux[c])
                x_flux[c] = flux_x_up
            partial[r, c] = pick(main[MASS // 8], MASS, c) * here - total
        return carry

    third = weight_ref[3, 0]
    for c in range(COLS):
        q = [state[3 + k, cell(c)] for k in range(6)]
        edges = [edge_value(*q[k : k + 4]) for k in range(3)]
        for k in range(3):
            x_edges[3 + k, c] = edges[k]
        weights = [pick(third, XA + i, c) for i in range(3)]
        x_flux[c] = face_flux(weights, edges[1], edges[0], edges[2], q[2], q[3])
    lax.fori_loop(3, 13, functools.partial(row, True), 0, unroll=5)
    lax.fori_loop(0, 6, lambda k, carry: row(False, jnp.where(k < 3, k, k + 10), carry), 0, unroll=3)


def four_faces(q, weights):
    edges = [edge_value(*q[k : k + 4]) for k in range(6)]
    flux = [
        face_flux(weights[k], edges[k + 1], edges[k], edges[k + 2], q[k + 2], q[k + 3])
        for k in range(4)
    ]
    return [flux[k + 1] - flux[k] for k in range(3)]


def advect_outer(state, weight_ref, partial):
    def x_side(side, carry):
        base = 13 * side
        vectors = [weight_ref[base + k, 0] for k in range(4)]
        for c in range(COLS):
            q = [state[base + k, cell(c)] for k in range(9)]
            weights = [[pick(vector, XA + i, c) for i in range(3)] for vector in vectors]
            for k, value in enumerate(four_faces(q, weights)):
                partial[base + k, c] -= value
        return carry

    lax.fori_loop(0, 2, x_side, 0)

    def row(r, carry):
        main = [weight_ref[r, 0], weight_ref[r, 1]]

        def weights(c):
            field, place = (YA, c) if c < COLS else (WA, 0)
            return [pick(main[(field + i) // 8], field + i, place) for i in range(3)]

        found = {}
        for base in (0, 13):
            q = [state[r + 3, cell(base - 3 + k)] for k in range(9)]
            for k, value in enumerate(four_faces(q, [weights(base + j) for j in range(4)])):
                found[base + k] = value
        for c in range(COLS):
            value = partial[r, c]
            if c in found:
                value = value - found[c]
            state[r + 3, cell(c)] = value * pick(main[INV // 8], INV, c)
        return carry

    lax.fori_loop(0, ROWS, row, 0, unroll=16)


def react(state, sel_ref, net_ref, coeff_ref, rate_ref):
    def block(n, carry):
        rows = [3 + 16 * n + i for i in range(16)]
        inner = pl.ds(24, 128)
        conc = jnp.concatenate([state[r, inner] for r in rows], 0).astype(BF16)
        for k in range(2):
            part = slice(256 * k, 256 * k + 256)
            one = jnp.dot(conc, sel_ref[:, part], preferred_element_type=F32)
            two = jnp.dot(
                conc, sel_ref[:, 512 + 256 * k : 768 + 256 * k], preferred_element_type=F32
            )
            rate_ref[:, part] = (coeff_ref[:, part] * one * two).astype(BF16)
        change = jnp.dot(rate_ref[...], net_ref[...], preferred_element_type=F32)
        change = change.astype(BF16).astype(F32)
        for i, r in enumerate(rows):
            state[r, inner] += change[128 * i : 128 * i + 128]
        return carry

    lax.fori_loop(0, ROWS // 16, block, 0)


def inner_kernel(weight_ref, state, partial, *work):
    advect_inner(state, weight_ref, partial, *work)


def first_kernel(
    place_ref, weather_ref, row_lo, row_hi, col_lo, col_hi, sel_ref, net_ref, coeff_ref,
    in_ref, partial_ref,
    state, partial, later_ref, row_up, row_down, col_right, col_left, now_ref, rate_ref,
):
    del in_ref, partial_ref
    halos = (row_lo, row_hi, col_lo, col_hi)
    for s, ref in enumerate((now_ref, later_ref)):
        write_weights(s, place_ref, weather_ref, halos, ref)
    read_edges(state, *halos)
    advect_outer(state, now_ref, partial)
    react(state, sel_ref, net_ref, coeff_ref, rate_ref)
    write_edges(state, row_up, row_down, col_right, col_left)


def second_kernel(
    weight_ref, row_lo, row_hi, col_lo, col_hi, sel_ref, net_ref, coeff_ref, in_ref, partial_ref,
    state, partial, out_ref, turn_ref, rate_ref,
):
    del in_ref, partial_ref
    read_edges(state, row_lo, row_hi, col_lo, col_hi)
    advect_outer(state, weight_ref, partial)
    react(state, sel_ref, net_ref, coeff_ref, rate_ref)

    def row(r, carry):
        turned = []
        for half in range(2):
            base = 128 * (2 * (r & 1) + half)
            whole = state[r + 3, pl.ds(24, 128), 128 * half : 128 * half + 128]
            turn_ref[pl.ds(pl.multiple_of(base, 128), 128), :] = whole
            parts = [
                turn_ref[pl.ds(base + 64 * (i % 2) + i // 2, 8, stride=8), :] for i in range(16)
            ]
            turned.append(jnp.concatenate(parts, 0).T)
        turned = jnp.concatenate([turned[0], turned[1][0:64]], 0)
        for g in range(24):
            out_ref[g // 3, 16 * (g % 3) + r] = turned[8 * g : 8 * g + 8]
        return carry

    lax.fori_loop(0, ROWS, row, 0, unroll=16)


def blocks(*lead):
    return jax.ShapeDtypeStruct(lead + (8, 128), F32)


def call(kernel, outs, specs, scratch=(), args=(), aliases=None, out_spec=VMEM, grant=40 * 2**20, cost=None):
    single = not isinstance(outs, (list, tuple))
    return pl.pallas_call(
        kernel,
        out_shape=outs,
        in_specs=specs,
        out_specs=out_spec if single else [VMEM] * len(outs),
        scratch_shapes=list(scratch),
        input_output_aliases=aliases or {},
        cost_estimate=cost,
        compiler_params=pltpu.CompilerParams(vmem_limit_bytes=grant),
    )(*args)


def swap(x):
    return lax.all_to_all(x, "tracer", split_axis=0, concat_axis=0, tiled=True)


def halo(row_up, row_down, col_right, col_left):
    tiles = [(i, i + 1) for i in range(lax.axis_size("tile") - 1)]
    columns = list(zip(ORDER[:-1], ORDER[1:]))

    def back(pairs):
        return [(target, source) for source, target in pairs]

    return (
        lax.ppermute(row_up, "tile", tiles),
        lax.ppermute(row_down, "tile", back(tiles)),
        lax.ppermute(col_right, "tracer", columns),
        lax.ppermute(col_left, "tracer", back(columns)),
    )


def per_device(
    tracers, air_mass, flux_x, flux_y, flux_z, reactants, products, rate_coeff, record_of_step
):
    reactions, species = products.shape
    place = jnp.stack([lax.axis_index("tile"), lax.axis_index("tracer")]).astype(jnp.int32)
    pairs = reactants.T
    ident = lax.broadcasted_iota(jnp.int32, (LANES, reactions), 0)
    hot = [pairs[k : k + 1] == ident for k in range(2)]
    selector = jnp.concatenate(hot, 1).astype(BF16)
    ident = lax.broadcasted_iota(jnp.int32, (reactions, LANES), 1)
    net = jnp.pad(products, ((0, 0), (0, LANES - species)))
    for k in range(2):
        net = net - (reactants[:, k : k + 1] == ident).astype(jnp.int32)
    constants = (selector, net.astype(BF16), rate_coeff[None, :])

    sent = call(
        pack_kernel,
        blocks(8, 56),
        [ANY] * 5,
        [
            pltpu.VMEM((3072, 128), F32),
            pltpu.VMEM((4, 128, 128), F32),
            pltpu.VMEM((8, 56, 8, 128), F32),
            pltpu.SemaphoreType.DMA((7,)),
            pltpu.SemaphoreType.DMA((4,)),
        ],
        [x.reshape(-1, 128) for x in (tracers, air_mass, flux_x, flux_y, flux_z)],
        out_spec=ANY,
        grant=63 * 2**20,
    )

    def edge_blocks(*counts):
        return [jax.ShapeDtypeStruct((count, LANES), BF16) for count in counts]

    state_shape = jax.ShapeDtypeStruct((ROWS + 6, 8 * (COLS + 6), LANES), F32)
    turn = pltpu.VMEM((512, 128), F32)
    weights = (ROWS + 1, 2, 8, 128)
    weights_shape = jax.ShapeDtypeStruct(weights, F32)
    state, weather, early, *edges = call(
        arrange_kernel,
        [state_shape, blocks(STEPS, 8), weights_shape] + edge_blocks(400, 400, 400, 416),
        [SMEM, SMEM, VMEM],
        [turn],
        (record_of_step, place, swap(sent)),
    )
    column = pltpu.VMEM((2, 16 * COLS + 16, 128), F32)
    work = [
        pltpu.VMEM((19, COLS, 8, LANES), F32),
        pltpu.VMEM((COLS, 8, LANES), F32),
        column, column, column,
    ]
    rates = pltpu.VMEM((2048, reactions), BF16)
    partial_shape = jax.ShapeDtypeStruct((ROWS, COLS, 8, LANES), F32)
    halos = halo(*edges)
    partial = call(
        inner_kernel, partial_shape, [VMEM] * 2, work, (early, state), cost=COST
    )
    state, _, later, *edges = call(
        first_kernel,
        [state_shape, partial_shape, weights_shape]
        + edge_blocks(384, 384, 384, 384),
        [SMEM] + [VMEM] * 10,
        [pltpu.VMEM(weights, F32), rates],
        (place, weather) + halos + constants + (state, partial),
        {9: 0, 10: 1},
    )
    halos = halo(*edges)
    partial = call(
        inner_kernel, partial_shape, [VMEM] * 2, work, (later, state), cost=COST
    )
    _, _, sent = call(
        second_kernel,
        [state_shape, partial_shape, blocks(8, 48)],
        [VMEM] * 10,
        [turn, rates],
        (later,) + halos + constants + (state, partial),
        {8: 0, 9: 1},
    )
    out = call(
        unpack_kernel,
        jax.ShapeDtypeStruct((tracers.size // 128, 128), F32),
        [VMEM],
        [pltpu.VMEM((3072, 128), F32), pltpu.SemaphoreType.DMA((3,))],
        (swap(sent),),
        out_spec=ANY,
    )
    return out.reshape(tracers.shape)


def solution(mesh):
    fields = P("tracer", None, "tile", None)
    return jax.shard_map(
        per_device,
        mesh=mesh,
        in_specs=(fields,) * 5 + (P(),) * 4,
        out_specs=fields,
        check_vma=False,
    )
```
